128 devices in a mesh: mem: 2 (over y_lo), gx: 8 (over x, core), gy: 8 (over z, y_hi).
Axes of the slice: x: 4, y: 4 (y_hi: 2, y_lo: 2; y = y_hi * 2 + y_lo), z: 4, core: 2. Of those that a mesh axis runs over, the one named last changes fastest.
Arguments:
- alpha: float32 [128, 2, 8, 32, 1024], P('mem', None, None, 'gy', 'gx'), may hold values from -6 to 6
- static_control: float32 [2, 8, 32, 1024], P(None, None, 'gy', 'gx'), may hold values from -6 to 6
- perturbations: bfloat16 [128, 2, 8, 32, 1024], P('mem', None, None, 'gy', 'gx'), may hold values from -6 to 6
- sigma: float32 [2, 8, 32, 1024], P(None, None, 'gy', 'gx'), may hold values from 0.5 to 2
- obs_coef: float32 [2, 8, 65536], P(None, None, ('gx', 'gy')), may hold values from -1.5 to 1.5
- interp_weights: float32 [4, 65536], P(None, ('gx', 'gy')), may hold values from 0.1 to 0.9
- obs_values: float32 [65536], P(('gx', 'gy')), may hold values from -6 to 6
- obs_weights: float32 [65536], P(('gx', 'gy')), may hold values from 0.5 to 4
- obs_tile: int32 [65536, 1], P(('gx', 'gy')), may hold values from 0 to 63; in each aligned block of 1024 rows (0 to 1023, 1024 to 2047, ...) at most 32 rows name the same one
- obs_cell: int32 [65536], P(('gx', 'gy')), may hold values from 0 to 2047
Outputs:
- alpha_out: float32 [128, 2, 8, 32, 1024], P('mem', None, None, 'gy', 'gx')
- static_out: float32 [2, 8, 32, 1024], P(None, None, 'gy', 'gx')
- increment: float32 [2, 8, 32, 1024], P(None, None, 'gy', 'gx')
The draws below stay inside these ranges and needn't reach their ends.
Inputs may be any that keep to these rules, and one draw needn't show every extreme that they name: `obs_tile`: within the rows of one device no tile is named more than 32 times; in some devices' rows a tile is named exactly 32 times.
All inputs are finite; a program needn't handle non-finite values.
Results may differ from the reference program's by a relative error of at most 0.0003.
Values sent between devices are 32-bit elements; how exact they have to be, the bound alone decides.
A program may use at most 128 MiB of HBM per device.

```python
import math
import jax
import jax.numpy as jnp
import numpy as np
from jax import lax

MEMBERS = 128
VARS = 2
LEVELS = 8
CX = 128
CY = 4
OBS_DEV = 1024
ITERS = 2
NX = 1024
NY = 32
TILES = 64
OBS = 65536
CAP = 32
N_GY = 8


def touch_ends(values, rng, low, top_value):
    extent = values.shape
    spot = [jax.random.randint(jax.random.fold_in(rng, axis), (), 0, extent[axis]) for axis in range(len(extent))]
    values = values.at[tuple(spot)].set(low)
    longest = extent.index(max(extent))
    spot[longest] = (spot[longest] + 1) % extent[longest]
    return values.at[tuple(spot)].set(top_value)


def steps_of(key, dims, shards, low, high):
    def one(position, blocks):
        heights = jax.random.uniform(jax.random.fold_in(jax.random.fold_in(key, 6), position), (blocks,), jnp.float32, low / len(shards), high / len(shards))
        return jnp.repeat(jnp.exp(heights), dims[position] // blocks).reshape((-1,) + (1,) * (len(dims) - position - 1))

    factor_of = one(*shards[0])
    for cut in shards[1:]:
        factor_of = factor_of * one(*cut)
    return factor_of


def assign_block(rng, own, number, rows, count, top, most, slope):
    ranking = jax.random.permutation(rng, count)
    packed, usual = portions_of(count, rows * top, most, slope, True), portions_of(count, rows * top, most, slope, False)
    places = jnp.arange(count)

    def named(lengths, rotation):
        used = int((lengths > 0).sum())
        fixed = max(1, used // 4)
        shifted = fixed + (places - fixed + rotation * (used - fixed)) % max(1, count - fixed)
        return jnp.zeros((count,), jnp.int32).at[ranking[jnp.where(places < fixed, places, shifted)]].set(jnp.asarray(lengths, jnp.int32))

    lengths = jnp.where(number % 4 == 0, named(packed, number // 4), named(usual, number - number // 4 - 1))
    mixed = jax.random.permutation(jax.random.fold_in(own, 3), count)
    giver, taker = mixed[0:count // 2 * 2:2], mixed[1:count // 2 * 2:2]
    slack = jnp.minimum(lengths[giver] - 1, most - lengths[taker]) // 2
    slack = jnp.where((giver == ranking[0]) | (taker == ranking[0]) | (lengths[taker] == 0), 0, jnp.maximum(slack, 0))
    shifted = jax.random.randint(jax.random.fold_in(own, 4), (count // 2,), 0, 1 << 20) % (slack + 1)
    lengths = lengths.at[giver].add(-shifted).at[taker].add(shifted)
    members = jnp.searchsorted(jnp.cumsum(lengths), jnp.arange(rows * top), side="right").astype(jnp.int32)
    listing = members.reshape(top, rows).T
    listing = listing[jax.random.permutation(jax.random.fold_in(own, 1), rows)]
    rotation = jax.random.randint(jax.random.fold_in(own, 2), (rows, 1), 0, top)
    return jnp.take_along_axis(listing, (jnp.arange(top)[None, :] + rotation) % top, axis=1)


def portions_of(number_of, total, bound, lean, full):
    loads = [(1 << 20) // math.isqrt(standing ** lean) + 1 for standing in range(1, number_of + 1)]
    largest = bound if full else min(bound, max(-(-total // number_of), total * loads[0] // sum(loads)))
    least = 1 if total - largest >= number_of - 1 else 0
    holding, spare = [largest] + [least] * (number_of - 1), total - largest - least * (number_of - 1)
    while spare > 0:
        candidates = [i for i in range(1, number_of) if holding[i] < largest] or [i for i in range(1, number_of) if holding[i] < bound]
        mass, left = sum([loads[i] for i in candidates]), spare
        for i in candidates:
            addition = min(bound - holding[i], max(1, left * loads[i] // mass), spare)
            holding[i] = holding[i] + addition
            spare = spare - addition
    return np.array(holding)


def normal_values(key, extent, width, limit, pieces=(), kind=jnp.bfloat16):
    factor_of = steps_of(key, extent, pieces, -0.22, 0.18) if pieces else 1.0
    array = jax.random.normal(key, extent, jnp.float32) * width * factor_of
    return jnp.minimum(jnp.maximum(array, -limit), limit).astype(kind)


def setup_inputs(seed: int = 0) -> dict:
    arg_keys = jax.random.split(jax.random.key(seed), 11)
    alpha = normal_values(arg_keys[0], (MEMBERS, VARS, LEVELS, NY, NX), 1.0, 6.0, ((0, 2), (3, 8), (4, 8)), jnp.float32)
    static_control = normal_values(arg_keys[1], (VARS, LEVELS, NY, NX), 1.0, 6.0, ((2, 8), (3, 8)), jnp.float32)
    perturbations = normal_values(arg_keys[2], (MEMBERS, VARS, LEVELS, NY, NX), 1.0, 6.0, ((0, 2), (3, 8), (4, 8)))
    sigma = jnp.clip(jnp.exp(math.log(2.0) - 1.3862944 * jax.random.uniform(arg_keys[3], (VARS, LEVELS, NY, NX), jnp.float32) ** steps_of(arg_keys[3], (VARS, LEVELS, NY, NX), ((2, 8), (3, 8)), -0.2, 0.2)), 0.5, 2.0)
    obs_coef = normal_values(arg_keys[4], (VARS, LEVELS, OBS), (VARS * LEVELS) ** -0.5, 1.5, ((2, 64),), jnp.float32)
    interp_weights = jnp.clip(0.1 + 0.79999997 * jax.random.uniform(arg_keys[5], (4, OBS), jnp.float32) ** steps_of(arg_keys[5], (4, OBS), ((1, 64),), -0.2, 0.2), 0.1, 0.9)
    obs_values = normal_values(arg_keys[6], (OBS,), 1.0, 6.0, ((0, 64),), jnp.float32)
    obs_weights = jnp.clip(jnp.exp(math.log(4.0) - 2.0794415 * jax.random.uniform(arg_keys[7], (OBS,), jnp.float32) ** steps_of(arg_keys[7], (OBS,), ((0, 64),), -0.2, 0.2)), 0.5, 4.0)
    obs_tile_keys = jax.random.split(jax.random.fold_in(arg_keys[8], 1), OBS // OBS_DEV)
    obs_tile_turns = jax.random.permutation(jax.random.fold_in(arg_keys[8], 3), OBS // OBS_DEV)
    obs_tile = jax.vmap(lambda own, number: assign_block(jax.random.fold_in(arg_keys[8], 2), own, number, OBS_DEV, TILES, 1, CAP, 2))(obs_tile_keys, obs_tile_turns).reshape((OBS, 1))
    obs_cell = touch_ends(jax.random.randint(arg_keys[9], (OBS,), 0, 4 * CY * CX), jax.random.fold_in(arg_keys[9], 1), 0, (4 * CY * CX) - 1).astype(jnp.int32)
    return {"alpha": alpha, "static_control": static_control, "perturbations": perturbations, "sigma": sigma, "obs_coef": obs_coef, "interp_weights": interp_weights, "obs_values": obs_values, "obs_weights": obs_weights, "obs_tile": obs_tile, "obs_cell": obs_cell}


diffusion = 0.45
loc_gain = 4.0
ens_share = 0.8660254037844386
static_share = 0.5
descent = 0.2

def relax(grid_field, axis_pos):
    count_cells = grid_field.shape[axis_pos]
    widths = [(0, 0)] * grid_field.ndim
    widths[axis_pos] = (1, 1)
    for repeat in range(4):
        padded = jnp.pad(grid_field, widths)
        lower = lax.slice_in_dim(padded, 0, count_cells, axis=axis_pos)
        upper = lax.slice_in_dim(padded, 2, count_cells + 2, axis=axis_pos)
        grid_field = grid_field + diffusion * (lower + upper - 2.0 * grid_field)
    return grid_field

def localize(grid_field):
    ndims = grid_field.ndim
    return loc_gain * relax(relax(grid_field, ndims - 1), ndims - 2)

def reference(alpha, static_control, perturbations, sigma, obs_coef, interp_weights, obs_values, obs_weights, obs_tile, obs_cell):
    channels = VARS * LEVELS
    ens_scale = ens_share / math.sqrt(MEMBERS - 1)
    tile_index = obs_tile[:, 0]
    fine_row = obs_cell // (2 * CX)
    fine_column = obs_cell % (2 * CX)
    coarse_row = tile_index % N_GY * CY + fine_row // 2
    coarse_column = tile_index // N_GY * CX + fine_column // 2
    base_index = (coarse_row * (NX + 1) + coarse_column).astype(jnp.int32)
    offsets = (0, 1, NX + 1, NX + 2)
    coefficients = obs_coef.reshape(channels, -1)

    def ensemble_step(carry, member):
        return (carry + member[1].astype(jnp.float32) * localize(member[0]), None)
    increment = jnp.zeros((VARS, LEVELS, NY, NX), jnp.float32)
    for iteration in range(ITERS):
        ensemble, unused = lax.scan(ensemble_step, jnp.zeros((VARS, LEVELS, NY, NX), jnp.float32), (alpha, perturbations))
        increment = ens_scale * ensemble + static_share * sigma * localize(static_control)
        padded = jnp.pad(increment.reshape(channels, NY, NX), ((0, 0), (0, 1), (0, 1))).reshape(channels, -1)
        mapped = jnp.zeros(coefficients.shape, jnp.float32)
        for corner in range(4):
            mapped = mapped + interp_weights[corner][None] * padded[:, base_index + offsets[corner]]
        model_obs = lax.optimization_barrier(jnp.sum(coefficients * mapped, axis=0))
        misfit = obs_weights * (model_obs - obs_values)
        spread = coefficients * misfit[None]
        adjoint = jnp.zeros((channels, (NY + 1) * (NX + 1)), jnp.float32)
        for corner in range(4):
            adjoint = adjoint.at[:, base_index + offsets[corner]].add(interp_weights[corner][None] * spread)
        adjoint = adjoint.reshape(channels, NY + 1, NX + 1)[:, :NY, :NX].reshape(VARS, LEVELS, NY, NX)

        def member_gradient(member):
            return member[0] + ens_scale * localize(member[1].astype(jnp.float32) * adjoint)
        gradient = lax.map(member_gradient, (alpha, perturbations))
        static_gradient = static_control + static_share * localize(sigma * adjoint)
        alpha = alpha - descent * gradient
        static_control = static_control - descent * static_gradient
    return (alpha, static_control, increment)
```

```python
import math

import jax
import jax.numpy as jnp
from jax import lax
from jax.experimental import pallas as pl
from jax.experimental.pallas import tpu as pltpu
from jax.sharding import PartitionSpec as P

f32, bf16, i32 = jnp.float32, jnp.bfloat16, jnp.int32
MESH = pl.DeviceIdType.MESH

MEMBERS = 128
ITERS = 2
ENS = 0.8660254037844386 / math.sqrt(MEMBERS - 1)
STATIC = 0.5
DESCENT = 0.2
GAIN = 4.0


def four_passes():
    taps = [1.0]
    for _ in range(4):
        wide = [0.0] * (len(taps) + 2)
        for i, t in enumerate(taps):
            wide[i] += 0.45 * t
            wide[i + 1] += 0.1 * t
            wide[i + 2] += 0.45 * t
        taps = wide
    return taps[4:]


TAP = four_passes()

CHUNK = 256
CHUNKS = 16
BELOW, ABOVE, OWN = 0, 1, 2


def split2(x):
    hi = x.astype(bf16)
    return hi, (x - hi.astype(f32)).astype(bf16)


def split3(x):
    hi = x.astype(bf16)
    rest = x - hi.astype(f32)
    mid = rest.astype(bf16)
    return hi, mid, (rest - mid.astype(f32)).astype(bf16)


def dot(a, b):
    return jnp.dot(a, b, preferred_element_type=f32)


def dot_nt(a, b):
    return lax.dot_general(a, b, (((1,), (1,)), ((), ())), preferred_element_type=f32)


def iota(shape, dim):
    return lax.broadcasted_iota(i32, shape, dim)


def tap_of(distance):
    out = jnp.zeros(distance.shape, f32)
    for d in range(5):
        out = jnp.where(distance == d, TAP[d], out)
    return out


def body(
    alpha, pert, stat, sig, coef, interp, oval, owgt, tile, cell,
    alpha_out, stat_out, inc_out,
    buf, xb, pack, side, wf, wa, y_s, yh_s, vh_s, eb, eh_s, msend, mrecv,
    f_dn, f_up, f_up2, f_mem, nsend, nrecv, gb, g_dn, g_up, g_dn2, gx_s, gh_s,
    feat, key_s, sb, tb, rb, qt, cm, ov, lh, gacc,
    ps, pr, fs, fr, as_, ar, o1s, o1r, o2s, o2r, ms, mr, bs, br, ns, nr, ds_, dr,
):
    mem, gx, gy = lax.axis_index("mem"), lax.axis_index("gx"), lax.axis_index("gy")
    ngx, ngy = lax.axis_size("gx"), lax.axis_size("gy")
    par = lax.rem(gy, 2)
    partner = gy + 1 - 2 * par
    gy_f = gy + 2 - 4 * par
    has_f = (gy_f >= 0) & (gy_f < ngy)
    gy_b = gy - 2 + 4 * par
    has_b = (gy_b >= 0) & (gy_b < ngy)
    top = jnp.where(gy == 0, 1.0, 0.0)
    bottom = jnp.where(gy == ngy - 1, 1.0, 0.0)
    west = jnp.where(gx == 0, 1.0, 0.0)
    east = jnp.where(gx == ngx - 1, 1.0, 0.0)
    has_l, has_r = gx > 0, gx < ngx - 1
    lane8 = iota((8, 128), 1)

    barrier = pltpu.get_barrier_semaphore()
    for j in range(1, ngx):
        pl.semaphore_signal(barrier, inc=1, device_id=(mem, lax.rem(gx + j, ngx), gy), device_id_type=MESH)
    for j in range(1, ngy):
        pl.semaphore_signal(barrier, inc=1, device_id=(mem, gx, lax.rem(gy + j, ngy)), device_id_type=MESH)
    for j in range(ngy):
        pl.semaphore_signal(barrier, inc=1, device_id=(1 - mem, gx, lax.rem(gy + j, ngy)), device_id_type=MESH)
    pl.semaphore_wait(barrier, ngx + 2 * ngy - 2)

    def remote(src, dst, s, r, device):
        return pltpu.make_async_remote_copy(
            src_ref=src, dst_ref=dst, send_sem=s, recv_sem=r, device_id=device, device_id_type=MESH
        )

    def rows_of(i):
        return pl.ds(pl.multiple_of(i * CHUNK, CHUNK), CHUNK)

    def direct(i):
        return remote(pert.at[rows_of(i)], buf.at[par, rows_of(i)], ps.at[i], pr.at[i], (mem, gx, partner))

    def arrival(i):
        return remote(pert.at[rows_of(i)], buf.at[1 - par, rows_of(i)], ps.at[i], pr.at[i], (mem, gx, partner))

    def forward(i):
        return remote(
            buf.at[1 - par, rows_of(i)], buf.at[par, rows_of(i)], fs.at[i], fr.at[i],
            (mem, gx, lax.rem(gy_f + ngy, ngy)),
        )

    def direct_x():
        return remote(xb.at[OWN], xb.at[par], ps.at[CHUNKS], pr.at[CHUNKS], (mem, gx, partner))

    def arrival_x():
        return remote(xb.at[OWN], xb.at[1 - par], ps.at[CHUNKS], pr.at[CHUNKS], (mem, gx, partner))

    def forward_x():
        return remote(
            xb.at[1 - par], xb.at[par], fs.at[CHUNKS], fr.at[CHUNKS], (mem, gx, lax.rem(gy_f + ngy, ngy))
        )

    def pump(i):
        arrival(i).wait_recv()

        @pl.when(has_f)
        def _():
            forward(i).start()

    def landed(i):
        @pl.when(has_b)
        def _():
            forward(i).wait_recv()

    for i in range(CHUNKS // 2):
        direct(i).start()

    @pl.when(jnp.logical_not(has_b))
    def _():
        @pl.loop(0, CHUNKS)
        def _(i):
            buf[par, rows_of(i), :] = jnp.zeros((CHUNK, 128), f32)

        xb[par] = jnp.zeros(xb.shape[1:], f32)

    @pl.when(gx == 0)
    def _():
        side[0] = jnp.zeros(side.shape[1:], f32)
        for it in range(ITERS):
            mrecv[it, 0] = jnp.zeros(mrecv.shape[2:], f32)
            nrecv[it, 0] = jnp.zeros(nrecv.shape[2:], f32)

    @pl.when(gx == ngx - 1)
    def _():
        side[1] = jnp.zeros(side.shape[1:], f32)
        for it in range(ITERS):
            mrecv[it, 1] = jnp.zeros(mrecv.shape[2:], f32)
            nrecv[it, 1] = jnp.zeros(nrecv.shape[2:], f32)

    @pl.when(gy == 0)
    def _():
        f_dn[...] = jnp.zeros(f_dn.shape, f32)
        g_dn[...] = jnp.zeros(g_dn.shape, f32)

    @pl.when(gy < 2)
    def _():
        g_dn2[...] = jnp.zeros(g_dn2.shape, f32)

    @pl.when(gy == ngy - 1)
    def _():
        f_up[...] = jnp.zeros(f_up.shape, f32)
        g_up[...] = jnp.zeros(g_up.shape, f32)

    @pl.when(gy >= ngy - 2)
    def _():
        f_up2[...] = jnp.zeros(f_up2.shape, f32)

    pack[...] = jnp.zeros(pack.shape, f32)
    px, pa = iota((128, 128), 0), iota((128, 128), 1)

    def selection(i):
        j = pa - 8 * i
        last = jnp.where((j >= 0) & (j < 4) & (px == 124 + j), 1.0, 0.0)
        first = jnp.where((j >= 4) & (j < 8) & (px == j - 4), 1.0, 0.0)
        return jnp.concatenate([last, first], axis=1).astype(bf16)

    @pl.loop(0, CHUNKS)
    def _(i):
        picked = dot(pert[rows_of(i), :].astype(bf16), selection(i))
        pack[0, :CHUNK] += picked[:, :128]
        pack[1, :CHUNK] += picked[:, 128:]

    scaled = sig[...] * (STATIC / ENS)
    xb[OWN, 320:384] = scaled
    hi, mid, lo = split3(scaled)
    sel = selection(0)
    picked = dot(hi, sel) + dot(mid, sel) + dot(lo, sel)
    pack[0, CHUNK:] = picked[:, :128]
    pack[1, CHUNK:] = picked[:, 128:]

    right, left = lax.rem(gx + 1, ngx), lax.rem(gx + ngx - 1, ngx)

    def to_right(src, dst, sems, recvs):
        return remote(src, dst, sems.at[0], recvs.at[0], (mem, right, gy))

    def to_left(src, dst, sems, recvs):
        return remote(src, dst, sems.at[1], recvs.at[1], (mem, left, gy))

    def exchange_lon(a_src, b_src, dst, sems, recvs):
        a, b = to_right(a_src, dst.at[0], sems, recvs), to_left(b_src, dst.at[1], sems, recvs)

        @pl.when(has_r)
        def _():
            a.start()

        @pl.when(has_l)
        def _():
            b.start()

        @pl.when(has_l)
        def _():
            a.wait_recv()

        @pl.when(has_r)
        def _():
            b.wait_recv()

        @pl.when(has_r)
        def _():
            a.wait_send()

        @pl.when(has_l)
        def _():
            b.wait_send()

    exchange_lon(pack.at[0], pack.at[1], side, as_, ar)
    xb[OWN, :320] = side[0] + side[1]
    direct_x().start()
    for i in range(CHUNKS // 2, CHUNKS):
        direct(i).start()
    pump(0)

    main = tap_of(jnp.abs(px - pa)) - west * tap_of(px + pa + 2) - east * tap_of(256 - px - pa)
    main_hi, main_lo = split2(main)

    @pl.loop(0, CHUNKS)
    def _(i):
        j = pa - 8 * i
        d = jnp.where(j < 4, px + 4 - j, 124 + j - px)
        h_hi, h_lo = split2(jnp.where((j >= 0) & (j < 8), tap_of(d), 0.0))
        wf[i, 0] = jnp.concatenate([main_hi, h_hi], axis=1)
        wf[i, 1] = jnp.concatenate([main_lo, h_lo], axis=1)
        j = px - 8 * i
        d = jnp.where(j < 4, pa + 4 - j, 124 + j - pa)
        h_hi, h_lo = split2(jnp.where((j >= 0) & (j < 8), tap_of(d), 0.0))
        wa[i, 0] = jnp.concatenate([main_hi, h_hi], axis=0)
        wa[i, 1] = jnp.concatenate([main_lo, h_lo], axis=0)

    pump(1)
    pump(2)

    tri = jnp.where(px < pa, 1.0, 0.0).astype(bf16)
    totals = jnp.zeros((64, 1), f32)
    for b in range(8):
        t = tile[:, b * 128 : (b + 1) * 128]
        one = jnp.where(iota((64, 128), 0) == t, 1.0, 0.0)
        before = dot(one.astype(bf16), tri) + totals
        rank = jnp.sum(before * one, axis=0, keepdims=True).astype(i32)
        totals = totals + jnp.sum(one, axis=1, keepdims=True)
        key_s[0:1, b * 128 : (b + 1) * 128] = (rank >> 3) * 512 + t * 8 + (rank & 7)
    feat[...] = jnp.zeros(feat.shape, f32)
    feat[0:16] = coef[...]
    feat[16:20] = interp[...]
    feat[20:21] = (cell[...] >> 9).astype(f32)
    feat[21:22] = ((cell[...] & 255) >> 1).astype(f32)
    feat[22:23] = oval[...]
    feat[23:24] = owgt[...]
    zero32 = jnp.zeros((32, 1024), bf16)

    @pl.loop(0, 4)
    def _(q):
        total = jnp.zeros((128, 128), f32)
        key = key_s[0:1, :]
        parts = split3(feat[...])
        for g in range(4):
            pick = jnp.where(iota((128, 1024), 0) + (g * 512 + q * 128) == key, 1.0, 0.0).astype(bf16)
            for part in parts:
                placed = jnp.concatenate([part if n == g else zero32 for n in range(4)], axis=0)
                total = total + dot_nt(pick, placed)
        sb[pl.ds(pl.multiple_of(q * 128, 128), 128), :] = total

    pump(3)
    pump(4)

    def o1(j):
        to = lax.rem(gx + j, ngx)
        return remote(
            sb.at[pl.ds(pl.multiple_of(to * 64, 64), 64)], tb.at[gx], o1s.at[j], o1r.at[gx], (mem, to, gy)
        )

    def o1_in(j):
        of = lax.rem(gx - j + ngx, ngx)
        return remote(sb.at[pl.ds(0, 64)], tb.at[of], o1s.at[j], o1r.at[of], (mem, of, gy))

    for j in range(1, ngx):
        o1(j).start()
    tb[gx] = sb[pl.ds(pl.multiple_of(gx * 64, 64), 64), :]
    for j in range(1, ngx):
        o1_in(j).wait_recv()

    def near(j):
        return mem if j % 2 == 0 else 1 - mem

    def o2(j):
        to = lax.rem(gy + j, ngy)
        return remote(
            tb.at[:, pl.ds(pl.multiple_of(to * 8, 8), 8)], rb.at[gy], o2s.at[j], o2r.at[gy], (near(j), gx, to)
        )

    def o2_in(j):
        of = lax.rem(gy - j + ngy, ngy)
        return remote(tb.at[:, pl.ds(0, 8)], rb.at[of], o2s.at[j], o2r.at[of], (near(j), gx, of))

    for j in range(1, ngy):
        o2(j).start()
    rb[gy] = tb[:, pl.ds(pl.multiple_of(gy * 8, 8), 8), :]
    pump(5)
    pump(6)
    for j in range(1, ngy):
        o2_in(j).wait_recv()

    @pl.loop(0, 4)
    def _(q):
        turned = rb[pl.ds(q * 2, 2)].reshape(128, 128).T
        for g in range(4):
            at = pl.ds(pl.multiple_of((g * 4 + q) * 128, 128), 128)
            f = turned[g * 32 : (g + 1) * 32]
            rr, xx = f[20:21], f[21:22]
            for dc in range(2):
                upper, lower = f[16 + dc : 17 + dc], f[18 + dc : 19 + dc]
                for row in range(5):
                    w = jnp.where(rr == float(row), upper, 0.0) + jnp.where(rr == float(row - 1), lower, 0.0)
                    qt[dc * 80 + row * 16 : dc * 80 + row * 16 + 16, at] = f[0:16] * w
            cm[:, at] = jnp.where(px.astype(f32) == xx, 1.0, 0.0).astype(bf16)
            ov[0:1, at] = f[22:23]
            ov[1:2, at] = f[23:24]

    pump(7)

    def lat(row, i):
        d = abs(row - i)
        if d > 4:
            return None
        c = GAIN * TAP[d]
        if 0 <= row < 4:
            if row + i + 2 <= 4:
                c = c - top * (GAIN * TAP[row + i + 2])
            if 8 - row - i <= 4:
                c = c - bottom * (GAIN * TAP[8 - row - i])
        return c

    COEF = [[lat(row - 4, i) for i in range(4)] for row in range(12)]

    def lat_out(y):
        z = []
        for row in range(12):
            acc = None
            for i in range(4):
                if COEF[row][i] is not None:
                    term = COEF[row][i] * y[i]
                    acc = term if acc is None else acc + term
            z.append(acc)
        return z

    def lat_in(q):
        v = []
        for i in range(4):
            acc = None
            for row in range(12):
                if COEF[row][i] is not None:
                    term = COEF[row][i] * q[row]
                    acc = term if acc is None else acc + term
            v.append(acc)
        return v

    def every4(start):
        return pl.ds(start, 8, stride=4)

    def pert_rows(start):
        at = [every4(start + r) for r in range(4)]
        return (
            [buf[BELOW, a, :] for a in at] + [pert[a, :] for a in at] + [buf[ABOVE, a, :] for a in at]
        )

    def xb_rows(start):
        return [xb[b, every4(start + r), :] for b in (BELOW, OWN, ABOVE) for r in range(4)]

    def lon(x, w, i):
        hi, lo = split2(x)
        return dot(hi, w[i, 0]) + dot(lo, w[i, 0]) + dot(hi, w[i, 1])

    def eb_at(row, c8):
        return pl.ds((row + 1) * 16 + c8 * 8, 8)

    def accumulate(y, first, count, rows):
        for c8 in range(2):
            acc = [eb[eb_at(row, c8), :] for row in range(12)]
            for k in range(count):
                start = k * 64 + c8 * 32
                z = lat_out([y[every4(first + start + r), :] for r in range(4)])
                p = rows(start)
                acc = [acc[row] + z[row] * p[row] for row in range(12)]
            for row in range(12):
                eb[eb_at(row, c8), :] = acc[row]

    def clear():
        eb[...] = jnp.zeros(eb.shape, f32)
        yh_s[...] = jnp.zeros(yh_s.shape, f32)

    def member_chunk(src, i):
        wide = lon(src[rows_of(i), :], wf, i)
        y_s[:CHUNK] = wide[:, :128]
        yh_s[:CHUNK] += wide[:, 128:]
        accumulate(y_s, 0, 4, lambda start: pert_rows(pl.multiple_of(i * CHUNK, CHUNK) + start))

    def static_chunk(src):
        wide = lon(src[...] * jnp.where(mem == 0, 1.0, 0.0), wf, 0)
        y_s[CHUNK:] = wide[:, :128]
        yh_s[CHUNK:] = wide[:, 128:]
        accumulate(y_s, CHUNK, 1, lambda start: xb_rows(320 + start))

    lane192 = iota((192, 128), 1)
    lane16 = iota((16, 128), 1)

    def around(x):
        for s in (8, 16, 32, 64):
            x = x + pltpu.roll(x, s, 1)
        return x

    def reduce_and_observe(it):
        for c8 in range(2):
            acc = [jnp.zeros((8, 128), f32) for _ in range(12)]
            for k in range(5):
                start = k * 64 + c8 * 32
                z = lat_out([yh_s[every4(start + r), :] for r in range(4)])
                p = xb_rows(start)
                acc = [acc[row] + z[row] * p[row] for row in range(12)]
            for row in range(12):
                eh_s[row * 16 + c8 * 8 : row * 16 + c8 * 8 + 8] = acc[row]
        eh = around(eh_s[...])
        e = eb[16:208]
        msend[...] = jnp.where(
            lane192 < 8,
            pltpu.roll(eh, 124, 1),
            jnp.where(lane192 >= 120, pltpu.roll(eh, 4, 1), jnp.where(lane192 == 16, pltpu.roll(e, 16, 1), 0.0)),
        )
        exchange_lon(msend, msend, mrecv.at[it], ms.at[it], mr.at[it])
        m_l, m_r = mrecv[it, 0], mrecv[it, 1]
        eb[16:208] = e + jnp.where(lane192 < 4, m_l, 0.0) + jnp.where(lane192 >= 124, m_r, 0.0)
        beyond = pltpu.roll(m_r, 112, 1) + msend[...]
        xv = jnp.zeros((16, 128), f32)
        for row in range(12):
            b = beyond[row * 16 : row * 16 + 16]
            xv = xv + jnp.where(lane16 == row, pltpu.roll(b, row, 1) if row else b, 0.0)
        eb[0:16] = xv
        eb[208:224] = xv

        def sends():
            out = []
            n = 0
            for flip in range(2):
                m = mem if flip == 0 else 1 - mem
                out.append((gy < ngy - 1, remote(eb.at[pl.ds(144, 80)], f_dn.at[it, mem], bs.at[it, n], br.at[it, n], (m, gx, lax.rem(gy + 1, ngy)))))
                out.append((gy > 0, remote(eb.at[pl.ds(0, 96)], f_up.at[it, mem], bs.at[it, n + 1], br.at[it, n + 1], (m, gx, lax.rem(gy + ngy - 1, ngy)))))
                out.append((gy > 1, remote(eb.at[pl.ds(0, 32)], f_up2.at[it, mem], bs.at[it, n + 2], br.at[it, n + 2], (m, gx, lax.rem(gy + ngy - 2, ngy)))))
                n += 3
            out.append((None, remote(eb.at[pl.ds(80, 80)], f_mem.at[it, pl.ds(0, 80)], bs.at[it, 6], br.at[it, 6], (1 - mem, gx, gy))))
            out.append((None, remote(eb.at[pl.ds(208, 16)], f_mem.at[it, pl.ds(80, 16)], bs.at[it, 7], br.at[it, 7], (1 - mem, gx, gy))))
            return out

        def receives():
            out = []
            n = 0
            for flip in range(2):
                m = mem if flip == 0 else 1 - mem
                out.append((gy > 0, remote(eb.at[pl.ds(144, 80)], f_dn.at[it, m], bs.at[it, n], br.at[it, n], (mem, gx, gy))))
                out.append((gy < ngy - 1, remote(eb.at[pl.ds(0, 96)], f_up.at[it, m], bs.at[it, n + 1], br.at[it, n + 1], (mem, gx, gy))))
                out.append((gy < ngy - 2, remote(eb.at[pl.ds(0, 32)], f_up2.at[it, m], bs.at[it, n + 2], br.at[it, n + 2], (mem, gx, gy))))
                n += 3
            out.append((None, remote(eb.at[pl.ds(80, 80)], f_mem.at[it, pl.ds(0, 80)], bs.at[it, 6], br.at[it, 6], (mem, gx, gy))))
            out.append((None, remote(eb.at[pl.ds(208, 16)], f_mem.at[it, pl.ds(80, 16)], bs.at[it, 7], br.at[it, 7], (mem, gx, gy))))
            return out

        run(sends(), "start")
        run(receives(), "wait_recv")
        run(sends(), "wait_send")

        def block_sum(own, own_xv, m):
            rows = []
            for r in range(5):
                t = own(r) + f_up[it, m, (r + 1) * 16 : (r + 2) * 16]
                if r < 4:
                    t = t + f_dn[it, m, r * 16 : r * 16 + 16]
                else:
                    t = t + f_up2[it, m, 16:32]
                rows.append(t)
            x = own_xv + pltpu.roll(f_dn[it, m, 64:80], 124, 1) + pltpu.roll(f_up[it, m, 0:16], 4, 1)
            x = x + pltpu.roll(jnp.where(lane16 == 0, f_up2[it, m, 0:16], 0.0), 8, 1)
            return rows, x

        mine, x_mine = block_sum(lambda r: eb[80 + r * 16 : 96 + r * 16], eb[208:224], mem)
        theirs, x_theirs = block_sum(lambda r: f_mem[it, r * 16 : r * 16 + 16], f_mem[it, 80:96], 1 - mem)
        x = (x_mine + x_theirs) * ENS
        for r in range(5):
            dx = (mine[r] + theirs[r]) * ENS
            moved = jnp.where(lane16 == 127, pltpu.roll(x, 127 - (r + 4), 1), pltpu.roll(dx, 127, 1))
            if it == ITERS - 1 and r < 4:
                inc_out[every4(r), :] = dx[:8]
                inc_out[every4(32 + r), :] = dx[8:]
            for n, v in ((0, dx), (1, moved)):
                hi, lo = split2(v)
                lh[0, n * 80 + r * 16 : n * 80 + r * 16 + 16] = hi
                lh[1, n * 80 + r * 16 : n * 80 + r * 16 + 16] = lo

        gacc[...] = jnp.zeros(gacc.shape, f32)

        @pl.loop(0, 8)
        def _(n):
            at = pl.ds(pl.multiple_of(n * 256, 256), 256)
            c = cm[:, at]
            u = dot(lh[0], c) + dot(lh[1], c)
            q = qt[:, at]
            hx = jnp.sum(q * u, axis=0, keepdims=True)
            misfit = ov[1:2, at] * (hx - ov[0:1, at])
            hi, lo = split2(q * misfit)
            gacc[...] += dot_nt(hi, c) + dot_nt(lo, c)

        lane80 = iota((80, 128), 1)
        g0, g1 = gacc[0:80], gacc[80:160]
        g5 = g0 + jnp.where(lane80 == 0, 0.0, pltpu.roll(g1, 1, 1))
        nsend[...] = jnp.where(lane80 == 64, pltpu.roll(g1, 65, 1), g5)
        exchange_lon(nsend, nsend, nrecv.at[it], ns.at[it], nr.at[it])
        n_l, n_r = nrecv[it, 0], nrecv[it, 1]
        gb[16:96] = g5 + jnp.where(lane80 == 0, pltpu.roll(n_l, 64, 1), 0.0)
        halo = jnp.where(
            lane80 < 4,
            pltpu.roll(n_l, 4, 1),
            jnp.where(lane80 < 8, pltpu.roll(n_r, 4, 1) + jnp.where(lane80 == 4, pltpu.roll(g1, 5, 1), 0.0), 0.0),
        )
        ghv = halo[0:16]
        for r in range(1, 5):
            ghv = ghv + pltpu.roll(halo[r * 16 : r * 16 + 16], 8 * r, 1)
        gb[0:16] = ghv
        gb[96:112] = ghv

        def sends_g():
            return [
                (gy < ngy - 1, remote(gb.at[pl.ds(16, 96)], g_dn.at[it], ds_.at[it, 0], dr.at[it, 0], (1 - mem, gx, lax.rem(gy + 1, ngy)))),
                (gy > 0, remote(gb.at[pl.ds(0, 80)], g_up.at[it], ds_.at[it, 1], dr.at[it, 1], (1 - mem, gx, lax.rem(gy + ngy - 1, ngy)))),
                (gy < ngy - 2, remote(gb.at[pl.ds(80, 32)], g_dn2.at[it], ds_.at[it, 2], dr.at[it, 2], (mem, gx, lax.rem(gy + 2, ngy)))),
            ]

        def receives_g():
            both = sends_g()
            return [(gy > 0, both[0][1]), (gy < ngy - 1, both[1][1]), (gy > 1, both[2][1])]

        run(sends_g(), "start")
        run(receives_g(), "wait_recv")
        run(sends_g(), "wait_send")

        def ext(v, r):
            return jnp.where(lane16 < 8, pltpu.roll(v, 128 - 8 * r, 1) if r else v, 0.0)

        for r in range(4):
            below, own, above = g_dn[it, r * 16 : r * 16 + 16], gb[16 + r * 16 : 32 + r * 16], g_up[it, 16 + r * 16 : 32 + r * 16]
            hb, ho, ha = ext(g_dn[it, 80:96], r), ext(ghv, r), ext(g_up[it, 0:16], r)
            if r == 0:
                below, hb = below + g_dn2[it, 0:16], hb + ext(g_dn2[it, 16:32], 4)
                own, ho = own + g_dn[it, 64:80], ho + ext(g_dn[it, 80:96], 4)
                above, ha = above + gb[80:96], ha + ext(ghv, 4)
            for n, (v, h) in enumerate(((below, hb), (own, ho), (above, ha))):
                at = n * 64 + r * 16
                gx_s[at : at + 16] = v
                gh_s[at : at + 16] = h
        gh_s[...] = around(gh_s[...])

        for c8 in range(2):
            g = [gh_s[row * 16 + c8 * 8 : row * 16 + c8 * 8 + 8] for row in range(12)]
            for k in range(5):
                start = k * 64 + c8 * 32
                p = xb_rows(start)
                v = lat_in([p[row] * g[row] for row in range(12)])
                for r in range(4):
                    yh_s[every4(start + r), :] = v[r]
        hi, lo = split2(yh_s[...])
        vh_s[0] = hi
        vh_s[1] = lo

    def run(copies, what):
        for condition, copy in copies:
            if condition is None:
                getattr(copy, what)()
            else:
                pl.when(condition)(lambda copy=copy: getattr(copy, what)())

    def gradient(first, count, halo, rows, i):
        for c8 in range(2):
            g = [gx_s[row * 16 + c8 * 8 : row * 16 + c8 * 8 + 8] for row in range(12)]
            for k in range(count):
                start = k * 64 + c8 * 32
                p = rows(start)
                v = lat_in([p[row] * g[row] for row in range(12)])
                for r in range(4):
                    y_s[every4(first + start + r), :] = v[r]
        n = count * 64
        hi, lo = split2(y_s[first : first + n])
        hi = jnp.concatenate([hi, vh_s[0, halo : halo + n]], axis=1)
        lo = jnp.concatenate([lo, vh_s[1, halo : halo + n]], axis=1)
        return dot(hi, wa[i, 0]) + dot(lo, wa[i, 0]) + dot(hi, wa[i, 1])

    def member_step(src, i):
        u = gradient(0, 4, 0, lambda start: pert_rows(pl.multiple_of(i * CHUNK, CHUNK) + start), i)
        alpha_out[rows_of(i), :] = (1.0 - DESCENT) * src[rows_of(i), :] - (DESCENT * ENS) * u

    def static_step(src):
        u = gradient(CHUNK, 1, CHUNK, lambda start: xb_rows(320 + start), 0)
        stat_out[...] = (1.0 - DESCENT) * src[...] - (DESCENT * ENS) * u

    clear()

    @pl.loop(0, CHUNKS // 2)
    def _(i):
        pump(i + CHUNKS // 2)
        landed(i)
        member_chunk(alpha, i)

    arrival_x().wait_recv()

    @pl.when(has_f)
    def _():
        forward_x().start()

    @pl.loop(CHUNKS // 2, CHUNKS)
    def _(i):
        landed(i)
        member_chunk(alpha, i)

    @pl.when(has_b)
    def _():
        forward_x().wait_recv()

    static_chunk(stat)
    reduce_and_observe(0)
    clear()

    @pl.loop(0, CHUNKS)
    def _(i):
        member_step(alpha, i)
        member_chunk(alpha_out, i)

    static_step(stat)
    static_chunk(stat_out)
    reduce_and_observe(1)

    @pl.loop(0, CHUNKS)
    def _(i):
        member_step(alpha_out, i)

    static_step(stat_out)

    for i in range(CHUNKS):
        direct(i).wait_send()
    direct_x().wait_send()

    @pl.when(has_f)
    def _():
        for i in range(CHUNKS):
            forward(i).wait_send()
        forward_x().wait_send()

    for j in range(1, ngx):
        o1(j).wait_send()
    for j in range(1, ngy):
        o2(j).wait_send()


def per_device(
    alpha, static_control, perturbations, sigma, obs_coef, interp_weights, obs_values, obs_weights, obs_tile, obs_cell
):
    rows = alpha.size // 128
    vmem = pl.BlockSpec(memory_space=pltpu.VMEM)
    args = (
        alpha.reshape(rows, 128),
        perturbations.astype(f32).reshape(rows, 128),
        static_control.reshape(64, 128),
        sigma.reshape(64, 128),
        obs_coef.reshape(16, 1024),
        interp_weights,
        obs_values.reshape(1, 1024),
        obs_weights.reshape(1, 1024),
        obs_tile.reshape(1, 1024),
        obs_cell.reshape(1, 1024),
    )
    dma = pltpu.SemaphoreType.DMA
    V = pltpu.VMEM
    scratch = [
        V((2, rows, 128), f32),
        V((3, 384, 128), f32),
        V((2, 320, 128), f32),
        V((2, 320, 128), f32),
        V((CHUNKS, 2, 128, 256), bf16),
        V((CHUNKS, 2, 256, 128), bf16),
        V((320, 128), f32),
        V((320, 128), f32),
        V((2, 320, 128), bf16),
        V((224, 128), f32),
        V((192, 128), f32),
        V((192, 128), f32),
        V((ITERS, 2, 192, 128), f32),
        V((ITERS, 2, 80, 128), f32),
        V((ITERS, 2, 96, 128), f32),
        V((ITERS, 2, 32, 128), f32),
        V((ITERS, 96, 128), f32),
        V((80, 128), f32),
        V((ITERS, 2, 80, 128), f32),
        V((112, 128), f32),
        V((ITERS, 96, 128), f32),
        V((ITERS, 80, 128), f32),
        V((ITERS, 32, 128), f32),
        V((192, 128), f32),
        V((192, 128), f32),
        V((32, 1024), f32),
        V((8, 1024), i32),
        V((512, 128), f32),
        V((8, 64, 128), f32),
        V((8, 8, 8, 128), f32),
        V((160, 2048), f32),
        V((128, 2048), bf16),
        V((8, 2048), f32),
        V((2, 160, 128), bf16),
        V((160, 128), f32),
        dma((CHUNKS + 1,)), dma((CHUNKS + 1,)), dma((CHUNKS + 1,)), dma((CHUNKS + 1,)),
        dma((2,)), dma((2,)),
        dma((8,)), dma((8,)), dma((8,)), dma((8,)),
        dma((ITERS, 2)), dma((ITERS, 2)),
        dma((ITERS, 8)), dma((ITERS, 8)),
        dma((ITERS, 2)), dma((ITERS, 2)),
        dma((ITERS, 3)), dma((ITERS, 3)),
    ]
    outs = pl.pallas_call(
        body,
        out_shape=(
            jax.ShapeDtypeStruct((rows, 128), f32),
            jax.ShapeDtypeStruct((64, 128), f32),
            jax.ShapeDtypeStruct((64, 128), f32),
        ),
        in_specs=[vmem] * len(args),
        out_specs=(vmem,) * 3,
        scratch_shapes=scratch,
        name="assimilate",
        compiler_params=pltpu.CompilerParams(
            collective_id=0, has_side_effects=True, vmem_limit_bytes=56 << 20
        ),
    )(*args)
    return (
        outs[0].reshape(alpha.shape),
        outs[1].reshape(static_control.shape),
        outs[2].reshape(static_control.shape),
    )


def solution(mesh):
    placed = (
        P("mem", None, None, "gy", "gx"),
        P(None, None, "gy", "gx"),
        P("mem", None, None, "gy", "gx"),
        P(None, None, "gy", "gx"),
        P(None, None, ("gx", "gy")),
        P(None, ("gx", "gy")),
        P(("gx", "gy")),
        P(("gx", "gy")),
        P(("gx", "gy"), None),
        P(("gx", "gy")),
    )
    return jax.shard_map(
        per_device,
        mesh=mesh,
        in_specs=placed,
        out_specs=(
            P("mem", None, None, "gy", "gx"),
            P(None, None, "gy", "gx"),
            P(None, None, "gy", "gx"),
        ),
        check_vma=False,
    )
```

```python
import math

import jax
import jax.numpy as jnp
from jax import lax
from jax.experimental import pallas as pl
from jax.experimental.pallas import tpu as pltpu
from jax.sharding import PartitionSpec as P

f32, bf16, i32 = jnp.float32, jnp.bfloat16, jnp.int32
MESH = pl.DeviceIdType.MESH

MEMBERS = 128
ITERS = 2
ENS = 0.8660254037844386 / math.sqrt(MEMBERS - 1)
STATIC = 0.5
DESCENT = 0.2
GAIN = 4.0


def four_passes():
    taps = [1.0]
    for _ in range(4):
        wide = [0.0] * (len(taps) + 2)
        for i, t in enumerate(taps):
            wide[i] += 0.45 * t
            wide[i + 1] += 0.1 * t
            wide[i + 2] += 0.45 * t
        taps = wide
    return taps[4:]


TAP = four_passes()

CHUNK = 256
CHUNKS = 16
AHEAD = 5
BELOW, ABOVE, OWN = 0, 1, 2


def split2(x):
    hi = x.astype(bf16)
    return hi, (x - hi.astype(f32)).astype(bf16)


def split3(x):
    hi = x.astype(bf16)
    rest = x - hi.astype(f32)
    mid = rest.astype(bf16)
    return hi, mid, (rest - mid.astype(f32)).astype(bf16)


def dot(a, b):
    return jnp.dot(a, b, preferred_element_type=f32)


def dot_nt(a, b):
    return lax.dot_general(a, b, (((1,), (1,)), ((), ())), preferred_element_type=f32)


def iota(shape, dim):
    return lax.broadcasted_iota(i32, shape, dim)


def tap_of(distance):
    out = jnp.zeros(distance.shape, f32)
    for d in range(5):
        out = jnp.where(distance == d, TAP[d], out)
    return out


def body(
    alpha, pert, stat, sig, coef, interp, oval, owgt, tile, cell,
    alpha_out, stat_out, inc_out,
    own, work, buf, xb, pack, side, wf, wa, y_s, yh_s, vh_s, eb, eh_s, msend, mrecv,
    f_dn, f_up, f_up2, f_mem, nsend, nrecv, gb, g_dn, g_up, g_dn2, gx_s, gh_s,
    feat, ft, key_s, sb, tb, rb, qt, cm, ov, lh, gacc,
    ps, pr, fs, fr, as_, ar, o1s, o1r, o2s, o2r, ms, mr, bs, br, ns, nr, ds_, dr, al, ao,
):
    mem, gx, gy = lax.axis_index("mem"), lax.axis_index("gx"), lax.axis_index("gy")
    ngx, ngy = lax.axis_size("gx"), lax.axis_size("gy")
    par = lax.rem(gy, 2)
    partner = gy + 1 - 2 * par
    gy_f = gy + 2 - 4 * par
    has_f = (gy_f >= 0) & (gy_f < ngy)
    gy_b = gy - 2 + 4 * par
    has_b = (gy_b >= 0) & (gy_b < ngy)
    top = jnp.where(gy == 0, 1.0, 0.0)
    bottom = jnp.where(gy == ngy - 1, 1.0, 0.0)
    west = jnp.where(gx == 0, 1.0, 0.0)
    east = jnp.where(gx == ngx - 1, 1.0, 0.0)
    has_l, has_r = gx > 0, gx < ngx - 1
    lane8 = iota((8, 128), 1)

    barrier = pltpu.get_barrier_semaphore()
    for j in range(1, ngx):
        pl.semaphore_signal(barrier, inc=1, device_id=(mem, lax.rem(gx + j, ngx), gy), device_id_type=MESH)
    for j in range(1, ngy):
        pl.semaphore_signal(barrier, inc=1, device_id=(mem, gx, lax.rem(gy + j, ngy)), device_id_type=MESH)
    for j in range(ngy):
        pl.semaphore_signal(barrier, inc=1, device_id=(1 - mem, gx, lax.rem(gy + j, ngy)), device_id_type=MESH)
    pl.semaphore_wait(barrier, ngx + 2 * ngy - 2)

    def remote(src, dst, s, r, device):
        return pltpu.make_async_remote_copy(
            src_ref=src, dst_ref=dst, send_sem=s, recv_sem=r, device_id=device, device_id_type=MESH
        )

    def rows_of(i):
        return pl.ds(pl.multiple_of(i * CHUNK, CHUNK), CHUNK)

    def direct(i):
        return remote(own.at[rows_of(i)], buf.at[par, rows_of(i)], ps.at[i], pr.at[i], (mem, gx, partner))

    def arrival(i):
        return remote(own.at[rows_of(i)], buf.at[1 - par, rows_of(i)], ps.at[i], pr.at[i], (mem, gx, partner))

    def forward(i):
        return remote(
            buf.at[1 - par, rows_of(i)], buf.at[par, rows_of(i)], fs.at[i], fr.at[i],
            (mem, gx, lax.rem(gy_f + ngy, ngy)),
        )

    def direct_x():
        return remote(xb.at[OWN], xb.at[par], ps.at[CHUNKS], pr.at[CHUNKS], (mem, gx, partner))

    def arrival_x():
        return remote(xb.at[OWN], xb.at[1 - par], ps.at[CHUNKS], pr.at[CHUNKS], (mem, gx, partner))

    def forward_x():
        return remote(
            xb.at[1 - par], xb.at[par], fs.at[CHUNKS], fr.at[CHUNKS], (mem, gx, lax.rem(gy_f + ngy, ngy))
        )

    def issue(i):
        own[rows_of(i), :] = pert[rows_of(i), :].astype(f32)
        direct(i).start()

    def pump(i):
        arrival(i).wait_recv()

        @pl.when(has_f)
        def _():
            forward(i).start()

        if isinstance(i, int) and i + AHEAD < CHUNKS:
            issue(i + AHEAD)

    def landed(i):
        @pl.when(has_b)
        def _():
            forward(i).wait_recv()

    for i in range(AHEAD):
        issue(i)
    fetch = pltpu.make_async_copy(alpha, work, al.at[0])
    fetch.start()

    @pl.when(jnp.logical_not(has_b))
    def _():
        @pl.loop(0, CHUNKS)
        def _(i):
            buf[par, rows_of(i), :] = jnp.zeros((CHUNK, 128), f32)

        xb[par] = jnp.zeros(xb.shape[1:], f32)

    @pl.when(gx == 0)
    def _():
        side[0] = jnp.zeros(side.shape[1:], f32)
        for it in range(ITERS):
            mrecv[it, 0] = jnp.zeros(mrecv.shape[2:], f32)
            nrecv[it, 0] = jnp.zeros(nrecv.shape[2:], f32)

    @pl.when(gx == ngx - 1)
    def _():
        side[1] = jnp.zeros(side.shape[1:], f32)
        for it in range(ITERS):
            mrecv[it, 1] = jnp.zeros(mrecv.shape[2:], f32)
            nrecv[it, 1] = jnp.zeros(nrecv.shape[2:], f32)

    @pl.when(gy == 0)
    def _():
        f_dn[...] = jnp.zeros(f_dn.shape, f32)
        g_dn[...] = jnp.zeros(g_dn.shape, f32)

    @pl.when(gy < 2)
    def _():
        g_dn2[...] = jnp.zeros(g_dn2.shape, f32)

    @pl.when(gy == ngy - 1)
    def _():
        f_up[...] = jnp.zeros(f_up.shape, f32)
        g_up[...] = jnp.zeros(g_up.shape, f32)

    @pl.when(gy >= ngy - 2)
    def _():
        f_up2[...] = jnp.zeros(f_up2.shape, f32)

    pack[...] = jnp.zeros(pack.shape, f32)
    px, pa = iota((128, 128), 0), iota((128, 128), 1)

    def selection(i):
        j = pa - 8 * i
        last = jnp.where((j >= 0) & (j < 4) & (px == 124 + j), 1.0, 0.0)
        first = jnp.where((j >= 4) & (j < 8) & (px == j - 4), 1.0, 0.0)
        return jnp.concatenate([last, first], axis=1).astype(bf16)

    @pl.loop(0, CHUNKS)
    def _(i):
        picked = dot(pert[rows_of(i), :], selection(i))
        pack[0, :CHUNK] += picked[:, :128]
        pack[1, :CHUNK] += picked[:, 128:]

    scaled = sig[...] * (STATIC / ENS)
    xb[OWN, 320:384] = scaled
    hi, mid, lo = split3(scaled)
    sel = selection(0)
    picked = dot(hi, sel) + dot(mid, sel) + dot(lo, sel)
    pack[0, CHUNK:] = picked[:, :128]
    pack[1, CHUNK:] = picked[:, 128:]

    right, left = lax.rem(gx + 1, ngx), lax.rem(gx + ngx - 1, ngx)

    def to_right(src, dst, sems, recvs):
        return remote(src, dst, sems.at[0], recvs.at[0], (mem, right, gy))

    def to_left(src, dst, sems, recvs):
        return remote(src, dst, sems.at[1], recvs.at[1], (mem, left, gy))

    def exchange_lon(a_src, b_src, dst, sems, recvs, wait=True):
        a, b = to_right(a_src, dst.at[0], sems, recvs), to_left(b_src, dst.at[1], sems, recvs)

        @pl.when(has_r)
        def _():
            a.start()

        @pl.when(has_l)
        def _():
            b.start()

        if wait:
            finish_lon(a, b)

    def finish_lon(a, b):
        @pl.when(has_l)
        def _():
            a.wait_recv()

        @pl.when(has_r)
        def _():
            b.wait_recv()

        @pl.when(has_r)
        def _():
            a.wait_send()

        @pl.when(has_l)
        def _():
            b.wait_send()

    exchange_lon(pack.at[0], pack.at[1], side, as_, ar, False)
    pump(0)

    tri = jnp.where(px < pa, 1.0, 0.0).astype(bf16)
    totals = jnp.zeros((64, 1), f32)
    for b in range(8):
        t = tile[:, b * 128 : (b + 1) * 128]
        one = jnp.where(iota((64, 128), 0) == t, 1.0, 0.0)
        before = dot(one.astype(bf16), tri) + totals
        rank = jnp.sum(before * one, axis=0, keepdims=True).astype(i32)
        totals = totals + jnp.sum(one, axis=1, keepdims=True)
        key_s[0:1, b * 128 : (b + 1) * 128] = (rank >> 3) * 512 + t * 8 + (rank & 7)
    feat[...] = jnp.zeros(feat.shape, f32)
    feat[0:16] = coef[...]
    feat[16:20] = interp[...]
    feat[20:21] = (cell[...] >> 9).astype(f32)
    feat[21:22] = ((cell[...] & 255) >> 1).astype(f32)
    feat[22:23] = oval[...]
    feat[23:24] = owgt[...]
    for n, part in enumerate(split3(feat[...])):
        ft[n * 32 : (n + 1) * 32] = part
    ft[96:128] = jnp.zeros((32, 1024), bf16)
    pump(1)

    def sort_records(q):
        total = jnp.zeros((128, 128), f32)
        key = key_s[0:1, :]
        lane = iota((128, 128), 1)
        for g in range(4):
            pick = jnp.where(iota((128, 1024), 0) + (g * 512 + q * 128) == key, 1.0, 0.0).astype(bf16)
            x = dot_nt(pick, ft[...])
            x = x + pltpu.roll(x, 96, 1) + pltpu.roll(x, 64, 1)
            x = pltpu.roll(x, 32 * g, 1) if g else x
            total = total + jnp.where((lane >= 32 * g) & (lane < 32 * g + 32), x, 0.0)
        sb[q * 128 : (q + 1) * 128] = total

    sort_records(0)
    pump(2)
    sort_records(1)
    sort_records(2)
    pump(3)
    sort_records(3)

    def o1(j):
        to = lax.rem(gx + j, ngx)
        return remote(
            sb.at[pl.ds(pl.multiple_of(to * 64, 64), 64)], tb.at[gx], o1s.at[j], o1r.at[gx], (mem, to, gy)
        )

    def o1_in(j):
        of = lax.rem(gx - j + ngx, ngx)
        return remote(sb.at[pl.ds(0, 64)], tb.at[of], o1s.at[j], o1r.at[of], (mem, of, gy))

    for j in range(1, ngx):
        o1(j).start()
    tb[gx] = sb[pl.ds(pl.multiple_of(gx * 64, 64), 64), :]
    finish_lon(to_right(pack.at[0], side.at[0], as_, ar), to_left(pack.at[1], side.at[1], as_, ar))
    xb[OWN, :320] = side[0] + side[1]
    direct_x().start()
    pump(4)

    main = tap_of(jnp.abs(px - pa)) - west * tap_of(px + pa + 2) - east * tap_of(256 - px - pa)
    main_hi, main_lo = split2(main)

    def matrices(first, last):
        @pl.loop(first, last)
        def _(i):
            j = pa - 8 * i
            d = jnp.where(j < 4, px + 4 - j, 124 + j - px)
            h_hi, h_lo = split2(jnp.where((j >= 0) & (j < 8), tap_of(d), 0.0))
            wf[i, 0] = jnp.concatenate([main_hi, h_hi], axis=1)
            wf[i, 1] = jnp.concatenate([main_lo, h_lo], axis=1)
            j = px - 8 * i
            d = jnp.where(j < 4, pa + 4 - j, 124 + j - pa)
            h_hi, h_lo = split2(jnp.where((j >= 0) & (j < 8), tap_of(d), 0.0))
            wa[i, 0] = jnp.concatenate([main_hi, h_hi], axis=0)
            wa[i, 1] = jnp.concatenate([main_lo, h_lo], axis=0)

    matrices(0, 8)
    pump(5)
    for j in range(1, ngx):
        o1_in(j).wait_recv()

    def near(j):
        return mem if j % 2 == 0 else 1 - mem

    def o2(j):
        to = lax.rem(gy + j, ngy)
        return remote(
            tb.at[:, pl.ds(pl.multiple_of(to * 8, 8), 8)], rb.at[gy], o2s.at[j], o2r.at[gy], (near(j), gx, to)
        )

    def o2_in(j):
        of = lax.rem(gy - j + ngy, ngy)
        return remote(tb.at[:, pl.ds(0, 8)], rb.at[of], o2s.at[j], o2r.at[of], (near(j), gx, of))

    for j in range(1, ngy):
        o2(j).start()
    rb[gy] = tb[:, pl.ds(pl.multiple_of(gy * 8, 8), 8), :]
    pump(6)
    matrices(8, CHUNKS)
    pump(7)

    def operator(q):
        turned = rb[q * 2 : q * 2 + 2].reshape(128, 128).T
        for g in range(4):
            at = pl.ds((g * 4 + q) * 128, 128)
            f = turned[g * 32 : (g + 1) * 32]
            rr, xx = f[20:21], f[21:22]
            for dc in range(2):
                upper, lower = f[16 + dc : 17 + dc], f[18 + dc : 19 + dc]
                for row in range(5):
                    w = jnp.where(rr == float(row), upper, 0.0) + jnp.where(rr == float(row - 1), lower, 0.0)
                    qt[dc * 80 + row * 16 : dc * 80 + row * 16 + 16, at] = f[0:16] * w
            cm[:, at] = jnp.where(px.astype(f32) == xx, 1.0, 0.0).astype(bf16)
            ov[0:1, at] = f[22:23]
            ov[1:2, at] = f[23:24]

    def lat(row, i):
        d = abs(row - i)
        if d > 4:
            return None
        c = GAIN * TAP[d]
        if 0 <= row < 4:
            if row + i + 2 <= 4:
                c = c - top * (GAIN * TAP[row + i + 2])
            if 8 - row - i <= 4:
                c = c - bottom * (GAIN * TAP[8 - row - i])
        return c

    COEF = [[lat(row - 4, i) for i in range(4)] for row in range(12)]

    def lat_out(y):
        z = []
        for row in range(12):
            acc = None
            for i in range(4):
                if COEF[row][i] is not None:
                    term = COEF[row][i] * y[i]
                    acc = term if acc is None else acc + term
            z.append(acc)
        return z

    def lat_in(q):
        v = []
        for i in range(4):
            acc = None
            for row in range(12):
                if COEF[row][i] is not None:
                    term = COEF[row][i] * q[row]
                    acc = term if acc is None else acc + term
            v.append(acc)
        return v

    def every4(start):
        return pl.ds(start, 8, stride=4)

    def pert_rows(start):
        at = [every4(start + r) for r in range(4)]
        return (
            [buf[BELOW, a, :] for a in at] + [own[a, :] for a in at] + [buf[ABOVE, a, :] for a in at]
        )

    def xb_rows(start):
        return [xb[b, every4(start + r), :] for b in (BELOW, OWN, ABOVE) for r in range(4)]

    def lon(x, w, i):
        hi, lo = split2(x)
        return dot(hi, w[i, 0]) + dot(lo, w[i, 0]) + dot(hi, w[i, 1])

    def eb_at(row, c8):
        return pl.ds((row + 1) * 16 + c8 * 8, 8)

    def accumulate(y, first, count, rows):
        for c8 in range(2):
            acc = [eb[eb_at(row, c8), :] for row in range(12)]
            for k in range(count):
                start = k * 64 + c8 * 32
                z = lat_out([y[every4(first + start + r), :] for r in range(4)])
                p = rows(start)
                acc = [acc[row] + z[row] * p[row] for row in range(12)]
            for row in range(12):
                eb[eb_at(row, c8), :] = acc[row]

    def clear():
        eb[...] = jnp.zeros(eb.shape, f32)
        yh_s[...] = jnp.zeros(yh_s.shape, f32)

    def member_chunk(src, i):
        wide = lon(src[rows_of(i), :], wf, i)
        y_s[:CHUNK] = wide[:, :128]
        yh_s[:CHUNK] += wide[:, 128:]
        accumulate(y_s, 0, 4, lambda start: pert_rows(pl.multiple_of(i * CHUNK, CHUNK) + start))

    def static_chunk(src):
        wide = lon(src[...] * jnp.where(mem == 0, 1.0, 0.0), wf, 0)
        y_s[CHUNK:] = wide[:, :128]
        yh_s[CHUNK:] = wide[:, 128:]
        accumulate(y_s, CHUNK, 1, lambda start: xb_rows(320 + start))

    lane192 = iota((192, 128), 1)
    lane16 = iota((16, 128), 1)

    def around(x):
        for s in (8, 16, 32, 64):
            x = x + pltpu.roll(x, s, 1)
        return x

    def reduce_and_observe(it):
        for c8 in range(2):
            acc = [jnp.zeros((8, 128), f32) for _ in range(12)]
            for k in range(5):
                start = k * 64 + c8 * 32
                z = lat_out([yh_s[every4(start + r), :] for r in range(4)])
                p = xb_rows(start)
                acc = [acc[row] + z[row] * p[row] for row in range(12)]
            for row in range(12):
                eh_s[row * 16 + c8 * 8 : row * 16 + c8 * 8 + 8] = acc[row]
        eh = around(eh_s[...])
        e = eb[16:208]
        msend[...] = jnp.where(
            lane192 < 8,
            pltpu.roll(eh, 124, 1),
            jnp.where(lane192 >= 120, pltpu.roll(eh, 4, 1), jnp.where(lane192 == 16, pltpu.roll(e, 16, 1), 0.0)),
        )
        exchange_lon(msend, msend, mrecv.at[it], ms.at[it], mr.at[it])
        m_l, m_r = mrecv[it, 0], mrecv[it, 1]
        eb[16:208] = e + jnp.where(lane192 < 4, m_l, 0.0) + jnp.where(lane192 >= 124, m_r, 0.0)
        beyond = pltpu.roll(m_r, 112, 1) + msend[...]
        xv = jnp.zeros((16, 128), f32)
        for row in range(12):
            b = beyond[row * 16 : row * 16 + 16]
            xv = xv + jnp.where(lane16 == row, pltpu.roll(b, row, 1) if row else b, 0.0)
        eb[0:16] = xv
        eb[208:224] = xv

        def sends():
            out = []
            n = 0
            for flip in range(2):
                m = mem if flip == 0 else 1 - mem
                out.append((gy < ngy - 1, remote(eb.at[pl.ds(144, 80)], f_dn.at[it, mem], bs.at[it, n], br.at[it, n], (m, gx, lax.rem(gy + 1, ngy)))))
                out.append((gy > 0, remote(eb.at[pl.ds(0, 96)], f_up.at[it, mem], bs.at[it, n + 1], br.at[it, n + 1], (m, gx, lax.rem(gy + ngy - 1, ngy)))))
                out.append((gy > 1, remote(eb.at[pl.ds(0, 32)], f_up2.at[it, mem], bs.at[it, n + 2], br.at[it, n + 2], (m, gx, lax.rem(gy + ngy - 2, ngy)))))
                n += 3
            out.append((None, remote(eb.at[pl.ds(80, 80)], f_mem.at[it, pl.ds(0, 80)], bs.at[it, 6], br.at[it, 6], (1 - mem, gx, gy))))
            out.append((None, remote(eb.at[pl.ds(208, 16)], f_mem.at[it, pl.ds(80, 16)], bs.at[it, 7], br.at[it, 7], (1 - mem, gx, gy))))
            return out

        def receives():
            out = []
            n = 0
            for flip in range(2):
                m = mem if flip == 0 else 1 - mem
                out.append((gy > 0, remote(eb.at[pl.ds(144, 80)], f_dn.at[it, m], bs.at[it, n], br.at[it, n], (mem, gx, gy))))
                out.append((gy < ngy - 1, remote(eb.at[pl.ds(0, 96)], f_up.at[it, m], bs.at[it, n + 1], br.at[it, n + 1], (mem, gx, gy))))
                out.append((gy < ngy - 2, remote(eb.at[pl.ds(0, 32)], f_up2.at[it, m], bs.at[it, n + 2], br.at[it, n + 2], (mem, gx, gy))))
                n += 3
            out.append((None, remote(eb.at[pl.ds(80, 80)], f_mem.at[it, pl.ds(0, 80)], bs.at[it, 6], br.at[it, 6], (mem, gx, gy))))
            out.append((None, remote(eb.at[pl.ds(208, 16)], f_mem.at[it, pl.ds(80, 16)], bs.at[it, 7], br.at[it, 7], (mem, gx, gy))))
            return out

        run(sends(), "start")
        run(receives(), "wait_recv")
        run(sends(), "wait_send")

        def block_sum(own, own_xv, m):
            rows = []
            for r in range(5):
                t = own(r) + f_up[it, m, (r + 1) * 16 : (r + 2) * 16]
                if r < 4:
                    t = t + f_dn[it, m, r * 16 : r * 16 + 16]
                else:
                    t = t + f_up2[it, m, 16:32]
                rows.append(t)
            x = own_xv + pltpu.roll(f_dn[it, m, 64:80], 124, 1) + pltpu.roll(f_up[it, m, 0:16], 4, 1)
            x = x + pltpu.roll(jnp.where(lane16 == 0, f_up2[it, m, 0:16], 0.0), 8, 1)
            return rows, x

        mine, x_mine = block_sum(lambda r: eb[80 + r * 16 : 96 + r * 16], eb[208:224], mem)
        theirs, x_theirs = block_sum(lambda r: f_mem[it, r * 16 : r * 16 + 16], f_mem[it, 80:96], 1 - mem)
        x = (x_mine + x_theirs) * ENS
        for r in range(5):
            dx = (mine[r] + theirs[r]) * ENS
            moved = jnp.where(lane16 == 127, pltpu.roll(x, 127 - (r + 4), 1), pltpu.roll(dx, 127, 1))
            if it == ITERS - 1 and r < 4:
                inc_out[every4(r), :] = dx[:8]
                inc_out[every4(32 + r), :] = dx[8:]
            for n, v in ((0, dx), (1, moved)):
                hi, lo = split2(v)
                lh[0, n * 80 + r * 16 : n * 80 + r * 16 + 16] = hi
                lh[1, n * 80 + r * 16 : n * 80 + r * 16 + 16] = lo

        gacc[...] = jnp.zeros(gacc.shape, f32)

        @pl.loop(0, 8)
        def _(n):
            at = pl.ds(pl.multiple_of(n * 256, 256), 256)
            c = cm[:, at]
            u = dot(lh[0], c) + dot(lh[1], c)
            q = qt[:, at]
            hx = jnp.sum(q * u, axis=0, keepdims=True)
            misfit = ov[1:2, at] * (hx - ov[0:1, at])
            hi, lo = split2(q * misfit)
            gacc[...] += dot_nt(hi, c) + dot_nt(lo, c)

        lane80 = iota((80, 128), 1)
        g0, g1 = gacc[0:80], gacc[80:160]
        g5 = g0 + jnp.where(lane80 == 0, 0.0, pltpu.roll(g1, 1, 1))
        nsend[...] = jnp.where(lane80 == 64, pltpu.roll(g1, 65, 1), g5)
        exchange_lon(nsend, nsend, nrecv.at[it], ns.at[it], nr.at[it])
        n_l, n_r = nrecv[it, 0], nrecv[it, 1]
        gb[16:96] = g5 + jnp.where(lane80 == 0, pltpu.roll(n_l, 64, 1), 0.0)
        halo = jnp.where(
            lane80 < 4,
            pltpu.roll(n_l, 4, 1),
            jnp.where(lane80 < 8, pltpu.roll(n_r, 4, 1) + jnp.where(lane80 == 4, pltpu.roll(g1, 5, 1), 0.0), 0.0),
        )
        ghv = halo[0:16]
        for r in range(1, 5):
            ghv = ghv + pltpu.roll(halo[r * 16 : r * 16 + 16], 8 * r, 1)
        gb[0:16] = ghv
        gb[96:112] = ghv

        def sends_g():
            return [
                (gy < ngy - 1, remote(gb.at[pl.ds(16, 96)], g_dn.at[it], ds_.at[it, 0], dr.at[it, 0], (1 - mem, gx, lax.rem(gy + 1, ngy)))),
                (gy > 0, remote(gb.at[pl.ds(0, 80)], g_up.at[it], ds_.at[it, 1], dr.at[it, 1], (1 - mem, gx, lax.rem(gy + ngy - 1, ngy)))),
                (gy < ngy - 2, remote(gb.at[pl.ds(80, 32)], g_dn2.at[it], ds_.at[it, 2], dr.at[it, 2], (mem, gx, lax.rem(gy + 2, ngy)))),
            ]

        def receives_g():
            both = sends_g()
            return [(gy > 0, both[0][1]), (gy < ngy - 1, both[1][1]), (gy > 1, both[2][1])]

        run(sends_g(), "start")
        run(receives_g(), "wait_recv")
        run(sends_g(), "wait_send")

        def ext(v, r):
            return jnp.where(lane16 < 8, pltpu.roll(v, 128 - 8 * r, 1) if r else v, 0.0)

        for r in range(4):
            below, own, above = g_dn[it, r * 16 : r * 16 + 16], gb[16 + r * 16 : 32 + r * 16], g_up[it, 16 + r * 16 : 32 + r * 16]
            hb, ho, ha = ext(g_dn[it, 80:96], r), ext(ghv, r), ext(g_up[it, 0:16], r)
            if r == 0:
                below, hb = below + g_dn2[it, 0:16], hb + ext(g_dn2[it, 16:32], 4)
                own, ho = own + g_dn[it, 64:80], ho + ext(g_dn[it, 80:96], 4)
                above, ha = above + gb[80:96], ha + ext(ghv, 4)
            for n, (v, h) in enumerate(((below, hb), (own, ho), (above, ha))):
                at = n * 64 + r * 16
                gx_s[at : at + 16] = v
                gh_s[at : at + 16] = h
        gh_s[...] = around(gh_s[...])

        for c8 in range(2):
            g = [gh_s[row * 16 + c8 * 8 : row * 16 + c8 * 8 + 8] for row in range(12)]
            for k in range(5):
                start = k * 64 + c8 * 32
                p = xb_rows(start)
                v = lat_in([p[row] * g[row] for row in range(12)])
                for r in range(4):
                    yh_s[every4(start + r), :] = v[r]
        hi, lo = split2(yh_s[...])
        vh_s[0] = hi
        vh_s[1] = lo

    def run(copies, what):
        for condition, copy in copies:
            if condition is None:
                getattr(copy, what)()
            else:
                pl.when(condition)(lambda copy=copy: getattr(copy, what)())

    def gradient(first, count, halo, rows, i):
        for c8 in range(2):
            g = [gx_s[row * 16 + c8 * 8 : row * 16 + c8 * 8 + 8] for row in range(12)]
            for k in range(count):
                start = k * 64 + c8 * 32
                p = rows(start)
                v = lat_in([p[row] * g[row] for row in range(12)])
                for r in range(4):
                    y_s[every4(first + start + r), :] = v[r]
        n = count * 64
        hi, lo = split2(y_s[first : first + n])
        hi = jnp.concatenate([hi, vh_s[0, halo : halo + n]], axis=1)
        lo = jnp.concatenate([lo, vh_s[1, halo : halo + n]], axis=1)
        return dot(hi, wa[i, 0]) + dot(lo, wa[i, 0]) + dot(hi, wa[i, 1])

    def member_step(i):
        u = gradient(0, 4, 0, lambda start: pert_rows(pl.multiple_of(i * CHUNK, CHUNK) + start), i)
        work[rows_of(i), :] = (1.0 - DESCENT) * work[rows_of(i), :] - (DESCENT * ENS) * u

    def done(i):
        return pltpu.make_async_copy(work.at[rows_of(i)], alpha_out.at[rows_of(i)], ao.at[i])

    def static_step(src):
        u = gradient(CHUNK, 1, CHUNK, lambda start: xb_rows(320 + start), 0)
        stat_out[...] = (1.0 - DESCENT) * src[...] - (DESCENT * ENS) * u

    clear()

    fetch.wait()
    for i in range(8, CHUNKS):
        pump(i)
        if i == 10:
            for j in range(1, ngy):
                o2_in(j).wait_recv()
        if i >= 11 and i < 15:
            operator(i - 11)
        if i < 15:

            @pl.loop(2 * (i - 8), 2 * (i - 8) + 2)
            def _(n):
                landed(n)
                member_chunk(work, n)

    arrival_x().wait_recv()

    @pl.when(has_f)
    def _():
        forward_x().start()

    @pl.loop(CHUNKS - 2, CHUNKS)
    def _(i):
        landed(i)
        member_chunk(work, i)

    @pl.when(has_b)
    def _():
        forward_x().wait_recv()

    static_chunk(stat)
    reduce_and_observe(0)
    clear()

    @pl.loop(0, CHUNKS)
    def _(i):
        member_step(i)
        member_chunk(work, i)

    static_step(stat)
    static_chunk(stat_out)
    reduce_and_observe(1)

    @pl.loop(0, CHUNKS)
    def _(i):
        member_step(i)
        done(i).start()

    static_step(stat_out)
    for i in range(CHUNKS):
        done(i).wait()

    for i in range(CHUNKS):
        direct(i).wait_send()
    direct_x().wait_send()

    @pl.when(has_f)
    def _():
        for i in range(CHUNKS):
            forward(i).wait_send()
        forward_x().wait_send()

    for j in range(1, ngx):
        o1(j).wait_send()
    for j in range(1, ngy):
        o2(j).wait_send()


def per_device(
    alpha, static_control, perturbations, sigma, obs_coef, interp_weights, obs_values, obs_weights, obs_tile, obs_cell
):
    rows = alpha.size // 128
    vmem = pl.BlockSpec(memory_space=pltpu.VMEM)
    args = (
        alpha.reshape(rows, 128),
        perturbations.reshape(rows, 128),
        static_control.reshape(64, 128),
        sigma.reshape(64, 128),
        obs_coef.reshape(16, 1024),
        interp_weights,
        obs_values.reshape(1, 1024),
        obs_weights.reshape(1, 1024),
        obs_tile.reshape(1, 1024),
        obs_cell.reshape(1, 1024),
    )
    dma = pltpu.SemaphoreType.DMA
    V = pltpu.VMEM
    scratch = [
        V((rows, 128), f32),
        V((rows, 128), f32),
        V((2, rows, 128), f32),
        V((3, 384, 128), f32),
        V((2, 320, 128), f32),
        V((2, 320, 128), f32),
        V((CHUNKS, 2, 128, 256), bf16),
        V((CHUNKS, 2, 256, 128), bf16),
        V((320, 128), f32),
        V((320, 128), f32),
        V((2, 320, 128), bf16),
        V((224, 128), f32),
        V((192, 128), f32),
        V((192, 128), f32),
        V((ITERS, 2, 192, 128), f32),
        V((ITERS, 2, 80, 128), f32),
        V((ITERS, 2, 96, 128), f32),
        V((ITERS, 2, 32, 128), f32),
        V((ITERS, 96, 128), f32),
        V((80, 128), f32),
        V((ITERS, 2, 80, 128), f32),
        V((112, 128), f32),
        V((ITERS, 96, 128), f32),
        V((ITERS, 80, 128), f32),
        V((ITERS, 32, 128), f32),
        V((192, 128), f32),
        V((192, 128), f32),
        V((32, 1024), f32),
        V((128, 1024), bf16),
        V((8, 1024), i32),
        V((512, 128), f32),
        V((8, 64, 128), f32),
        V((8, 8, 8, 128), f32),
        V((160, 2048), f32),
        V((128, 2048), bf16),
        V((8, 2048), f32),
        V((2, 160, 128), bf16),
        V((160, 128), f32),
        dma((CHUNKS + 1,)), dma((CHUNKS + 1,)), dma((CHUNKS + 1,)), dma((CHUNKS + 1,)),
        dma((2,)), dma((2,)),
        dma((8,)), dma((8,)), dma((8,)), dma((8,)),
        dma((ITERS, 2)), dma((ITERS, 2)),
        dma((ITERS, 8)), dma((ITERS, 8)),
        dma((ITERS, 2)), dma((ITERS, 2)),
        dma((ITERS, 3)), dma((ITERS, 3)),
        dma((1,)), dma((CHUNKS,)),
    ]
    outs = pl.pallas_call(
        body,
        out_shape=(
            jax.ShapeDtypeStruct((rows, 128), f32),
            jax.ShapeDtypeStruct((64, 128), f32),
            jax.ShapeDtypeStruct((64, 128), f32),
        ),
        in_specs=[pl.BlockSpec(memory_space=pl.ANY)] + [vmem] * (len(args) - 1),
        out_specs=(pl.BlockSpec(memory_space=pl.ANY), vmem, vmem),
        scratch_shapes=scratch,
        name="assimilate",
        compiler_params=pltpu.CompilerParams(
            collective_id=0, has_side_effects=True, vmem_limit_bytes=56 << 20
        ),
    )(*args)
    return (
        outs[0].reshape(alpha.shape),
        outs[1].reshape(static_control.shape),
        outs[2].reshape(static_control.shape),
    )


def solution(mesh):
    placed = (
        P("mem", None, None, "gy", "gx"),
        P(None, None, "gy", "gx"),
        P("mem", None, None, "gy", "gx"),
        P(None, None, "gy", "gx"),
        P(None, None, ("gx", "gy")),
        P(None, ("gx", "gy")),
        P(("gx", "gy")),
        P(("gx", "gy")),
        P(("gx", "gy"), None),
        P(("gx", "gy")),
    )
    return jax.shard_map(
        per_device,
        mesh=mesh,
        in_specs=placed,
        out_specs=(
            P("mem", None, None, "gy", "gx"),
            P(None, None, "gy", "gx"),
            P(None, None, "gy", "gx"),
        ),
        check_vma=False,
    )
```

```python
import math

import jax
import jax.numpy as jnp
from jax import lax
from jax.experimental import pallas as pl
from jax.experimental.pallas import tpu as pltpu
from jax.sharding import PartitionSpec as P

f32, bf16, i32 = jnp.float32, jnp.bfloat16, jnp.int32
MESH = pl.DeviceIdType.MESH

MEMBERS = 128
ITERS = 2
ENS = 0.8660254037844386 / math.sqrt(MEMBERS - 1)
STATIC = 0.5
DESCENT = 0.2
GAIN = 4.0


def four_passes():
    taps = [1.0]
    for _ in range(4):
        wide = [0.0] * (len(taps) + 2)
        for i, t in enumerate(taps):
            wide[i] += 0.45 * t
            wide[i + 1] += 0.1 * t
            wide[i + 2] += 0.45 * t
        taps = wide
    return taps[4:]


TAP = four_passes()

CHUNK = 256
CHUNKS = 16
AHEAD = 3
BELOW, ABOVE, OWN = 0, 1, 2


def split2(x):
    hi = x.astype(bf16)
    return hi, (x - hi.astype(f32)).astype(bf16)


def split3(x):
    hi = x.astype(bf16)
    rest = x - hi.astype(f32)
    mid = rest.astype(bf16)
    return hi, mid, (rest - mid.astype(f32)).astype(bf16)


def dot(a, b):
    return jnp.dot(a, b, preferred_element_type=f32)


def dot_nt(a, b):
    return lax.dot_general(a, b, (((1,), (1,)), ((), ())), preferred_element_type=f32)


def iota(shape, dim):
    return lax.broadcasted_iota(i32, shape, dim)


def tap_of(distance):
    out = jnp.zeros(distance.shape, f32)
    for d in range(5):
        out = jnp.where(distance == d, TAP[d], out)
    return out


def body(
    alpha, pert, stat, sig, coef, interp, oval, owgt, tile, cell,
    alpha_out, stat_out, inc_out,
    own, work, buf, xb, pack, side, wf, wa, y_s, yh_s, vh_s, eb, eh_s, msend, mrecv,
    f_dn, f_up, f_up2, f_mem, nrecv, gb, g_dn, g_up, g_dn2, gx_s, gh_s,
    feat, ft, key_s, sb, tb, rb, qt, cm, ov, lh, gacc,
    ps, pr, fs, fr, as_, ar, o1s, o1r, o2s, o2r, ms, mr, bs, br, ns, nr, ds_, dr, al, ao,
):
    mem, gx, gy = lax.axis_index("mem"), lax.axis_index("gx"), lax.axis_index("gy")
    ngx, ngy = lax.axis_size("gx"), lax.axis_size("gy")
    par = lax.rem(gy, 2)
    partner = gy + 1 - 2 * par
    gy_f = gy + 2 - 4 * par
    has_f = (gy_f >= 0) & (gy_f < ngy)
    gy_b = gy - 2 + 4 * par
    has_b = (gy_b >= 0) & (gy_b < ngy)
    top = jnp.where(gy == 0, 1.0, 0.0)
    bottom = jnp.where(gy == ngy - 1, 1.0, 0.0)
    west = jnp.where(gx == 0, 1.0, 0.0)
    east = jnp.where(gx == ngx - 1, 1.0, 0.0)
    has_l, has_r = gx > 0, gx < ngx - 1
    lane8 = iota((8, 128), 1)

    barrier = pltpu.get_barrier_semaphore()

    def greet(m, x, y):
        pl.semaphore_signal(barrier, inc=1, device_id=(m, lax.rem(x + ngx, ngx), lax.rem(y + ngy, ngy)), device_id_type=MESH)

    for j in range(1, ngx):
        greet(mem, gx + j, gy)
    for j in range(1, ngy):
        greet(mem, gx, gy + j)
    for j in range(ngy):
        greet(1 - mem, gx, gy + j)
    for dx in (-1, 1):
        greet(1 - mem, gx + dx, gy)
        for dy in (-1, 1):
            greet(1 - mem, gx + dx, gy + dy)
        for dy in (-2, 2):
            greet(mem, gx + dx, gy + dy)
    pl.semaphore_wait(barrier, ngx + 2 * ngy - 2 + 10)

    def remote(src, dst, s, r, device):
        return pltpu.make_async_remote_copy(
            src_ref=src, dst_ref=dst, send_sem=s, recv_sem=r, device_id=device, device_id_type=MESH
        )

    def rows_of(i):
        return pl.ds(pl.multiple_of(i * CHUNK, CHUNK), CHUNK)

    def direct(i):
        return remote(own.at[rows_of(i)], buf.at[par, rows_of(i)], ps.at[i], pr.at[i], (mem, gx, partner))

    def arrival(i):
        return remote(own.at[rows_of(i)], buf.at[1 - par, rows_of(i)], ps.at[i], pr.at[i], (mem, gx, partner))

    def forward(i):
        return remote(
            buf.at[1 - par, rows_of(i)], buf.at[par, rows_of(i)], fs.at[i], fr.at[i],
            (mem, gx, lax.rem(gy_f + ngy, ngy)),
        )

    def direct_x():
        return remote(xb.at[OWN], xb.at[par], ps.at[CHUNKS], pr.at[CHUNKS], (mem, gx, partner))

    def arrival_x():
        return remote(xb.at[OWN], xb.at[1 - par], ps.at[CHUNKS], pr.at[CHUNKS], (mem, gx, partner))

    def forward_x():
        return remote(
            xb.at[1 - par], xb.at[par], fs.at[CHUNKS], fr.at[CHUNKS], (mem, gx, lax.rem(gy_f + ngy, ngy))
        )

    def issue(i):
        own[rows_of(i), :] = pert[rows_of(i), :].astype(f32)
        direct(i).start()

    def pump(i):
        arrival(i).wait_recv()

        @pl.when(has_f)
        def _():
            forward(i).start()

        if isinstance(i, int) and i + AHEAD < CHUNKS:
            issue(i + AHEAD)

    def landed(i):
        @pl.when(has_b)
        def _():
            forward(i).wait_recv()

    for i in range(AHEAD):
        issue(i)
    fetch = pltpu.make_async_copy(alpha, work, al.at[0])
    fetch.start()

    @pl.when(jnp.logical_not(has_b))
    def _():
        @pl.loop(0, CHUNKS)
        def _(i):
            buf[par, rows_of(i), :] = jnp.zeros((CHUNK, 128), f32)

        xb[par] = jnp.zeros(xb.shape[1:], f32)

    @pl.when(gx == 0)
    def _():
        side[0] = jnp.zeros(side.shape[1:], f32)
        for it in range(ITERS):
            mrecv[it, 0] = jnp.zeros(mrecv.shape[2:], f32)
            for n in range(4):
                nrecv[it, n, 0] = jnp.zeros((16, 128), f32)

    @pl.when(gx == ngx - 1)
    def _():
        side[1] = jnp.zeros(side.shape[1:], f32)
        for it in range(ITERS):
            mrecv[it, 1] = jnp.zeros(mrecv.shape[2:], f32)
            for n in range(4):
                nrecv[it, n, 1] = jnp.zeros((16, 128), f32)

    @pl.when(gy == 0)
    def _():
        f_dn[...] = jnp.zeros(f_dn.shape, f32)
        g_dn[...] = jnp.zeros(g_dn.shape, f32)
        for it in range(ITERS):
            nrecv[it, 1] = jnp.zeros((2, 16, 128), f32)

    @pl.when(gy < 2)
    def _():
        g_dn2[...] = jnp.zeros(g_dn2.shape, f32)
        for it in range(ITERS):
            nrecv[it, 3] = jnp.zeros((2, 16, 128), f32)

    @pl.when(gy == ngy - 1)
    def _():
        f_up[...] = jnp.zeros(f_up.shape, f32)
        g_up[...] = jnp.zeros(g_up.shape, f32)
        for it in range(ITERS):
            nrecv[it, 2] = jnp.zeros((2, 16, 128), f32)

    @pl.when(gy >= ngy - 2)
    def _():
        f_up2[...] = jnp.zeros(f_up2.shape, f32)

    px, pa = iota((128, 128), 0), iota((128, 128), 1)

    tri = jnp.where(px < pa, 1.0, 0.0).astype(bf16)
    totals = jnp.zeros((64, 1), f32)
    for b in range(8):
        t = tile[:, b * 128 : (b + 1) * 128]
        one = jnp.where(iota((64, 128), 0) == t, 1.0, 0.0)
        before = dot(one.astype(bf16), tri) + totals
        rank = jnp.sum(before * one, axis=0, keepdims=True).astype(i32)
        totals = totals + jnp.sum(one, axis=1, keepdims=True)
        key_s[0:1, b * 128 : (b + 1) * 128] = (rank >> 3) * 512 + t * 8 + (rank & 7)
    feat[...] = jnp.zeros(feat.shape, f32)
    feat[0:16] = coef[...]
    feat[16:20] = interp[...]
    feat[20:21] = (cell[...] >> 9).astype(f32)
    feat[21:22] = ((cell[...] & 255) >> 1).astype(f32)
    feat[22:23] = oval[...]
    feat[23:24] = owgt[...]
    for n, part in enumerate(split3(feat[...])):
        ft[n * 32 : (n + 1) * 32] = part
    ft[96:128] = jnp.zeros((32, 1024), bf16)
    pump(0)

    def sort_records(q):
        total = jnp.zeros((128, 128), f32)
        key = key_s[0:1, :]
        lane = iota((128, 128), 1)
        for g in range(4):
            pick = jnp.where(iota((128, 1024), 0) + (g * 512 + q * 128) == key, 1.0, 0.0).astype(bf16)
            x = dot_nt(pick, ft[...])
            x = x + pltpu.roll(x, 96, 1) + pltpu.roll(x, 64, 1)
            x = pltpu.roll(x, 32 * g, 1) if g else x
            total = total + jnp.where((lane >= 32 * g) & (lane < 32 * g + 32), x, 0.0)
        sb[q * 128 : (q + 1) * 128] = total

    sort_records(0)
    sort_records(1)
    pump(1)
    sort_records(2)
    sort_records(3)
    pump(2)

    def o1(j):
        to = lax.rem(gx + j, ngx)
        return remote(
            sb.at[pl.ds(pl.multiple_of(to * 64, 64), 64)], tb.at[gx], o1s.at[j], o1r.at[gx], (mem, to, gy)
        )

    def o1_in(j):
        of = lax.rem(gx - j + ngx, ngx)
        return remote(sb.at[pl.ds(0, 64)], tb.at[of], o1s.at[j], o1r.at[of], (mem, of, gy))

    for j in range(1, ngx):
        o1(j).start()
    tb[gx] = sb[pl.ds(pl.multiple_of(gx * 64, 64), 64), :]
    pump(3)

    pack[...] = jnp.zeros(pack.shape, f32)

    def selection(i):
        j = pa - 8 * i
        last = jnp.where((j >= 0) & (j < 4) & (px == 124 + j), 1.0, 0.0)
        first = jnp.where((j >= 4) & (j < 8) & (px == j - 4), 1.0, 0.0)
        return jnp.concatenate([last, first], axis=1).astype(bf16)

    @pl.loop(0, CHUNKS)
    def _(i):
        picked = dot(pert[rows_of(i), :], selection(i))
        pack[0, :CHUNK] += picked[:, :128]
        pack[1, :CHUNK] += picked[:, 128:]

    scaled = sig[...] * (STATIC / ENS)
    xb[OWN, 320:384] = scaled
    hi, mid, lo = split3(scaled)
    sel = selection(0)
    picked = dot(hi, sel) + dot(mid, sel) + dot(lo, sel)
    pack[0, CHUNK:] = picked[:, :128]
    pack[1, CHUNK:] = picked[:, 128:]

    right, left = lax.rem(gx + 1, ngx), lax.rem(gx + ngx - 1, ngx)

    def to_right(src, dst, sems, recvs):
        return remote(src, dst, sems.at[0], recvs.at[0], (mem, right, gy))

    def to_left(src, dst, sems, recvs):
        return remote(src, dst, sems.at[1], recvs.at[1], (mem, left, gy))

    def exchange_lon(a_src, b_src, dst, sems, recvs, wait=True):
        a, b = to_right(a_src, dst.at[0], sems, recvs), to_left(b_src, dst.at[1], sems, recvs)

        @pl.when(has_r)
        def _():
            a.start()

        @pl.when(has_l)
        def _():
            b.start()

        if wait:
            finish_lon(a, b)

    def finish_lon(a, b):
        @pl.when(has_l)
        def _():
            a.wait_recv()

        @pl.when(has_r)
        def _():
            b.wait_recv()

        @pl.when(has_r)
        def _():
            a.wait_send()

        @pl.when(has_l)
        def _():
            b.wait_send()

    exchange_lon(pack.at[0], pack.at[1], side, as_, ar, False)
    pump(4)

    main = tap_of(jnp.abs(px - pa)) - west * tap_of(px + pa + 2) - east * tap_of(256 - px - pa)
    main_hi, main_lo = split2(main)

    def matrices(first, last):
        @pl.loop(first, last)
        def _(i):
            j = pa - 8 * i
            d = jnp.where(j < 4, px + 4 - j, 124 + j - px)
            h_hi, h_lo = split2(jnp.where((j >= 0) & (j < 8), tap_of(d), 0.0))
            wf[i, 0] = jnp.concatenate([main_hi, h_hi], axis=1)
            wf[i, 1] = jnp.concatenate([main_lo, h_lo], axis=1)
            j = px - 8 * i
            d = jnp.where(j < 4, pa + 4 - j, 124 + j - pa)
            h_hi, h_lo = split2(jnp.where((j >= 0) & (j < 8), tap_of(d), 0.0))
            wa[i, 0] = jnp.concatenate([main_hi, h_hi], axis=0)
            wa[i, 1] = jnp.concatenate([main_lo, h_lo], axis=0)

    matrices(0, 8)
    pump(5)
    matrices(8, CHUNKS)
    pump(6)
    pump(7)
    for j in range(1, ngx):
        o1_in(j).wait_recv()

    def near(j):
        return mem if j % 2 == 0 else 1 - mem

    def o2(j):
        to = lax.rem(gy + j, ngy)
        return remote(
            tb.at[:, pl.ds(pl.multiple_of(to * 8, 8), 8)], rb.at[gy], o2s.at[j], o2r.at[gy], (near(j), gx, to)
        )

    def o2_in(j):
        of = lax.rem(gy - j + ngy, ngy)
        return remote(tb.at[:, pl.ds(0, 8)], rb.at[of], o2s.at[j], o2r.at[of], (near(j), gx, of))

    for j in range(1, ngy):
        o2(j).start()
    rb[gy] = tb[:, pl.ds(pl.multiple_of(gy * 8, 8), 8), :]
    def operator(q):
        turned = rb[q * 2 : q * 2 + 2].reshape(128, 128).T
        for g in range(4):
            at = pl.ds((g * 4 + q) * 128, 128)
            f = turned[g * 32 : (g + 1) * 32]
            rr, xx = f[20:21], f[21:22]
            for dc in range(2):
                upper, lower = f[16 + dc : 17 + dc], f[18 + dc : 19 + dc]
                for row in range(5):
                    w = jnp.where(rr == float(row), upper, 0.0) + jnp.where(rr == float(row - 1), lower, 0.0)
                    qt[dc * 80 + row * 16 : dc * 80 + row * 16 + 16, at] = f[0:16] * w
            cm[:, at] = jnp.where(px.astype(f32) == xx, 1.0, 0.0).astype(bf16)
            ov[0:1, at] = f[22:23]
            ov[1:2, at] = f[23:24]

    def lat(row, i):
        d = abs(row - i)
        if d > 4:
            return None
        c = GAIN * TAP[d]
        if 0 <= row < 4:
            if row + i + 2 <= 4:
                c = c - top * (GAIN * TAP[row + i + 2])
            if 8 - row - i <= 4:
                c = c - bottom * (GAIN * TAP[8 - row - i])
        return c

    COEF = [[lat(row - 4, i) for i in range(4)] for row in range(12)]

    def lat_out(y):
        z = []
        for row in range(12):
            acc = None
            for i in range(4):
                if COEF[row][i] is not None:
                    term = COEF[row][i] * y[i]
                    acc = term if acc is None else acc + term
            z.append(acc)
        return z

    def lat_in(q):
        v = []
        for i in range(4):
            acc = None
            for row in range(12):
                if COEF[row][i] is not None:
                    term = COEF[row][i] * q[row]
                    acc = term if acc is None else acc + term
            v.append(acc)
        return v

    def every4(start):
        return pl.ds(start, 8, stride=4)

    def pert_rows(start):
        at = [every4(start + r) for r in range(4)]
        return (
            [buf[BELOW, a, :] for a in at] + [own[a, :] for a in at] + [buf[ABOVE, a, :] for a in at]
        )

    def xb_rows(start):
        return [xb[b, every4(start + r), :] for b in (BELOW, OWN, ABOVE) for r in range(4)]

    def lon(x, w, i):
        hi, lo = split2(x)
        return dot(hi, w[i, 0]) + dot(lo, w[i, 0]) + dot(hi, w[i, 1])

    def eb_at(row, c8):
        return pl.ds((row + 1) * 16 + c8 * 8, 8)

    def accumulate(y, first, count, rows):
        for c8 in range(2):
            acc = [eb[eb_at(row, c8), :] for row in range(12)]
            for k in range(count):
                start = k * 64 + c8 * 32
                z = lat_out([y[every4(first + start + r), :] for r in range(4)])
                p = rows(start)
                acc = [acc[row] + z[row] * p[row] for row in range(12)]
            for row in range(12):
                eb[eb_at(row, c8), :] = acc[row]

    def clear():
        eb[...] = jnp.zeros(eb.shape, f32)
        yh_s[...] = jnp.zeros(yh_s.shape, f32)

    def member_chunk(src, i):
        wide = lon(src[rows_of(i), :], wf, i)
        y_s[:CHUNK] = wide[:, :128]
        yh_s[:CHUNK] += wide[:, 128:]
        accumulate(y_s, 0, 4, lambda start: pert_rows(pl.multiple_of(i * CHUNK, CHUNK) + start))

    def static_chunk(src):
        wide = lon(src[...] * jnp.where(mem == 0, 1.0, 0.0), wf, 0)
        y_s[CHUNK:] = wide[:, :128]
        yh_s[CHUNK:] = wide[:, 128:]
        accumulate(y_s, CHUNK, 1, lambda start: xb_rows(320 + start))

    lane16 = iota((16, 128), 1)
    group16, place16 = lane16 >> 3, lane16 & 7

    def around(x):
        for s in (8, 16, 32, 64):
            x = x + pltpu.roll(x, s, 1)
        return x

    def turn(x, s):
        s = s % 128
        return pltpu.roll(x, s, 1) if s else x

    def reduce_and_observe(it):
        whole = remote(eb.at[pl.ds(16, 192)], f_mem.at[it], bs.at[it, 0], br.at[it, 0], (1 - mem, gx, gy))
        whole.start()
        for c8 in range(2):
            acc = [jnp.zeros((8, 128), f32) for _ in range(12)]
            for k in range(5):
                start = k * 64 + c8 * 32
                z = lat_out([yh_s[every4(start + r), :] for r in range(4)])
                p = xb_rows(start)
                acc = [acc[row] + z[row] * p[row] for row in range(12)]
            for row in range(12):
                eh_s[row * 16 + c8 * 8 : row * 16 + c8 * 8 + 8] = acc[row]
        eh = around(eh_s[...])
        halo, edge = jnp.zeros((16, 128), f32), jnp.zeros((16, 128), f32)
        for row in range(12):
            at = row * 16
            halo = jnp.where(group16 == row, eh[at : at + 16], halo)
            edge = jnp.where(lane16 == 8 * row + 4, turn(eb[16 + at : 32 + at], 8 * row + 4), edge)
        msend[0:16] = halo
        msend[16:32] = edge

        def columns():
            out = []
            for flip in range(2):
                m = mem if flip == 0 else 1 - mem
                out.append((has_r, has_l, remote(msend, mrecv.at[it, 0, mem], ms.at[it, flip], mr.at[it, flip], (m, right, gy))))
                out.append((has_l, has_r, remote(msend, mrecv.at[it, 1, mem], ms.at[it, 2 + flip], mr.at[it, 2 + flip], (m, left, gy))))
            out.append((None, None, remote(msend, mrecv.at[it, 2, 0], ms.at[it, 4], mr.at[it, 4], (1 - mem, gx, gy))))
            return out

        run([(c, x) for c, _, x in columns()], "start")
        run([(c, x) for _, c, x in columns()] + [(None, whole)], "wait_recv")
        run([(c, x) for c, _, x in columns()] + [(None, whole)], "wait_send")
        m_l = mrecv[it, 0, 0] + mrecv[it, 0, 1]
        m_r = mrecv[it, 1, 0] + mrecv[it, 1, 1]
        m_o = halo + mrecv[it, 2, 0, 0:16]
        for row in range(12):
            at = row * 16
            e = eb[16 + at : 32 + at] + f_mem[it, at : at + 16]
            e = e + jnp.where(lane16 < 4, turn(m_l[0:16], -8 * row - 4), 0.0)
            e = e + jnp.where(lane16 >= 124, turn(m_r[0:16], 124 - 8 * row), 0.0)
            eb[16 + at : 32 + at] = e
        xv = jnp.where((place16 == 4) & (lane16 < 96), m_r[16:32] + m_o, 0.0)
        eb[0:16] = xv
        eb[208:224] = xv

        def rows_out():
            return [
                (gy < ngy - 1, gy > 0, remote(eb.at[pl.ds(144, 80)], f_dn.at[it], bs.at[it, 1], br.at[it, 1], (1 - mem, gx, lax.rem(gy + 1, ngy)))),
                (gy > 0, gy < ngy - 1, remote(eb.at[pl.ds(0, 96)], f_up.at[it], bs.at[it, 2], br.at[it, 2], (1 - mem, gx, lax.rem(gy + ngy - 1, ngy)))),
                (gy > 1, gy < ngy - 2, remote(eb.at[pl.ds(0, 32)], f_up2.at[it], bs.at[it, 3], br.at[it, 3], (mem, gx, lax.rem(gy + ngy - 2, ngy)))),
            ]

        run([(c, x) for c, _, x in rows_out()], "start")
        run([(c, x) for _, c, x in rows_out()], "wait_recv")
        run([(c, x) for c, _, x in rows_out()], "wait_send")
        x = xv + turn(f_dn[it, 64:80], -32) + turn(f_up[it, 0:16], 32)
        x = (x + turn(jnp.where(lane16 == 4, f_up2[it, 0:16], 0.0), 64)) * ENS
        for r in range(5):
            dx = eb[80 + r * 16 : 96 + r * 16] + f_up[it, (r + 1) * 16 : (r + 2) * 16]
            dx = (dx + (f_dn[it, r * 16 : r * 16 + 16] if r < 4 else f_up2[it, 16:32])) * ENS
            moved = jnp.where(lane16 == 127, turn(x, 127 - 8 * (r + 4) - 4), turn(dx, 127))
            if it == ITERS - 1 and r < 4:
                inc_out[every4(r), :] = dx[:8]
                inc_out[every4(32 + r), :] = dx[8:]
            for n, v in ((0, dx), (1, moved)):
                hi, lo = split2(v)
                lh[0, n * 80 + r * 16 : n * 80 + r * 16 + 16] = hi
                lh[1, n * 80 + r * 16 : n * 80 + r * 16 + 16] = lo

        gacc[...] = jnp.zeros(gacc.shape, f32)

        @pl.loop(0, 8)
        def _(n):
            at = pl.ds(pl.multiple_of(n * 256, 256), 256)
            c = cm[:, at]
            u = dot(lh[0], c) + dot(lh[1], c)
            q = qt[:, at]
            hx = jnp.sum(q * u, axis=0, keepdims=True)
            misfit = ov[1:2, at] * (hx - ov[0:1, at])
            hi, lo = split2(q * misfit)
            gacc[...] += dot_nt(hi, c) + dot_nt(lo, c)

        lane80 = iota((80, 128), 1)
        g0, g1 = gacc[0:80], gacc[80:160]
        gb[16:96] = g0 + jnp.where(lane80 == 0, 0.0, turn(g1, 1))
        sides = jnp.zeros((16, 128), f32)
        for r in range(5):
            at = r * 16
            g5 = gb[16 + at : 32 + at]
            both = jnp.where(place16 < 4, turn(g5, 8 * r + 4), turn(g5, 8 * r + 4))
            sides = jnp.where(group16 == r, both, sides)
            sides = jnp.where(lane16 == 64 + 8 * r, turn(g1[at : at + 16], 64 + 8 * r - 127), sides)
        gb[0:16] = sides
        gb[96:112] = sides

        def terms():
            out = [
                (gy < ngy - 1, gy > 0, remote(gb.at[pl.ds(16, 96)], g_dn.at[it], ds_.at[it, 0], dr.at[it, 0], (1 - mem, gx, lax.rem(gy + 1, ngy)))),
                (gy > 0, gy < ngy - 1, remote(gb.at[pl.ds(0, 80)], g_up.at[it], ds_.at[it, 1], dr.at[it, 1], (1 - mem, gx, lax.rem(gy + ngy - 1, ngy)))),
                (gy < ngy - 2, gy > 1, remote(gb.at[pl.ds(80, 32)], g_dn2.at[it], ds_.at[it, 2], dr.at[it, 2], (mem, gx, lax.rem(gy + 2, ngy)))),
            ]
            for n, (m, step) in enumerate(((mem, 0), (1 - mem, 1), (1 - mem, -1), (mem, 2))):
                to, of = gy + step, gy - step
                there, here = (to >= 0) & (to < ngy), (of >= 0) & (of < ngy)
                row = lax.rem(to + ngy, ngy)
                for k, (x, c, d) in enumerate(((right, has_r, has_l), (left, has_l, has_r))):
                    copy = remote(gb.at[pl.ds(0, 16)], nrecv.at[it, n, k], ns.at[it, 2 * n + k], nr.at[it, 2 * n + k], (m, x, row))
                    out.append((c & there, d & here, copy))
            return out

        run([(c, x) for c, _, x in terms()], "start")
        run([(c, x) for _, c, x in terms()], "wait_recv")
        run([(c, x) for c, _, x in terms()], "wait_send")
        beside = [nrecv[it, n] for n in range(4)]
        centre = [sides, g_dn[it, 80:96], g_up[it, 0:16], g_dn2[it, 16:32]]

        def halos(n):
            own = jnp.where((place16 == 4) & (lane16 < 40), turn(centre[n], -60), 0.0)
            return jnp.where(place16 < 4, beside[n][0], beside[n][1] + own)

        def row_of(n, v, r):
            return v + jnp.where(lane16 == 0, turn(beside[n][0], -64 - 8 * r), 0.0)

        halo_own, halo_dn, halo_up, halo_dn2 = [halos(n) for n in range(4)]

        def ext(v, r):
            return jnp.where(lane16 < 8, turn(v, -8 * r), 0.0)

        for r in range(4):
            at = r * 16
            below, own, above = row_of(1, g_dn[it, at : at + 16], r), row_of(0, gb[16 + at : 32 + at], r), row_of(2, g_up[it, 16 + at : 32 + at], r)
            hb, ho, ha = ext(halo_dn, r), ext(halo_own, r), ext(halo_up, r)
            if r == 0:
                below, hb = below + row_of(3, g_dn2[it, 0:16], 4), hb + ext(halo_dn2, 4)
                own, ho = own + row_of(1, g_dn[it, 64:80], 4), ho + ext(halo_dn, 4)
                above, ha = above + row_of(0, gb[80:96], 4), ha + ext(halo_own, 4)
            for n, (v, h) in enumerate(((below, hb), (own, ho), (above, ha))):
                at = n * 64 + r * 16
                gx_s[at : at + 16] = v
                gh_s[at : at + 16] = h
        gh_s[...] = around(gh_s[...])

        for c8 in range(2):
            g = [gh_s[row * 16 + c8 * 8 : row * 16 + c8 * 8 + 8] for row in range(12)]
            for k in range(5):
                start = k * 64 + c8 * 32
                p = xb_rows(start)
                v = lat_in([p[row] * g[row] for row in range(12)])
                for r in range(4):
                    yh_s[every4(start + r), :] = v[r]
        hi, lo = split2(yh_s[...])
        vh_s[0] = hi
        vh_s[1] = lo

    def run(copies, what):
        for condition, copy in copies:
            if condition is None:
                getattr(copy, what)()
            else:
                pl.when(condition)(lambda copy=copy: getattr(copy, what)())

    def gradient(first, count, halo, rows, i):
        for c8 in range(2):
            g = [gx_s[row * 16 + c8 * 8 : row * 16 + c8 * 8 + 8] for row in range(12)]
            for k in range(count):
                start = k * 64 + c8 * 32
                p = rows(start)
                v = lat_in([p[row] * g[row] for row in range(12)])
                for r in range(4):
                    y_s[every4(first + start + r), :] = v[r]
        n = count * 64
        hi, lo = split2(y_s[first : first + n])
        hi = jnp.concatenate([hi, vh_s[0, halo : halo + n]], axis=1)
        lo = jnp.concatenate([lo, vh_s[1, halo : halo + n]], axis=1)
        return dot(hi, wa[i, 0]) + dot(lo, wa[i, 0]) + dot(hi, wa[i, 1])

    def member_step(i):
        u = gradient(0, 4, 0, lambda start: pert_rows(pl.multiple_of(i * CHUNK, CHUNK) + start), i)
        work[rows_of(i), :] = (1.0 - DESCENT) * work[rows_of(i), :] - (DESCENT * ENS) * u

    def done(i):
        return pltpu.make_async_copy(work.at[rows_of(i)], alpha_out.at[rows_of(i)], ao.at[i])

    def static_step(src):
        u = gradient(CHUNK, 1, CHUNK, lambda start: xb_rows(320 + start), 0)
        stat_out[...] = (1.0 - DESCENT) * src[...] - (DESCENT * ENS) * u

    clear()

    fetch.wait()
    for i in range(8, CHUNKS):
        pump(i)
        if i == 9:
            finish_lon(to_right(pack.at[0], side.at[0], as_, ar), to_left(pack.at[1], side.at[1], as_, ar))
            xb[OWN, :320] = side[0] + side[1]
            direct_x().start()
        if i == 13:
            for j in range(1, ngy):
                o2_in(j).wait_recv()
        if i >= 13 and i < 15:
            operator(2 * i - 26)
            operator(2 * i - 25)
        if i < 15:

            @pl.loop(2 * (i - 8), 2 * (i - 8) + 2)
            def _(n):
                landed(n)
                member_chunk(work, n)

    arrival_x().wait_recv()

    @pl.when(has_f)
    def _():
        forward_x().start()

    @pl.loop(CHUNKS - 2, CHUNKS)
    def _(i):
        landed(i)
        member_chunk(work, i)

    @pl.when(has_b)
    def _():
        forward_x().wait_recv()

    static_chunk(stat)
    reduce_and_observe(0)
    clear()

    @pl.loop(0, CHUNKS)
    def _(i):
        member_step(i)
        member_chunk(work, i)

    static_step(stat)
    static_chunk(stat_out)
    reduce_and_observe(1)

    @pl.loop(0, CHUNKS)
    def _(i):
        member_step(i)
        done(i).start()

    static_step(stat_out)
    for i in range(CHUNKS):
        done(i).wait()

    for i in range(CHUNKS):
        direct(i).wait_send()
    direct_x().wait_send()

    @pl.when(has_f)
    def _():
        for i in range(CHUNKS):
            forward(i).wait_send()
        forward_x().wait_send()

    for j in range(1, ngx):
        o1(j).wait_send()
    for j in range(1, ngy):
        o2(j).wait_send()


def per_device(
    alpha, static_control, perturbations, sigma, obs_coef, interp_weights, obs_values, obs_weights, obs_tile, obs_cell
):
    rows = alpha.size // 128
    vmem = pl.BlockSpec(memory_space=pltpu.VMEM)
    args = (
        alpha.reshape(rows, 128),
        perturbations.reshape(rows, 128),
        static_control.reshape(64, 128),
        sigma.reshape(64, 128),
        obs_coef.reshape(16, 1024),
        interp_weights,
        obs_values.reshape(1, 1024),
        obs_weights.reshape(1, 1024),
        obs_tile.reshape(1, 1024),
        obs_cell.reshape(1, 1024),
    )
    dma = pltpu.SemaphoreType.DMA
    V = pltpu.VMEM
    scratch = [
        V((rows, 128), f32),
        V((rows, 128), f32),
        V((2, rows, 128), f32),
        V((3, 384, 128), f32),
        V((2, 320, 128), f32),
        V((2, 320, 128), f32),
        V((CHUNKS, 2, 128, 256), bf16),
        V((CHUNKS, 2, 256, 128), bf16),
        V((320, 128), f32),
        V((320, 128), f32),
        V((2, 320, 128), bf16),
        V((224, 128), f32),
        V((192, 128), f32),
        V((32, 128), f32),
        V((ITERS, 3, 2, 32, 128), f32),
        V((ITERS, 80, 128), f32),
        V((ITERS, 96, 128), f32),
        V((ITERS, 32, 128), f32),
        V((ITERS, 192, 128), f32),
        V((ITERS, 4, 2, 16, 128), f32),
        V((112, 128), f32),
        V((ITERS, 96, 128), f32),
        V((ITERS, 80, 128), f32),
        V((ITERS, 32, 128), f32),
        V((192, 128), f32),
        V((192, 128), f32),
        V((32, 1024), f32),
        V((128, 1024), bf16),
        V((8, 1024), i32),
        V((512, 128), f32),
        V((8, 64, 128), f32),
        V((8, 8, 8, 128), f32),
        V((160, 2048), f32),
        V((128, 2048), bf16),
        V((8, 2048), f32),
        V((2, 160, 128), bf16),
        V((160, 128), f32),
        dma((CHUNKS + 1,)), dma((CHUNKS + 1,)), dma((CHUNKS + 1,)), dma((CHUNKS + 1,)),
        dma((2,)), dma((2,)),
        dma((8,)), dma((8,)), dma((8,)), dma((8,)),
        dma((ITERS, 5)), dma((ITERS, 5)),
        dma((ITERS, 4)), dma((ITERS, 4)),
        dma((ITERS, 8)), dma((ITERS, 8)),
        dma((ITERS, 3)), dma((ITERS, 3)),
        dma((1,)), dma((CHUNKS,)),
    ]
    outs = pl.pallas_call(
        body,
        out_shape=(
            jax.ShapeDtypeStruct((rows, 128), f32),
            jax.ShapeDtypeStruct((64, 128), f32),
            jax.ShapeDtypeStruct((64, 128), f32),
        ),
        in_specs=[pl.BlockSpec(memory_space=pl.ANY)] + [vmem] * (len(args) - 1),
        out_specs=(pl.BlockSpec(memory_space=pl.ANY), vmem, vmem),
        scratch_shapes=scratch,
        name="assimilate",
        compiler_params=pltpu.CompilerParams(
            collective_id=0, has_side_effects=True, vmem_limit_bytes=56 << 20
        ),
    )(*args)
    return (
        outs[0].reshape(alpha.shape),
        outs[1].reshape(static_control.shape),
        outs[2].reshape(static_control.shape),
    )


def solution(mesh):
    placed = (
        P("mem", None, None, "gy", "gx"),
        P(None, None, "gy", "gx"),
        P("mem", None, None, "gy", "gx"),
        P(None, None, "gy", "gx"),
        P(None, None, ("gx", "gy")),
        P(None, ("gx", "gy")),
        P(("gx", "gy")),
        P(("gx", "gy")),
        P(("gx", "gy"), None),
        P(("gx", "gy")),
    )
    return jax.shard_map(
        per_device,
        mesh=mesh,
        in_specs=placed,
        out_specs=(
            P("mem", None, None, "gy", "gx"),
            P(None, None, "gy", "gx"),
            P(None, None, "gy", "gx"),
        ),
        check_vma=False,
    )
```

```python
import math

import jax
import jax.numpy as jnp
from jax import lax
from jax.experimental import pallas as pl
from jax.experimental.pallas import tpu as pltpu
from jax.sharding import PartitionSpec as P

f32, bf16, i32 = jnp.float32, jnp.bfloat16, jnp.int32
MESH = pl.DeviceIdType.MESH

MEMBERS = 128
ITERS = 2
ENS = 0.8660254037844386 / math.sqrt(MEMBERS - 1)
STATIC = 0.5
DESCENT = 0.2
GAIN = 4.0


def four_passes():
    taps = [1.0]
    for _ in range(4):
        wide = [0.0] * (len(taps) + 2)
        for i, t in enumerate(taps):
            wide[i] += 0.45 * t
            wide[i + 1] += 0.1 * t
            wide[i + 2] += 0.45 * t
        taps = wide
    return taps[4:]


TAP = four_passes()

CHUNK = 256
CHUNKS = 16
AHEAD = 3
BELOW, ABOVE, OWN = 0, 1, 2


def split2(x):
    hi = x.astype(bf16)
    return hi, (x - hi.astype(f32)).astype(bf16)


def split3(x):
    hi = x.astype(bf16)
    rest = x - hi.astype(f32)
    mid = rest.astype(bf16)
    return hi, mid, (rest - mid.astype(f32)).astype(bf16)


def dot(a, b):
    return jnp.dot(a, b, preferred_element_type=f32)


def dot_nt(a, b):
    return lax.dot_general(a, b, (((1,), (1,)), ((), ())), preferred_element_type=f32)


def iota(shape, dim):
    return lax.broadcasted_iota(i32, shape, dim)


def tap_of(distance):
    out = jnp.zeros(distance.shape, f32)
    for d in range(5):
        out = jnp.where(distance == d, TAP[d], out)
    return out


def body(
    alpha, pert, stat, sig, coef, interp, oval, owgt, tile, cell,
    alpha_out, stat_out, inc_out,
    own, work, buf, xb, pack, side, wf, wa, y_a, y_b, y_c, yh_s, vh_s, eb, eh_s, msend, mrecv,
    f_dn, f_up, f_up2, f_mem, nrecv, gb, g_dn, g_up, g_dn2, gx_s, gh_s,
    feat, ft, key_s, sb, tb, rb, qt, cm, ov, lh, gacc,
    ps, pr, fs, fr, as_, ar, o1s, o1r, o2s, o2r, ms, mr, bs, br, ns, nr, ds_, dr, al, ao,
):
    mem, gx, gy = lax.axis_index("mem"), lax.axis_index("gx"), lax.axis_index("gy")
    ngx, ngy = lax.axis_size("gx"), lax.axis_size("gy")
    par = lax.rem(gy, 2)
    partner = gy + 1 - 2 * par
    gy_f = gy + 2 - 4 * par
    has_f = (gy_f >= 0) & (gy_f < ngy)
    gy_b = gy - 2 + 4 * par
    has_b = (gy_b >= 0) & (gy_b < ngy)
    top = jnp.where(gy == 0, 1.0, 0.0)
    bottom = jnp.where(gy == ngy - 1, 1.0, 0.0)
    west = jnp.where(gx == 0, 1.0, 0.0)
    east = jnp.where(gx == ngx - 1, 1.0, 0.0)
    has_l, has_r = gx > 0, gx < ngx - 1
    lane8 = iota((8, 128), 1)

    barrier = pltpu.get_barrier_semaphore()

    def greet(m, x, y):
        pl.semaphore_signal(barrier, inc=1, device_id=(m, lax.rem(x + ngx, ngx), lax.rem(y + ngy, ngy)), device_id_type=MESH)

    for j in range(1, ngx):
        greet(mem, gx + j, gy)
    for j in range(1, ngy):
        greet(mem, gx, gy + j)
    for j in range(ngy):
        greet(1 - mem, gx, gy + j)
    for dx in (-1, 1):
        greet(1 - mem, gx + dx, gy)
        for dy in (-1, 1):
            greet(1 - mem, gx + dx, gy + dy)
        for dy in (-2, 2):
            greet(mem, gx + dx, gy + dy)
    pl.semaphore_wait(barrier, ngx + 2 * ngy - 2 + 10)

    def remote(src, dst, s, r, device):
        return pltpu.make_async_remote_copy(
            src_ref=src, dst_ref=dst, send_sem=s, recv_sem=r, device_id=device, device_id_type=MESH
        )

    def rows_of(i):
        return pl.ds(pl.multiple_of(i * CHUNK, CHUNK), CHUNK)

    def direct(i):
        return remote(own.at[rows_of(i)], buf.at[par, rows_of(i)], ps.at[i], pr.at[i], (mem, gx, partner))

    def arrival(i):
        return remote(own.at[rows_of(i)], buf.at[1 - par, rows_of(i)], ps.at[i], pr.at[i], (mem, gx, partner))

    def forward(i):
        return remote(
            buf.at[1 - par, rows_of(i)], buf.at[par, rows_of(i)], fs.at[i], fr.at[i],
            (mem, gx, lax.rem(gy_f + ngy, ngy)),
        )

    def direct_x():
        return remote(xb.at[OWN], xb.at[par], ps.at[CHUNKS], pr.at[CHUNKS], (mem, gx, partner))

    def arrival_x():
        return remote(xb.at[OWN], xb.at[1 - par], ps.at[CHUNKS], pr.at[CHUNKS], (mem, gx, partner))

    def forward_x():
        return remote(
            xb.at[1 - par], xb.at[par], fs.at[CHUNKS], fr.at[CHUNKS], (mem, gx, lax.rem(gy_f + ngy, ngy))
        )

    def issue(i):
        own[rows_of(i), :] = pert[rows_of(i), :].astype(f32)
        direct(i).start()

    def pump(i):
        arrival(i).wait_recv()

        @pl.when(has_f)
        def _():
            forward(i).start()

        if isinstance(i, int) and i + AHEAD < CHUNKS:
            issue(i + AHEAD)

    def landed(i):
        @pl.when(has_b)
        def _():
            forward(i).wait_recv()

    for i in range(AHEAD):
        issue(i)
    fetch = pltpu.make_async_copy(alpha, work, al.at[0])
    fetch.start()

    @pl.when(jnp.logical_not(has_b))
    def _():
        @pl.loop(0, CHUNKS)
        def _(i):
            buf[par, rows_of(i), :] = jnp.zeros((CHUNK, 128), f32)

        xb[par] = jnp.zeros(xb.shape[1:], f32)

    @pl.when(gx == 0)
    def _():
        side[0] = jnp.zeros(side.shape[1:], f32)
        for it in range(ITERS):
            mrecv[it, 0] = jnp.zeros(mrecv.shape[2:], f32)
            for n in range(4):
                nrecv[it, n, 0] = jnp.zeros((16, 128), f32)

    @pl.when(gx == ngx - 1)
    def _():
        side[1] = jnp.zeros(side.shape[1:], f32)
        for it in range(ITERS):
            mrecv[it, 1] = jnp.zeros(mrecv.shape[2:], f32)
            for n in range(4):
                nrecv[it, n, 1] = jnp.zeros((16, 128), f32)

    @pl.when(gy == 0)
    def _():
        f_dn[...] = jnp.zeros(f_dn.shape, f32)
        g_dn[...] = jnp.zeros(g_dn.shape, f32)
        for it in range(ITERS):
            nrecv[it, 1] = jnp.zeros((2, 16, 128), f32)

    @pl.when(gy < 2)
    def _():
        g_dn2[...] = jnp.zeros(g_dn2.shape, f32)
        for it in range(ITERS):
            nrecv[it, 3] = jnp.zeros((2, 16, 128), f32)

    @pl.when(gy == ngy - 1)
    def _():
        f_up[...] = jnp.zeros(f_up.shape, f32)
        g_up[...] = jnp.zeros(g_up.shape, f32)
        for it in range(ITERS):
            nrecv[it, 2] = jnp.zeros((2, 16, 128), f32)

    @pl.when(gy >= ngy - 2)
    def _():
        f_up2[...] = jnp.zeros(f_up2.shape, f32)

    px, pa = iota((128, 128), 0), iota((128, 128), 1)

    tri = jnp.where(px < pa, 1.0, 0.0).astype(bf16)
    totals = jnp.zeros((64, 1), f32)
    for b in range(8):
        t = tile[:, b * 128 : (b + 1) * 128]
        one = jnp.where(iota((64, 128), 0) == t, 1.0, 0.0)
        before = dot(one.astype(bf16), tri) + totals
        rank = jnp.sum(before * one, axis=0, keepdims=True).astype(i32)
        totals = totals + jnp.sum(one, axis=1, keepdims=True)
        key_s[0:1, b * 128 : (b + 1) * 128] = (rank >> 3) * 512 + t * 8 + (rank & 7)
    feat[...] = jnp.zeros(feat.shape, f32)
    feat[0:16] = coef[...]
    feat[16:20] = interp[...]
    feat[20:21] = (cell[...] >> 9).astype(f32)
    feat[21:22] = ((cell[...] & 255) >> 1).astype(f32)
    feat[22:23] = oval[...]
    feat[23:24] = owgt[...]
    for n, part in enumerate(split3(feat[...])):
        ft[n * 32 : (n + 1) * 32] = part
    ft[96:128] = jnp.zeros((32, 1024), bf16)
    pump(0)

    def sort_records(q):
        total = jnp.zeros((128, 128), f32)
        key = key_s[0:1, :]
        lane = iota((128, 128), 1)
        for g in range(4):
            pick = jnp.where(iota((128, 1024), 0) + (g * 512 + q * 128) == key, 1.0, 0.0).astype(bf16)
            x = dot_nt(pick, ft[...])
            x = x + pltpu.roll(x, 96, 1) + pltpu.roll(x, 64, 1)
            x = pltpu.roll(x, 32 * g, 1) if g else x
            total = total + jnp.where((lane >= 32 * g) & (lane < 32 * g + 32), x, 0.0)
        sb[q * 128 : (q + 1) * 128] = total

    sort_records(0)
    sort_records(1)
    pump(1)
    sort_records(2)
    sort_records(3)
    pump(2)

    def o1(j):
        to = lax.rem(gx + j, ngx)
        return remote(
            sb.at[pl.ds(pl.multiple_of(to * 64, 64), 64)], tb.at[gx], o1s.at[j], o1r.at[gx], (mem, to, gy)
        )

    def o1_in(j):
        of = lax.rem(gx - j + ngx, ngx)
        return remote(sb.at[pl.ds(0, 64)], tb.at[of], o1s.at[j], o1r.at[of], (mem, of, gy))

    for j in range(1, ngx):
        o1(j).start()
    tb[gx] = sb[pl.ds(pl.multiple_of(gx * 64, 64), 64), :]
    pump(3)

    pack[...] = jnp.zeros(pack.shape, f32)

    def selection(i):
        j = pa - 8 * i
        last = jnp.where((j >= 0) & (j < 4) & (px == 124 + j), 1.0, 0.0)
        first = jnp.where((j >= 4) & (j < 8) & (px == j - 4), 1.0, 0.0)
        return jnp.concatenate([last, first], axis=1).astype(bf16)

    @pl.loop(0, CHUNKS)
    def _(i):
        picked = dot(pert[rows_of(i), :], selection(i))
        pack[0, :CHUNK] += picked[:, :128]
        pack[1, :CHUNK] += picked[:, 128:]

    scaled = sig[...] * (STATIC / ENS)
    xb[OWN, 320:384] = scaled
    hi, mid, lo = split3(scaled)
    sel = selection(0)
    picked = dot(hi, sel) + dot(mid, sel) + dot(lo, sel)
    pack[0, CHUNK:] = picked[:, :128]
    pack[1, CHUNK:] = picked[:, 128:]

    right, left = lax.rem(gx + 1, ngx), lax.rem(gx + ngx - 1, ngx)

    def to_right(src, dst, sems, recvs):
        return remote(src, dst, sems.at[0], recvs.at[0], (mem, right, gy))

    def to_left(src, dst, sems, recvs):
        return remote(src, dst, sems.at[1], recvs.at[1], (mem, left, gy))

    def exchange_lon(a_src, b_src, dst, sems, recvs, wait=True):
        a, b = to_right(a_src, dst.at[0], sems, recvs), to_left(b_src, dst.at[1], sems, recvs)

        @pl.when(has_r)
        def _():
            a.start()

        @pl.when(has_l)
        def _():
            b.start()

        if wait:
            finish_lon(a, b)

    def finish_lon(a, b):
        @pl.when(has_l)
        def _():
            a.wait_recv()

        @pl.when(has_r)
        def _():
            b.wait_recv()

        @pl.when(has_r)
        def _():
            a.wait_send()

        @pl.when(has_l)
        def _():
            b.wait_send()

    exchange_lon(pack.at[0], pack.at[1], side, as_, ar, False)
    pump(4)

    main = tap_of(jnp.abs(px - pa)) - west * tap_of(px + pa + 2) - east * tap_of(256 - px - pa)
    main_hi, main_lo = split2(main)

    def matrices(first, last):
        @pl.loop(first, last)
        def _(i):
            j = pa - 8 * i
            d = jnp.where(j < 4, px + 4 - j, 124 + j - px)
            h_hi, h_lo = split2(jnp.where((j >= 0) & (j < 8), tap_of(d), 0.0))
            wf[i, 0:128] = jnp.concatenate([main_hi, h_hi], axis=1)
            wf[i, 128:256] = jnp.concatenate([main_hi, h_hi], axis=1)
            wf[i, 256:384] = jnp.concatenate([main_lo, h_lo], axis=1)
            j = px - 8 * i
            d = jnp.where(j < 4, pa + 4 - j, 124 + j - pa)
            h_hi, h_lo = split2(jnp.where((j >= 0) & (j < 8), tap_of(d), 0.0))
            wa[i, :, :128] = jnp.concatenate([main_hi, h_hi], axis=0)
            wa[i, :, 128:] = jnp.concatenate([main_lo, h_lo], axis=0)

    matrices(0, 8)
    pump(5)
    matrices(8, CHUNKS)
    pump(6)
    pump(7)
    for j in range(1, ngx):
        o1_in(j).wait_recv()

    def near(j):
        return mem if j % 2 == 0 else 1 - mem

    def o2(j):
        to = lax.rem(gy + j, ngy)
        return remote(
            tb.at[:, pl.ds(pl.multiple_of(to * 8, 8), 8)], rb.at[gy], o2s.at[j], o2r.at[gy], (near(j), gx, to)
        )

    def o2_in(j):
        of = lax.rem(gy - j + ngy, ngy)
        return remote(tb.at[:, pl.ds(0, 8)], rb.at[of], o2s.at[j], o2r.at[of], (near(j), gx, of))

    for j in range(1, ngy):
        o2(j).start()
    rb[gy] = tb[:, pl.ds(pl.multiple_of(gy * 8, 8), 8), :]
    def operator(q):
        turned = rb[q * 2 : q * 2 + 2].reshape(128, 128).T
        for g in range(4):
            at = pl.ds((g * 4 + q) * 128, 128)
            f = turned[g * 32 : (g + 1) * 32]
            rr, xx = f[20:21], f[21:22]
            for dc in range(2):
                upper, lower = f[16 + dc : 17 + dc], f[18 + dc : 19 + dc]
                for row in range(5):
                    w = jnp.where(rr == float(row), upper, 0.0) + jnp.where(rr == float(row - 1), lower, 0.0)
                    qt[dc * 80 + row * 16 : dc * 80 + row * 16 + 16, at] = f[0:16] * w
            cm[:, at] = jnp.where(px.astype(f32) == xx, 1.0, 0.0).astype(bf16)
            ov[0:1, at] = f[22:23]
            ov[1:2, at] = f[23:24]

    def lat(row, i):
        d = abs(row - i)
        if d > 4:
            return None
        c = GAIN * TAP[d]
        if 0 <= row < 4:
            if row + i + 2 <= 4:
                c = c - top * (GAIN * TAP[row + i + 2])
            if 8 - row - i <= 4:
                c = c - bottom * (GAIN * TAP[8 - row - i])
        return c

    COEF = [[lat(row - 4, i) for i in range(4)] for row in range(12)]

    def lat_out(y):
        z = []
        for row in range(12):
            acc = None
            for i in range(4):
                if COEF[row][i] is not None:
                    term = COEF[row][i] * y[i]
                    acc = term if acc is None else acc + term
            z.append(acc)
        return z

    def lat_in(q):
        v = []
        for i in range(4):
            acc = None
            for row in range(12):
                if COEF[row][i] is not None:
                    term = COEF[row][i] * q[row]
                    acc = term if acc is None else acc + term
            v.append(acc)
        return v

    def every4(start):
        return pl.ds(start, 8, stride=4)

    def pert_rows(start):
        at = [every4(start + r) for r in range(4)]
        return (
            [buf[BELOW, a, :] for a in at] + [own[a, :] for a in at] + [buf[ABOVE, a, :] for a in at]
        )

    def xb_rows(start):
        return [xb[b, every4(start + r), :] for b in (BELOW, OWN, ABOVE) for r in range(4)]

    def lon(x, i):
        hi, lo = split2(x)
        return dot(jnp.concatenate([hi, lo], axis=1), wf[i, 0:256]) + dot(hi, wf[i, 256:384])

    def eb_at(row, c8):
        return pl.ds((row + 1) * 16 + c8 * 8, 8)

    def accumulate(parts, count):
        for c8 in range(2):
            acc = [eb[eb_at(row, c8), :] for row in range(12)]
            for y, rows in parts:
                for k in range(count):
                    start = k * 64 + c8 * 32
                    z = lat_out([y[every4(start + r), :] for r in range(4)])
                    p = rows(start)
                    acc = [acc[row] + z[row] * p[row] for row in range(12)]
            for row in range(12):
                eb[eb_at(row, c8), :] = acc[row]

    def clear():
        eb[...] = jnp.zeros(eb.shape, f32)
        yh_s[...] = jnp.zeros(yh_s.shape, f32)

    def rows_from(i):
        return lambda start: pert_rows(pl.multiple_of(i * CHUNK, CHUNK) + start)

    def member_pair(i, xs):
        for y, x, n in zip((y_a, y_b), xs, (i, i + 1)):
            wide = lon(x, n)
            y[...] = wide[:, :128]
            yh_s[:CHUNK] += wide[:, 128:]
        accumulate([(y_a, rows_from(i)), (y_b, rows_from(i + 1))], 4)

    def static_chunk(src):
        wide = lon(src[...] * jnp.where(mem == 0, 1.0, 0.0), 0)
        y_c[...] = wide[:, :128]
        yh_s[CHUNK:] = wide[:, 128:]
        accumulate([(y_c, lambda start: xb_rows(320 + start))], 1)

    lane16 = iota((16, 128), 1)
    group16, place16 = lane16 >> 3, lane16 & 7

    def around(x):
        for s in (8, 16, 32, 64):
            x = x + pltpu.roll(x, s, 1)
        return x

    def turn(x, s):
        s = s % 128
        return pltpu.roll(x, s, 1) if s else x

    def reduce_and_observe(it):
        whole = remote(eb.at[pl.ds(16, 192)], f_mem.at[it], bs.at[it, 0], br.at[it, 0], (1 - mem, gx, gy))
        whole.start()
        for c8 in range(2):
            acc = [jnp.zeros((8, 128), f32) for _ in range(12)]
            for k in range(5):
                start = k * 64 + c8 * 32
                z = lat_out([yh_s[every4(start + r), :] for r in range(4)])
                p = xb_rows(start)
                acc = [acc[row] + z[row] * p[row] for row in range(12)]
            for row in range(12):
                eh_s[row * 16 + c8 * 8 : row * 16 + c8 * 8 + 8] = acc[row]
        eh = around(eh_s[...])
        halo, edge = jnp.zeros((16, 128), f32), jnp.zeros((16, 128), f32)
        for row in range(12):
            at = row * 16
            halo = jnp.where(group16 == row, eh[at : at + 16], halo)
            edge = jnp.where(lane16 == 8 * row + 4, turn(eb[16 + at : 32 + at], 8 * row + 4), edge)
        msend[0:16] = halo
        msend[16:32] = edge

        def columns():
            out = []
            for flip in range(2):
                m = mem if flip == 0 else 1 - mem
                out.append((has_r, has_l, remote(msend, mrecv.at[it, 0, mem], ms.at[it, flip], mr.at[it, flip], (m, right, gy))))
                out.append((has_l, has_r, remote(msend, mrecv.at[it, 1, mem], ms.at[it, 2 + flip], mr.at[it, 2 + flip], (m, left, gy))))
            out.append((None, None, remote(msend, mrecv.at[it, 2, 0], ms.at[it, 4], mr.at[it, 4], (1 - mem, gx, gy))))
            return out

        run([(c, x) for c, _, x in columns()], "start")
        run([(c, x) for _, c, x in columns()] + [(None, whole)], "wait_recv")
        run([(c, x) for c, _, x in columns()] + [(None, whole)], "wait_send")
        m_l = mrecv[it, 0, 0] + mrecv[it, 0, 1]
        m_r = mrecv[it, 1, 0] + mrecv[it, 1, 1]
        m_o = halo + mrecv[it, 2, 0, 0:16]
        for row in range(12):
            at = row * 16
            e = eb[16 + at : 32 + at] + f_mem[it, at : at + 16]
            e = e + jnp.where(lane16 < 4, turn(m_l[0:16], -8 * row - 4), 0.0)
            e = e + jnp.where(lane16 >= 124, turn(m_r[0:16], 124 - 8 * row), 0.0)
            eb[16 + at : 32 + at] = e
        xv = jnp.where((place16 == 4) & (lane16 < 96), m_r[16:32] + m_o, 0.0)
        eb[0:16] = xv
        eb[208:224] = xv

        def rows_out():
            return [
                (gy < ngy - 1, gy > 0, remote(eb.at[pl.ds(144, 80)], f_dn.at[it], bs.at[it, 1], br.at[it, 1], (1 - mem, gx, lax.rem(gy + 1, ngy)))),
                (gy > 0, gy < ngy - 1, remote(eb.at[pl.ds(0, 96)], f_up.at[it], bs.at[it, 2], br.at[it, 2], (1 - mem, gx, lax.rem(gy + ngy - 1, ngy)))),
                (gy > 1, gy < ngy - 2, remote(eb.at[pl.ds(0, 32)], f_up2.at[it], bs.at[it, 3], br.at[it, 3], (mem, gx, lax.rem(gy + ngy - 2, ngy)))),
            ]

        run([(c, x) for c, _, x in rows_out()], "start")
        run([(c, x) for _, c, x in rows_out()], "wait_recv")
        run([(c, x) for c, _, x in rows_out()], "wait_send")
        x = xv + turn(f_dn[it, 64:80], -32) + turn(f_up[it, 0:16], 32)
        x = (x + turn(jnp.where(lane16 == 4, f_up2[it, 0:16], 0.0), 64)) * ENS
        for r in range(5):
            dx = eb[80 + r * 16 : 96 + r * 16] + f_up[it, (r + 1) * 16 : (r + 2) * 16]
            dx = (dx + (f_dn[it, r * 16 : r * 16 + 16] if r < 4 else f_up2[it, 16:32])) * ENS
            moved = jnp.where(lane16 == 127, turn(x, 127 - 8 * (r + 4) - 4), turn(dx, 127))
            if it == ITERS - 1 and r < 4:
                inc_out[every4(r), :] = dx[:8]
                inc_out[every4(32 + r), :] = dx[8:]
            for n, v in ((0, dx), (1, moved)):
                hi, lo = split2(v)
                lh[n * 80 + r * 16 : n * 80 + r * 16 + 16, :128] = hi
                lh[n * 80 + r * 16 : n * 80 + r * 16 + 16, 128:] = lo

        gacc[...] = jnp.zeros(gacc.shape, f32)

        @pl.loop(0, 8)
        def _(n):
            at = pl.ds(pl.multiple_of(n * 256, 256), 256)
            c = cm[:, at]
            u = dot(lh[...], jnp.concatenate([c, c], axis=0))
            q = qt[:, at]
            hx = jnp.sum(q * u, axis=0, keepdims=True)
            misfit = ov[1:2, at] * (hx - ov[0:1, at])
            hi, lo = split2(q * misfit)
            both = dot_nt(jnp.concatenate([hi, lo], axis=0), c)
            gacc[...] += both[:160] + both[160:]

        lane80 = iota((80, 128), 1)
        g0, g1 = gacc[0:80], gacc[80:160]
        gb[16:96] = g0 + jnp.where(lane80 == 0, 0.0, turn(g1, 1))
        sides = jnp.zeros((16, 128), f32)
        for r in range(5):
            at = r * 16
            g5 = gb[16 + at : 32 + at]
            sides = jnp.where(group16 == r, turn(g5, 8 * r + 4), sides)
            sides = jnp.where(lane16 == 64 + 8 * r, turn(g1[at : at + 16], 64 + 8 * r - 127), sides)
        gb[0:16] = sides
        gb[96:112] = sides

        def terms():
            out = [
                (gy < ngy - 1, gy > 0, remote(gb.at[pl.ds(16, 96)], g_dn.at[it], ds_.at[it, 0], dr.at[it, 0], (1 - mem, gx, lax.rem(gy + 1, ngy)))),
                (gy > 0, gy < ngy - 1, remote(gb.at[pl.ds(0, 80)], g_up.at[it], ds_.at[it, 1], dr.at[it, 1], (1 - mem, gx, lax.rem(gy + ngy - 1, ngy)))),
                (gy < ngy - 2, gy > 1, remote(gb.at[pl.ds(80, 32)], g_dn2.at[it], ds_.at[it, 2], dr.at[it, 2], (mem, gx, lax.rem(gy + 2, ngy)))),
            ]
            for n, (m, step) in enumerate(((mem, 0), (1 - mem, 1), (1 - mem, -1), (mem, 2))):
                to, of = gy + step, gy - step
                there, here = (to >= 0) & (to < ngy), (of >= 0) & (of < ngy)
                row = lax.rem(to + ngy, ngy)
                for k, (x, c, d) in enumerate(((right, has_r, has_l), (left, has_l, has_r))):
                    copy = remote(gb.at[pl.ds(0, 16)], nrecv.at[it, n, k], ns.at[it, 2 * n + k], nr.at[it, 2 * n + k], (m, x, row))
                    out.append((c & there, d & here, copy))
            return out

        run([(c, x) for c, _, x in terms()], "start")
        run([(c, x) for _, c, x in terms()], "wait_recv")
        run([(c, x) for c, _, x in terms()], "wait_send")
        beside = [nrecv[it, n] for n in range(4)]
        centre = [sides, g_dn[it, 80:96], g_up[it, 0:16], g_dn2[it, 16:32]]

        def halos(n):
            own = jnp.where((place16 == 4) & (lane16 < 40), turn(centre[n], -60), 0.0)
            return jnp.where(place16 < 4, beside[n][0], beside[n][1] + own)

        def row_of(n, v, r):
            return v + jnp.where(lane16 == 0, turn(beside[n][0], -64 - 8 * r), 0.0)

        halo_own, halo_dn, halo_up, halo_dn2 = [halos(n) for n in range(4)]

        def ext(v, r):
            return jnp.where(lane16 < 8, turn(v, -8 * r), 0.0)

        for r in range(4):
            at = r * 16
            below, own, above = row_of(1, g_dn[it, at : at + 16], r), row_of(0, gb[16 + at : 32 + at], r), row_of(2, g_up[it, 16 + at : 32 + at], r)
            hb, ho, ha = ext(halo_dn, r), ext(halo_own, r), ext(halo_up, r)
            if r == 0:
                below, hb = below + row_of(3, g_dn2[it, 0:16], 4), hb + ext(halo_dn2, 4)
                own, ho = own + row_of(1, g_dn[it, 64:80], 4), ho + ext(halo_dn, 4)
                above, ha = above + row_of(0, gb[80:96], 4), ha + ext(halo_own, 4)
            for n, (v, h) in enumerate(((below, hb), (own, ho), (above, ha))):
                at = n * 64 + r * 16
                gx_s[at : at + 16] = v
                gh_s[at : at + 16] = h
        gh_s[...] = around(gh_s[...])

        for c8 in range(2):
            g = [gh_s[row * 16 + c8 * 8 : row * 16 + c8 * 8 + 8] for row in range(12)]
            for k in range(5):
                start = k * 64 + c8 * 32
                p = xb_rows(start)
                v = lat_in([p[row] * g[row] for row in range(12)])
                for r in range(4):
                    yh_s[every4(start + r), :] = v[r]
        hi, lo = split2(yh_s[...])
        vh_s[0] = hi
        vh_s[1] = lo

    def run(copies, what):
        for condition, copy in copies:
            if condition is None:
                getattr(copy, what)()
            else:
                pl.when(condition)(lambda copy=copy: getattr(copy, what)())

    def gradient_rows(parts, count):
        for c8 in range(2):
            g = [gx_s[row * 16 + c8 * 8 : row * 16 + c8 * 8 + 8] for row in range(12)]
            for y, rows in parts:
                for k in range(count):
                    start = k * 64 + c8 * 32
                    p = rows(start)
                    v = lat_in([p[row] * g[row] for row in range(12)])
                    for r in range(4):
                        y[every4(start + r), :] = v[r]

    def gradient(y, halo, i):
        n = y.shape[0]
        hi, lo = split2(y[...])
        hi = jnp.concatenate([hi, vh_s[0, halo : halo + n]], axis=1)
        lo = jnp.concatenate([lo, vh_s[1, halo : halo + n]], axis=1)
        both = dot(hi, wa[i])
        return both[:, :128] + both[:, 128:] + dot(lo, wa[i, :, :128])

    def member_steps(i):
        gradient_rows([(y_a, rows_from(i)), (y_b, rows_from(i + 1))], 4)
        out = []
        for y, n in ((y_a, i), (y_b, i + 1)):
            x = (1.0 - DESCENT) * work[rows_of(n), :] - (DESCENT * ENS) * gradient(y, 0, n)
            work[rows_of(n), :] = x
            out.append(x)
        return out

    def done(i):
        return pltpu.make_async_copy(work.at[rows_of(i)], alpha_out.at[rows_of(i)], ao.at[i])

    def static_step(src):
        gradient_rows([(y_c, lambda start: xb_rows(320 + start))], 1)
        stat_out[...] = (1.0 - DESCENT) * src[...] - (DESCENT * ENS) * gradient(y_c, CHUNK, 0)

    clear()

    fetch.wait()
    for i in range(8, CHUNKS):
        pump(i)
        if i == 8:
            finish_lon(to_right(pack.at[0], side.at[0], as_, ar), to_left(pack.at[1], side.at[1], as_, ar))
            xb[OWN, :320] = side[0] + side[1]
            direct_x().start()
        if i == 13:
            arrival_x().wait_recv()

            @pl.when(has_f)
            def _():
                forward_x().start()

            for j in range(1, ngy):
                o2_in(j).wait_recv()
        if i >= 13 and i < 15:
            operator(2 * i - 26)
            operator(2 * i - 25)
        if i < 15:

            n = 2 * (i - 8)
            landed(n)
            landed(n + 1)
            member_pair(n, [work[rows_of(n), :], work[rows_of(n + 1), :]])

    landed(CHUNKS - 2)
    landed(CHUNKS - 1)
    member_pair(CHUNKS - 2, [work[rows_of(CHUNKS - 2), :], work[rows_of(CHUNKS - 1), :]])

    @pl.when(has_b)
    def _():
        forward_x().wait_recv()

    static_chunk(stat)
    reduce_and_observe(0)
    clear()

    @pl.loop(0, CHUNKS // 2)
    def _(i):
        member_pair(2 * i, member_steps(2 * i))

    static_step(stat)
    static_chunk(stat_out)
    reduce_and_observe(1)

    @pl.loop(0, CHUNKS // 2)
    def _(i):
        member_steps(2 * i)
        done(2 * i).start()
        done(2 * i + 1).start()

    static_step(stat_out)
    for i in range(CHUNKS):
        done(i).wait()

    for i in range(CHUNKS):
        direct(i).wait_send()
    direct_x().wait_send()

    @pl.when(has_f)
    def _():
        for i in range(CHUNKS):
            forward(i).wait_send()
        forward_x().wait_send()

    for j in range(1, ngx):
        o1(j).wait_send()
    for j in range(1, ngy):
        o2(j).wait_send()


def hand_over(a, b, c, a_out, b_out, c_out, a_s, b_s, c_s, ins, outs):
    parts = [pl.ds(n * (a.shape[0] // 8), a.shape[0] // 8) for n in range(8)]
    moves = [(a.at[p], a_s.at[p], a_out.at[p]) for p in parts] + [(b, b_s, b_out), (c, c_s, c_out)]
    fetches = [pltpu.make_async_copy(x, y, ins.at[n]) for n, (x, y, _) in enumerate(moves)]
    stores = [pltpu.make_async_copy(y, z, outs.at[n]) for n, (_, y, z) in enumerate(moves)]
    for copy in fetches:
        copy.start()
    for fetch, store in zip(fetches, stores):
        fetch.wait()
        store.start()
    for copy in stores:
        copy.wait()


def per_device(
    alpha, static_control, perturbations, sigma, obs_coef, interp_weights, obs_values, obs_weights, obs_tile, obs_cell
):
    rows = alpha.size // 128
    vmem = pl.BlockSpec(memory_space=pltpu.VMEM)
    args = (
        alpha.reshape(rows, 128),
        perturbations.reshape(rows, 128),
        static_control.reshape(64, 128),
        sigma.reshape(64, 128),
        obs_coef.reshape(16, 1024),
        interp_weights,
        obs_values.reshape(1, 1024),
        obs_weights.reshape(1, 1024),
        obs_tile.reshape(1, 1024),
        obs_cell.reshape(1, 1024),
    )
    dma = pltpu.SemaphoreType.DMA
    V = pltpu.VMEM
    scratch = [
        V((rows, 128), f32),
        V((rows, 128), f32),
        V((2, rows, 128), f32),
        V((3, 384, 128), f32),
        V((2, 320, 128), f32),
        V((2, 320, 128), f32),
        V((CHUNKS, 384, 256), bf16),
        V((CHUNKS, 256, 256), bf16),
        V((CHUNK, 128), f32),
        V((CHUNK, 128), f32),
        V((64, 128), f32),
        V((320, 128), f32),
        V((2, 320, 128), bf16),
        V((224, 128), f32),
        V((192, 128), f32),
        V((32, 128), f32),
        V((ITERS, 3, 2, 32, 128), f32),
        V((ITERS, 80, 128), f32),
        V((ITERS, 96, 128), f32),
        V((ITERS, 32, 128), f32),
        V((ITERS, 192, 128), f32),
        V((ITERS, 4, 2, 16, 128), f32),
        V((112, 128), f32),
        V((ITERS, 96, 128), f32),
        V((ITERS, 80, 128), f32),
        V((ITERS, 32, 128), f32),
        V((192, 128), f32),
        V((192, 128), f32),
        V((32, 1024), f32),
        V((128, 1024), bf16),
        V((8, 1024), i32),
        V((512, 128), f32),
        V((8, 64, 128), f32),
        V((8, 8, 8, 128), f32),
        V((160, 2048), f32),
        V((128, 2048), bf16),
        V((8, 2048), f32),
        V((160, 256), bf16),
        V((160, 128), f32),
        dma((CHUNKS + 1,)), dma((CHUNKS + 1,)), dma((CHUNKS + 1,)), dma((CHUNKS + 1,)),
        dma((2,)), dma((2,)),
        dma((8,)), dma((8,)), dma((8,)), dma((8,)),
        dma((ITERS, 5)), dma((ITERS, 5)),
        dma((ITERS, 4)), dma((ITERS, 4)),
        dma((ITERS, 8)), dma((ITERS, 8)),
        dma((ITERS, 3)), dma((ITERS, 3)),
        dma((1,)), dma((CHUNKS,)),
    ]
    outs = pl.pallas_call(
        body,
        out_shape=(
            jax.ShapeDtypeStruct((rows, 128), f32),
            jax.ShapeDtypeStruct((64, 128), f32),
            jax.ShapeDtypeStruct((64, 128), f32),
        ),
        in_specs=[pl.BlockSpec(memory_space=pl.ANY)] + [vmem] * (len(args) - 1),
        out_specs=(pl.BlockSpec(memory_space=pl.ANY), vmem, vmem),
        scratch_shapes=scratch,
        name="assimilate",
        compiler_params=pltpu.CompilerParams(
            collective_id=0, has_side_effects=True, vmem_limit_bytes=56 << 20
        ),
    )(*args)
    anywhere = pl.BlockSpec(memory_space=pl.ANY)
    outs = pl.pallas_call(
        hand_over,
        out_shape=tuple(jax.ShapeDtypeStruct(x.shape, f32) for x in outs),
        in_specs=[anywhere] * 3,
        out_specs=(anywhere,) * 3,
        scratch_shapes=[V(x.shape, f32) for x in outs] + [dma((10,)), dma((10,))],
        name="hand_over",
    )(*outs)
    return (
        outs[0].reshape(alpha.shape),
        outs[1].reshape(static_control.shape),
        outs[2].reshape(static_control.shape),
    )


def solution(mesh):
    placed = (
        P("mem", None, None, "gy", "gx"),
        P(None, None, "gy", "gx"),
        P("mem", None, None, "gy", "gx"),
        P(None, None, "gy", "gx"),
        P(None, None, ("gx", "gy")),
        P(None, ("gx", "gy")),
        P(("gx", "gy")),
        P(("gx", "gy")),
        P(("gx", "gy"), None),
        P(("gx", "gy")),
    )
    return jax.shard_map(
        per_device,
        mesh=mesh,
        in_specs=placed,
        out_specs=(
            P("mem", None, None, "gy", "gx"),
            P(None, None, "gy", "gx"),
            P(None, None, "gy", "gx"),
        ),
        check_vma=False,
    )
```

```python
import math

import jax
import jax.numpy as jnp
from jax import lax
from jax.experimental import pallas as pl
from jax.experimental.pallas import tpu as pltpu
from jax.sharding import PartitionSpec as P

f32, bf16, i32 = jnp.float32, jnp.bfloat16, jnp.int32
MESH = pl.DeviceIdType.MESH

MEMBERS = 128
ITERS = 2
ENS = 0.8660254037844386 / math.sqrt(MEMBERS - 1)
STATIC = 0.5
DESCENT = 0.2
GAIN = 4.0


def four_passes():
    taps = [1.0]
    for _ in range(4):
        wide = [0.0] * (len(taps) + 2)
        for i, t in enumerate(taps):
            wide[i] += 0.45 * t
            wide[i + 1] += 0.1 * t
            wide[i + 2] += 0.45 * t
        taps = wide
    return taps[4:]


TAP = four_passes()

CHUNK = 256
CHUNKS = 16
AHEAD = 3
BELOW, ABOVE, OWN = 0, 1, 2


def split2(x):
    hi = x.astype(bf16)
    return hi, (x - hi.astype(f32)).astype(bf16)


def split3(x):
    hi = x.astype(bf16)
    rest = x - hi.astype(f32)
    mid = rest.astype(bf16)
    return hi, mid, (rest - mid.astype(f32)).astype(bf16)


def dot(a, b):
    return jnp.dot(a, b, preferred_element_type=f32)


def dot_nt(a, b):
    return lax.dot_general(a, b, (((1,), (1,)), ((), ())), preferred_element_type=f32)


def iota(shape, dim):
    return lax.broadcasted_iota(i32, shape, dim)


def tap_of(distance):
    out = jnp.zeros(distance.shape, f32)
    for d in range(5):
        out = jnp.where(distance == d, TAP[d], out)
    return out


def body(
    alpha, pert, stat, sig, coef, interp, oval, owgt, tile, cell,
    alpha_out, stat_out, inc_out,
    own, work, buf, xb, pack, side, wf, wa, y_all, y_a, y_b, y_c, yh_s, vh_s, eb, eh_s, msend, mrecv,
    f_dn, f_up, f_up2, f_mem, nrecv, gb, g_dn, g_up, g_dn2, gx_s, gh_s,
    feat, ft, key_s, sb, tb, rb, qt, cm, ov, lh, gacc,
    ps, pr, fs, fr, as_, ar, o1s, o1r, o2s, o2r, ms, mr, bs, br, ns, nr, ds_, dr, al, ao,
):
    mem, gx, gy = lax.axis_index("mem"), lax.axis_index("gx"), lax.axis_index("gy")
    ngx, ngy = lax.axis_size("gx"), lax.axis_size("gy")
    par = lax.rem(gy, 2)
    partner = gy + 1 - 2 * par
    gy_f = gy + 2 - 4 * par
    has_f = (gy_f >= 0) & (gy_f < ngy)
    gy_b = gy - 2 + 4 * par
    has_b = (gy_b >= 0) & (gy_b < ngy)
    top = jnp.where(gy == 0, 1.0, 0.0)
    bottom = jnp.where(gy == ngy - 1, 1.0, 0.0)
    west = jnp.where(gx == 0, 1.0, 0.0)
    east = jnp.where(gx == ngx - 1, 1.0, 0.0)
    has_l, has_r = gx > 0, gx < ngx - 1
    lane8 = iota((8, 128), 1)

    barrier = pltpu.get_barrier_semaphore()

    def greet(m, x, y):
        pl.semaphore_signal(barrier, inc=1, device_id=(m, lax.rem(x + ngx, ngx), lax.rem(y + ngy, ngy)), device_id_type=MESH)

    greet(mem, gx, partner)
    for j in range(2, ngy, 2):
        greet(mem, gx, gy + j)
    for j in range(1, ngx):
        greet(mem, gx + j, gy)
    greet(1 - mem, gx, gy)
    for j in range(1, ngy, 2):
        greet(1 - mem, gx, gy + j)
    for dx in (-1, 1):
        greet(1 - mem, gx + dx, gy)
        for dy in (-1, 1):
            greet(1 - mem, gx + dx, gy + dy)
        for dy in (-2, 2):
            greet(mem, gx + dx, gy + dy)
    pl.semaphore_wait(barrier, ngx + ngy + 10)

    def remote(src, dst, s, r, device):
        return pltpu.make_async_remote_copy(
            src_ref=src, dst_ref=dst, send_sem=s, recv_sem=r, device_id=device, device_id_type=MESH
        )

    def rows_of(i):
        return pl.ds(pl.multiple_of(i * CHUNK, CHUNK), CHUNK)

    def half(h):
        return pl.ds(pl.multiple_of(h * (CHUNK // 2), CHUNK // 2), CHUNK // 2)

    def third(n):
        return pl.ds(n * 128, 128)

    after = (mem, gx, lax.rem(gy_f + ngy, ngy))

    def direct(h):
        return remote(own.at[half(h)], buf.at[par, half(h)], ps.at[h], pr.at[h], (mem, gx, partner))

    def arrival(h):
        return remote(own.at[half(h)], buf.at[1 - par, half(h)], ps.at[h], pr.at[h], (mem, gx, partner))

    def forward(h):
        return remote(buf.at[1 - par, half(h)], buf.at[par, half(h)], fs.at[h], fr.at[h], after)

    def direct_x(n):
        h = 2 * CHUNKS + n
        return remote(xb.at[OWN, third(n)], xb.at[par, third(n)], ps.at[h], pr.at[h], (mem, gx, partner))

    def arrival_x(n):
        h = 2 * CHUNKS + n
        return remote(xb.at[OWN, third(n)], xb.at[1 - par, third(n)], ps.at[h], pr.at[h], (mem, gx, partner))

    def forward_x(n):
        h = 2 * CHUNKS + n
        return remote(xb.at[1 - par, third(n)], xb.at[par, third(n)], fs.at[h], fr.at[h], after)

    def issue(i):
        own[rows_of(i), :] = pert[rows_of(i), :].astype(f32)
        direct(2 * i).start()
        direct(2 * i + 1).start()

    def pump(i):
        for h in (2 * i, 2 * i + 1):
            arrival(h).wait_recv()
            pl.when(has_f)(lambda h=h: forward(h).start())
        if i + AHEAD < CHUNKS:
            issue(i + AHEAD)

    def landed(i):
        @pl.when(has_b)
        def _():
            forward(2 * i).wait_recv()
            forward(2 * i + 1).wait_recv()

    for i in range(AHEAD):
        issue(i)
    fetch = pltpu.make_async_copy(alpha, work, al.at[0])
    fetch.start()

    px, pa = iota((128, 128), 0), iota((128, 128), 1)

    tri = jnp.where(px < pa, 1.0, 0.0).astype(bf16)
    totals = jnp.zeros((64, 1), f32)
    for b in range(8):
        t = tile[:, b * 128 : (b + 1) * 128]
        one = jnp.where(iota((64, 128), 0) == t, 1.0, 0.0)
        before = dot(one.astype(bf16), tri) + totals
        rank = jnp.sum(before * one, axis=0, keepdims=True).astype(i32)
        totals = totals + jnp.sum(one, axis=1, keepdims=True)
        key_s[0:1, b * 128 : (b + 1) * 128] = (rank >> 3) * 512 + t * 8 + (rank & 7)
    feat[...] = jnp.zeros(feat.shape, f32)
    feat[0:16] = coef[...]
    feat[16:20] = interp[...]
    feat[20:21] = (cell[...] >> 9).astype(f32)
    feat[21:22] = ((cell[...] & 255) >> 1).astype(f32)
    feat[22:23] = oval[...]
    feat[23:24] = owgt[...]
    for n, part in enumerate(split3(feat[...])):
        ft[n * 32 : (n + 1) * 32] = part
    ft[96:128] = jnp.zeros((32, 1024), bf16)
    pump(0)

    def sort_records(q):
        total = jnp.zeros((128, 128), f32)
        key = key_s[0:1, :]
        lane = iota((128, 128), 1)
        for g in range(4):
            pick = jnp.where(iota((128, 1024), 0) + (g * 512 + q * 128) == key, 1.0, 0.0).astype(bf16)
            x = dot_nt(pick, ft[...])
            x = x + pltpu.roll(x, 96, 1) + pltpu.roll(x, 64, 1)
            x = pltpu.roll(x, 32 * g, 1) if g else x
            total = total + jnp.where((lane >= 32 * g) & (lane < 32 * g + 32), x, 0.0)
        sb[q * 128 : (q + 1) * 128] = total

    sort_records(0)
    sort_records(1)
    pump(1)
    sort_records(2)
    sort_records(3)
    pump(2)

    def o1(j):
        to = lax.rem(gx + j, ngx)
        return remote(
            sb.at[pl.ds(pl.multiple_of(to * 64, 64), 64)], tb.at[gx], o1s.at[j], o1r.at[gx], (mem, to, gy)
        )

    def o1_in(j):
        of = lax.rem(gx - j + ngx, ngx)
        return remote(sb.at[pl.ds(0, 64)], tb.at[of], o1s.at[j], o1r.at[of], (mem, of, gy))

    for j in range(1, ngx):
        o1(j).start()
    tb[gx] = sb[pl.ds(pl.multiple_of(gx * 64, 64), 64), :]
    pump(3)

    pack[...] = jnp.zeros(pack.shape, f32)

    def selection(i):
        j = pa - 8 * i
        last = jnp.where((j >= 0) & (j < 4) & (px == 124 + j), 1.0, 0.0)
        first = jnp.where((j >= 4) & (j < 8) & (px == j - 4), 1.0, 0.0)
        return jnp.concatenate([last, first], axis=1).astype(bf16)

    @pl.loop(0, CHUNKS)
    def _(i):
        picked = dot(pert[rows_of(i), :], selection(i))
        pack[0, :CHUNK] += picked[:, :128]
        pack[1, :CHUNK] += picked[:, 128:]

    scaled = sig[...] * (STATIC / ENS)
    xb[OWN, 320:384] = scaled
    hi, mid, lo = split3(scaled)
    sel = selection(0)
    picked = dot(hi, sel) + dot(mid, sel) + dot(lo, sel)
    pack[0, CHUNK:] = picked[:, :128]
    pack[1, CHUNK:] = picked[:, 128:]

    right, left = lax.rem(gx + 1, ngx), lax.rem(gx + ngx - 1, ngx)

    def to_right(src, dst, sems, recvs):
        return remote(src, dst, sems.at[0], recvs.at[0], (mem, right, gy))

    def to_left(src, dst, sems, recvs):
        return remote(src, dst, sems.at[1], recvs.at[1], (mem, left, gy))

    def exchange_lon(a_src, b_src, dst, sems, recvs, wait=True):
        a, b = to_right(a_src, dst.at[0], sems, recvs), to_left(b_src, dst.at[1], sems, recvs)

        @pl.when(has_r)
        def _():
            a.start()

        @pl.when(has_l)
        def _():
            b.start()

        if wait:
            finish_lon(a, b)

    def finish_lon(a, b):
        @pl.when(has_l)
        def _():
            a.wait_recv()

        @pl.when(has_r)
        def _():
            b.wait_recv()

        @pl.when(has_r)
        def _():
            a.wait_send()

        @pl.when(has_l)
        def _():
            b.wait_send()

    exchange_lon(pack.at[0], pack.at[1], side, as_, ar, False)
    pump(4)

    main = tap_of(jnp.abs(px - pa)) - west * tap_of(px + pa + 2) - east * tap_of(256 - px - pa)
    main_hi, main_lo = split2(main)

    def matrices(first, last):
        @pl.loop(first, last)
        def _(i):
            j = pa - 8 * i
            d = jnp.where(j < 4, px + 4 - j, 124 + j - px)
            h_hi, h_lo = split2(jnp.where((j >= 0) & (j < 8), tap_of(d), 0.0))
            wf[i, 0:128] = jnp.concatenate([main_hi, h_hi], axis=1)
            wf[i, 128:256] = jnp.concatenate([main_hi, h_hi], axis=1)
            wf[i, 256:384] = jnp.concatenate([main_lo, h_lo], axis=1)
            j = px - 8 * i
            d = jnp.where(j < 4, pa + 4 - j, 124 + j - pa)
            h_hi, h_lo = split2(jnp.where((j >= 0) & (j < 8), tap_of(d), 0.0))
            wa[i, :, :128] = jnp.concatenate([main_hi, h_hi], axis=0)
            wa[i, :, 128:] = jnp.concatenate([main_lo, h_lo], axis=0)

    matrices(0, 8)
    pump(5)
    matrices(8, CHUNKS)
    pump(6)

    @pl.when(jnp.logical_not(has_b))
    def _():
        @pl.loop(0, CHUNKS)
        def _(i):
            buf[par, rows_of(i), :] = jnp.zeros((CHUNK, 128), f32)

        xb[par] = jnp.zeros(xb.shape[1:], f32)

    @pl.when(gx == 0)
    def _():
        side[0] = jnp.zeros(side.shape[1:], f32)
        for it in range(ITERS):
            mrecv[it, 0] = jnp.zeros(mrecv.shape[2:], f32)
            for n in range(4):
                nrecv[it, n, 0] = jnp.zeros((16, 128), f32)

    @pl.when(gx == ngx - 1)
    def _():
        side[1] = jnp.zeros(side.shape[1:], f32)
        for it in range(ITERS):
            mrecv[it, 1] = jnp.zeros(mrecv.shape[2:], f32)
            for n in range(4):
                nrecv[it, n, 1] = jnp.zeros((16, 128), f32)

    @pl.when(gy == 0)
    def _():
        f_dn[...] = jnp.zeros(f_dn.shape, f32)
        g_dn[...] = jnp.zeros(g_dn.shape, f32)
        for it in range(ITERS):
            nrecv[it, 1] = jnp.zeros((2, 16, 128), f32)

    @pl.when(gy < 2)
    def _():
        g_dn2[...] = jnp.zeros(g_dn2.shape, f32)
        for it in range(ITERS):
            nrecv[it, 3] = jnp.zeros((2, 16, 128), f32)

    @pl.when(gy == ngy - 1)
    def _():
        f_up[...] = jnp.zeros(f_up.shape, f32)
        g_up[...] = jnp.zeros(g_up.shape, f32)
        for it in range(ITERS):
            nrecv[it, 2] = jnp.zeros((2, 16, 128), f32)

    @pl.when(gy >= ngy - 2)
    def _():
        f_up2[...] = jnp.zeros(f_up2.shape, f32)

    fetch.wait()
    eb[...] = jnp.zeros(eb.shape, f32)
    yh_s[...] = jnp.zeros(yh_s.shape, f32)

    def lon(x, i):
        hi, lo = split2(x)
        return dot(jnp.concatenate([hi, lo], axis=1), wf[i, 0:256]) + dot(hi, wf[i, 256:384])

    def lon_chunks(first, last):
        @pl.loop(first, last)
        def _(i):
            wide = lon(work[rows_of(i), :], i)
            y_all[rows_of(i), :] = wide[:, :128]
            yh_s[:CHUNK] += wide[:, 128:]

    lon_chunks(0, 8)
    pump(7)
    lon_chunks(8, CHUNKS)
    for j in range(1, ngx):
        o1_in(j).wait_recv()

    def near(j):
        return mem if j % 2 == 0 else 1 - mem

    def o2(j):
        to = lax.rem(gy + j, ngy)
        return remote(
            tb.at[:, pl.ds(pl.multiple_of(to * 8, 8), 8)], rb.at[gy], o2s.at[j], o2r.at[gy], (near(j), gx, to)
        )

    def o2_in(j):
        of = lax.rem(gy - j + ngy, ngy)
        return remote(tb.at[:, pl.ds(0, 8)], rb.at[of], o2s.at[j], o2r.at[of], (near(j), gx, of))

    for j in range(1, ngy):
        o2(j).start()
    rb[gy] = tb[:, pl.ds(pl.multiple_of(gy * 8, 8), 8), :]
    def operator(q):
        turned = rb[q * 2 : q * 2 + 2].reshape(128, 128).T
        for g in range(4):
            at = pl.ds((g * 4 + q) * 128, 128)
            f = turned[g * 32 : (g + 1) * 32]
            rr, xx = f[20:21], f[21:22]
            for dc in range(2):
                upper, lower = f[16 + dc : 17 + dc], f[18 + dc : 19 + dc]
                for row in range(5):
                    w = jnp.where(rr == float(row), upper, 0.0) + jnp.where(rr == float(row - 1), lower, 0.0)
                    qt[dc * 80 + row * 16 : dc * 80 + row * 16 + 16, at] = f[0:16] * w
            cm[:, at] = jnp.where(px.astype(f32) == xx, 1.0, 0.0).astype(bf16)
            ov[0:1, at] = f[22:23]
            ov[1:2, at] = f[23:24]

    def lat(row, i):
        d = abs(row - i)
        if d > 4:
            return None
        c = GAIN * TAP[d]
        if 0 <= row < 4:
            if row + i + 2 <= 4:
                c = c - top * (GAIN * TAP[row + i + 2])
            if 8 - row - i <= 4:
                c = c - bottom * (GAIN * TAP[8 - row - i])
        return c

    COEF = [[lat(row - 4, i) for i in range(4)] for row in range(12)]

    def lat_out(y):
        z = []
        for row in range(12):
            acc = None
            for i in range(4):
                if COEF[row][i] is not None:
                    term = COEF[row][i] * y[i]
                    acc = term if acc is None else acc + term
            z.append(acc)
        return z

    def lat_in(q):
        v = []
        for i in range(4):
            acc = None
            for row in range(12):
                if COEF[row][i] is not None:
                    term = COEF[row][i] * q[row]
                    acc = term if acc is None else acc + term
            v.append(acc)
        return v

    def every4(start):
        return pl.ds(start, 8, stride=4)

    def pert_rows(start):
        at = [every4(start + r) for r in range(4)]
        return (
            [buf[BELOW, a, :] for a in at] + [own[a, :] for a in at] + [buf[ABOVE, a, :] for a in at]
        )

    def xb_rows(start):
        return [xb[b, every4(start + r), :] for b in (BELOW, OWN, ABOVE) for r in range(4)]

    def eb_at(row, c8):
        return pl.ds((row + 1) * 16 + c8 * 8, 8)

    def accumulate(parts, count):
        for c8 in range(2):
            acc = [eb[eb_at(row, c8), :] for row in range(12)]
            for y, first, rows in parts:
                for k in range(count):
                    start = k * 64 + c8 * 32
                    z = lat_out([y[every4(first + start + r), :] for r in range(4)])
                    p = rows(start)
                    acc = [acc[row] + z[row] * p[row] for row in range(12)]
            for row in range(12):
                eb[eb_at(row, c8), :] = acc[row]

    def clear():
        eb[...] = jnp.zeros(eb.shape, f32)
        yh_s[...] = jnp.zeros(yh_s.shape, f32)

    def rows_from(i):
        return lambda start: pert_rows(pl.multiple_of(i * CHUNK, CHUNK) + start)

    def member_pair(i, xs):
        for y, x, n in zip((y_a, y_b), xs, (i, i + 1)):
            wide = lon(x, n)
            y[...] = wide[:, :128]
            yh_s[:CHUNK] += wide[:, 128:]
        accumulate([(y_a, 0, rows_from(i)), (y_b, 0, rows_from(i + 1))], 4)

    def arrived_pair(i):
        landed(i)
        landed(i + 1)
        accumulate([(y_all, n * CHUNK, rows_from(n)) for n in (i, i + 1)], 4)

    def static_chunk(src):
        wide = lon(src[...] * jnp.where(mem == 0, 1.0, 0.0), 0)
        y_c[...] = wide[:, :128]
        yh_s[CHUNK:] = wide[:, 128:]
        accumulate([(y_c, 0, lambda start: xb_rows(320 + start))], 1)

    lane16 = iota((16, 128), 1)
    group16, place16 = lane16 >> 3, lane16 & 7

    def around(x):
        for s in (8, 16, 32, 64):
            x = x + pltpu.roll(x, s, 1)
        return x

    def turn(x, s):
        s = s % 128
        return pltpu.roll(x, s, 1) if s else x

    def halo_columns():
        for c8 in range(2):
            acc = [jnp.zeros((8, 128), f32) for _ in range(12)]
            for k in range(5):
                start = k * 64 + c8 * 32
                z = lat_out([yh_s[every4(start + r), :] for r in range(4)])
                p = xb_rows(start)
                acc = [acc[row] + z[row] * p[row] for row in range(12)]
            for row in range(12):
                eh_s[row * 16 + c8 * 8 : row * 16 + c8 * 8 + 8] = acc[row]
        eh = around(eh_s[...])
        halo = jnp.zeros((16, 128), f32)
        for row in range(12):
            halo = jnp.where(group16 == row, eh[row * 16 : row * 16 + 16], halo)
        msend[0:16] = halo

    def reduce_and_observe(it):
        whole = remote(eb.at[pl.ds(16, 192)], f_mem.at[it], bs.at[it, 0], br.at[it, 0], (1 - mem, gx, gy))
        whole.start()
        if it > 0:
            halo_columns()
        edge = jnp.zeros((16, 128), f32)
        for row in range(12):
            at = row * 16
            edge = jnp.where(lane16 == 8 * row + 4, turn(eb[16 + at : 32 + at], 8 * row + 4), edge)
        halo = msend[0:16]
        msend[16:32] = edge

        def columns():
            out = []
            for flip in range(2):
                m = mem if flip == 0 else 1 - mem
                out.append((has_r, has_l, remote(msend, mrecv.at[it, 0, mem], ms.at[it, flip], mr.at[it, flip], (m, right, gy))))
                out.append((has_l, has_r, remote(msend, mrecv.at[it, 1, mem], ms.at[it, 2 + flip], mr.at[it, 2 + flip], (m, left, gy))))
            out.append((None, None, remote(msend, mrecv.at[it, 2, 0], ms.at[it, 4], mr.at[it, 4], (1 - mem, gx, gy))))
            return out

        run([(c, x) for c, _, x in columns()], "start")
        run([(c, x) for _, c, x in columns()] + [(None, whole)], "wait_recv")
        run([(c, x) for c, _, x in columns()] + [(None, whole)], "wait_send")
        m_l = mrecv[it, 0, 0] + mrecv[it, 0, 1]
        m_r = mrecv[it, 1, 0] + mrecv[it, 1, 1]
        m_o = halo + mrecv[it, 2, 0, 0:16]
        for row in range(12):
            at = row * 16
            e = eb[16 + at : 32 + at] + f_mem[it, at : at + 16]
            e = e + jnp.where(lane16 < 4, turn(m_l[0:16], -8 * row - 4), 0.0)
            e = e + jnp.where(lane16 >= 124, turn(m_r[0:16], 124 - 8 * row), 0.0)
            eb[16 + at : 32 + at] = e
        xv = jnp.where((place16 == 4) & (lane16 < 96), m_r[16:32] + m_o, 0.0)
        eb[0:16] = xv
        eb[208:224] = xv

        def rows_out():
            return [
                (gy < ngy - 1, gy > 0, remote(eb.at[pl.ds(144, 80)], f_dn.at[it], bs.at[it, 1], br.at[it, 1], (1 - mem, gx, lax.rem(gy + 1, ngy)))),
                (gy > 0, gy < ngy - 1, remote(eb.at[pl.ds(0, 96)], f_up.at[it], bs.at[it, 2], br.at[it, 2], (1 - mem, gx, lax.rem(gy + ngy - 1, ngy)))),
                (gy > 1, gy < ngy - 2, remote(eb.at[pl.ds(0, 32)], f_up2.at[it], bs.at[it, 3], br.at[it, 3], (mem, gx, lax.rem(gy + ngy - 2, ngy)))),
            ]

        run([(c, x) for c, _, x in rows_out()], "start")
        run([(c, x) for _, c, x in rows_out()], "wait_recv")
        run([(c, x) for c, _, x in rows_out()], "wait_send")
        x = xv + turn(f_dn[it, 64:80], -32) + turn(f_up[it, 0:16], 32)
        x = (x + turn(jnp.where(lane16 == 4, f_up2[it, 0:16], 0.0), 64)) * ENS
        for r in range(5):
            dx = eb[80 + r * 16 : 96 + r * 16] + f_up[it, (r + 1) * 16 : (r + 2) * 16]
            dx = (dx + (f_dn[it, r * 16 : r * 16 + 16] if r < 4 else f_up2[it, 16:32])) * ENS
            moved = jnp.where(lane16 == 127, turn(x, 127 - 8 * (r + 4) - 4), turn(dx, 127))
            if it == ITERS - 1 and r < 4:
                inc_out[every4(r), :] = dx[:8]
                inc_out[every4(32 + r), :] = dx[8:]
            for n, v in ((0, dx), (1, moved)):
                hi, lo = split2(v)
                lh[n * 80 + r * 16 : n * 80 + r * 16 + 16, :128] = hi
                lh[n * 80 + r * 16 : n * 80 + r * 16 + 16, 128:] = lo

        gacc[...] = jnp.zeros(gacc.shape, f32)

        @pl.loop(0, 8)
        def _(n):
            at = pl.ds(pl.multiple_of(n * 256, 256), 256)
            c = cm[:, at]
            u = dot(lh[...], jnp.concatenate([c, c], axis=0))
            q = qt[:, at]
            hx = jnp.sum(q * u, axis=0, keepdims=True)
            misfit = ov[1:2, at] * (hx - ov[0:1, at])
            hi, lo = split2(q * misfit)
            both = dot_nt(jnp.concatenate([hi, lo], axis=0), c)
            gacc[...] += both[:160] + both[160:]

        lane80 = iota((80, 128), 1)
        g0, g1 = gacc[0:80], gacc[80:160]
        gb[16:96] = g0 + jnp.where(lane80 == 0, 0.0, turn(g1, 1))
        sides = jnp.zeros((16, 128), f32)
        for r in range(5):
            at = r * 16
            g5 = gb[16 + at : 32 + at]
            sides = jnp.where(group16 == r, turn(g5, 8 * r + 4), sides)
            sides = jnp.where(lane16 == 64 + 8 * r, turn(g1[at : at + 16], 64 + 8 * r - 127), sides)
        gb[0:16] = sides
        gb[96:112] = sides

        def terms():
            out = [
                (gy < ngy - 1, gy > 0, remote(gb.at[pl.ds(16, 96)], g_dn.at[it], ds_.at[it, 0], dr.at[it, 0], (1 - mem, gx, lax.rem(gy + 1, ngy)))),
                (gy > 0, gy < ngy - 1, remote(gb.at[pl.ds(0, 80)], g_up.at[it], ds_.at[it, 1], dr.at[it, 1], (1 - mem, gx, lax.rem(gy + ngy - 1, ngy)))),
                (gy < ngy - 2, gy > 1, remote(gb.at[pl.ds(80, 32)], g_dn2.at[it], ds_.at[it, 2], dr.at[it, 2], (mem, gx, lax.rem(gy + 2, ngy)))),
            ]
            for n, (m, step) in enumerate(((mem, 0), (1 - mem, 1), (1 - mem, -1), (mem, 2))):
                to, of = gy + step, gy - step
                there, here = (to >= 0) & (to < ngy), (of >= 0) & (of < ngy)
                row = lax.rem(to + ngy, ngy)
                for k, (x, c, d) in enumerate(((right, has_r, has_l), (left, has_l, has_r))):
                    copy = remote(gb.at[pl.ds(0, 16)], nrecv.at[it, n, k], ns.at[it, 2 * n + k], nr.at[it, 2 * n + k], (m, x, row))
                    out.append((c & there, d & here, copy))
            return out

        run([(c, x) for c, _, x in terms()], "start")
        run([(c, x) for _, c, x in terms()], "wait_recv")
        run([(c, x) for c, _, x in terms()], "wait_send")
        beside = [nrecv[it, n] for n in range(4)]
        centre = [sides, g_dn[it, 80:96], g_up[it, 0:16], g_dn2[it, 16:32]]

        def halos(n):
            own = jnp.where((place16 == 4) & (lane16 < 40), turn(centre[n], -60), 0.0)
            return jnp.where(place16 < 4, beside[n][0], beside[n][1] + own)

        def row_of(n, v, r):
            return v + jnp.where(lane16 == 0, turn(beside[n][0], -64 - 8 * r), 0.0)

        halo_own, halo_dn, halo_up, halo_dn2 = [halos(n) for n in range(4)]

        def ext(v, r):
            return jnp.where(lane16 < 8, turn(v, -8 * r), 0.0)

        for r in range(4):
            at = r * 16
            below, own, above = row_of(1, g_dn[it, at : at + 16], r), row_of(0, gb[16 + at : 32 + at], r), row_of(2, g_up[it, 16 + at : 32 + at], r)
            hb, ho, ha = ext(halo_dn, r), ext(halo_own, r), ext(halo_up, r)
            if r == 0:
                below, hb = below + row_of(3, g_dn2[it, 0:16], 4), hb + ext(halo_dn2, 4)
                own, ho = own + row_of(1, g_dn[it, 64:80], 4), ho + ext(halo_dn, 4)
                above, ha = above + row_of(0, gb[80:96], 4), ha + ext(halo_own, 4)
            for n, (v, h) in enumerate(((below, hb), (own, ho), (above, ha))):
                at = n * 64 + r * 16
                gx_s[at : at + 16] = v
                gh_s[at : at + 16] = h
        gh_s[...] = around(gh_s[...])

        for c8 in range(2):
            g = [gh_s[row * 16 + c8 * 8 : row * 16 + c8 * 8 + 8] for row in range(12)]
            for k in range(5):
                start = k * 64 + c8 * 32
                p = xb_rows(start)
                v = lat_in([p[row] * g[row] for row in range(12)])
                for r in range(4):
                    yh_s[every4(start + r), :] = v[r]
        hi, lo = split2(yh_s[...])
        vh_s[0] = hi
        vh_s[1] = lo

    def run(copies, what):
        for condition, copy in copies:
            if condition is None:
                getattr(copy, what)()
            else:
                pl.when(condition)(lambda copy=copy: getattr(copy, what)())

    def gradient_rows(parts, count):
        for c8 in range(2):
            g = [gx_s[row * 16 + c8 * 8 : row * 16 + c8 * 8 + 8] for row in range(12)]
            for y, rows in parts:
                for k in range(count):
                    start = k * 64 + c8 * 32
                    p = rows(start)
                    v = lat_in([p[row] * g[row] for row in range(12)])
                    for r in range(4):
                        y[every4(start + r), :] = v[r]

    def gradient(y, halo, i):
        n = y.shape[0]
        hi, lo = split2(y[...])
        hi = jnp.concatenate([hi, vh_s[0, halo : halo + n]], axis=1)
        lo = jnp.concatenate([lo, vh_s[1, halo : halo + n]], axis=1)
        both = dot(hi, wa[i])
        return both[:, :128] + both[:, 128:] + dot(lo, wa[i, :, :128])

    def member_steps(i):
        gradient_rows([(y_a, rows_from(i)), (y_b, rows_from(i + 1))], 4)
        out = []
        for y, n in ((y_a, i), (y_b, i + 1)):
            x = (1.0 - DESCENT) * work[rows_of(n), :] - (DESCENT * ENS) * gradient(y, 0, n)
            work[rows_of(n), :] = x
            out.append(x)
        return out

    def done(i):
        return pltpu.make_async_copy(work.at[rows_of(i)], alpha_out.at[rows_of(i)], ao.at[i])

    def static_step(src):
        gradient_rows([(y_c, lambda start: xb_rows(320 + start))], 1)
        stat_out[...] = (1.0 - DESCENT) * src[...] - (DESCENT * ENS) * gradient(y_c, CHUNK, 0)

    for i in range(8, CHUNKS):
        pump(i)
        if i == 8:
            finish_lon(to_right(pack.at[0], side.at[0], as_, ar), to_left(pack.at[1], side.at[1], as_, ar))
            xb[OWN, :320] = side[0] + side[1]
        if 8 <= i < 11:
            direct_x(i - 8).start()
        if 12 <= i < 15:
            arrival_x(i - 12).wait_recv()
            pl.when(has_f)(lambda i=i: forward_x(i - 12).start())
        if i < 14:
            arrived_pair(2 * (i - 8))

    for j in range(1, ngy):
        o2_in(j).wait_recv()
    for q in range(4):
        operator(q)
    arrived_pair(CHUNKS - 4)

    @pl.when(has_b)
    def _():
        for n in range(3):
            forward_x(n).wait_recv()

    static_chunk(stat)
    halo_columns()
    arrived_pair(CHUNKS - 2)
    reduce_and_observe(0)
    clear()

    @pl.loop(0, CHUNKS // 2)
    def _(i):
        member_pair(2 * i, member_steps(2 * i))

    static_step(stat)
    static_chunk(stat_out)
    reduce_and_observe(1)

    @pl.loop(0, CHUNKS // 2)
    def _(i):
        member_steps(2 * i)
        done(2 * i).start()
        done(2 * i + 1).start()

    static_step(stat_out)
    for i in range(CHUNKS):
        done(i).wait()

    for h in range(2 * CHUNKS):
        direct(h).wait_send()
    for n in range(3):
        direct_x(n).wait_send()

    @pl.when(has_f)
    def _():
        for h in range(2 * CHUNKS):
            forward(h).wait_send()
        for n in range(3):
            forward_x(n).wait_send()

    for j in range(1, ngx):
        o1(j).wait_send()
    for j in range(1, ngy):
        o2(j).wait_send()


def hand_over(a, b, c, a_out, b_out, c_out, a_s, b_s, c_s, ins, outs):
    parts = [pl.ds(n * (a.shape[0] // 8), a.shape[0] // 8) for n in range(8)]
    moves = [(a.at[p], a_s.at[p], a_out.at[p]) for p in parts] + [(b, b_s, b_out), (c, c_s, c_out)]
    fetches = [pltpu.make_async_copy(x, y, ins.at[n]) for n, (x, y, _) in enumerate(moves)]
    stores = [pltpu.make_async_copy(y, z, outs.at[n]) for n, (_, y, z) in enumerate(moves)]
    for copy in fetches:
        copy.start()
    for fetch, store in zip(fetches, stores):
        fetch.wait()
        store.start()
    for copy in stores:
        copy.wait()


def per_device(
    alpha, static_control, perturbations, sigma, obs_coef, interp_weights, obs_values, obs_weights, obs_tile, obs_cell
):
    rows = alpha.size // 128
    vmem = pl.BlockSpec(memory_space=pltpu.VMEM)
    args = (
        alpha.reshape(rows, 128),
        perturbations.reshape(rows, 128),
        static_control.reshape(64, 128),
        sigma.reshape(64, 128),
        obs_coef.reshape(16, 1024),
        interp_weights,
        obs_values.reshape(1, 1024),
        obs_weights.reshape(1, 1024),
        obs_tile.reshape(1, 1024),
        obs_cell.reshape(1, 1024),
    )
    dma = pltpu.SemaphoreType.DMA
    V = pltpu.VMEM
    scratch = [
        V((rows, 128), f32),
        V((rows, 128), f32),
        V((2, rows, 128), f32),
        V((3, 384, 128), f32),
        V((2, 320, 128), f32),
        V((2, 320, 128), f32),
        V((CHUNKS, 384, 256), bf16),
        V((CHUNKS, 256, 256), bf16),
        V((rows, 128), f32),
        V((CHUNK, 128), f32),
        V((CHUNK, 128), f32),
        V((64, 128), f32),
        V((320, 128), f32),
        V((2, 320, 128), bf16),
        V((224, 128), f32),
        V((192, 128), f32),
        V((32, 128), f32),
        V((ITERS, 3, 2, 32, 128), f32),
        V((ITERS, 80, 128), f32),
        V((ITERS, 96, 128), f32),
        V((ITERS, 32, 128), f32),
        V((ITERS, 192, 128), f32),
        V((ITERS, 4, 2, 16, 128), f32),
        V((112, 128), f32),
        V((ITERS, 96, 128), f32),
        V((ITERS, 80, 128), f32),
        V((ITERS, 32, 128), f32),
        V((192, 128), f32),
        V((192, 128), f32),
        V((32, 1024), f32),
        V((128, 1024), bf16),
        V((8, 1024), i32),
        V((512, 128), f32),
        V((8, 64, 128), f32),
        V((8, 8, 8, 128), f32),
        V((160, 2048), f32),
        V((128, 2048), bf16),
        V((8, 2048), f32),
        V((160, 256), bf16),
        V((160, 128), f32),
        dma((2 * CHUNKS + 3,)), dma((2 * CHUNKS + 3,)), dma((2 * CHUNKS + 3,)), dma((2 * CHUNKS + 3,)),
        dma((2,)), dma((2,)),
        dma((8,)), dma((8,)), dma((8,)), dma((8,)),
        dma((ITERS, 5)), dma((ITERS, 5)),
        dma((ITERS, 4)), dma((ITERS, 4)),
        dma((ITERS, 8)), dma((ITERS, 8)),
        dma((ITERS, 3)), dma((ITERS, 3)),
        dma((1,)), dma((CHUNKS,)),
    ]
    outs = pl.pallas_call(
        body,
        out_shape=(
            jax.ShapeDtypeStruct((rows, 128), f32),
            jax.ShapeDtypeStruct((64, 128), f32),
            jax.ShapeDtypeStruct((64, 128), f32),
        ),
        in_specs=[pl.BlockSpec(memory_space=pl.ANY)] + [vmem] * (len(args) - 1),
        out_specs=(pl.BlockSpec(memory_space=pl.ANY), vmem, vmem),
        scratch_shapes=scratch,
        name="assimilate",
        compiler_params=pltpu.CompilerParams(
            collective_id=0, has_side_effects=True, vmem_limit_bytes=56 << 20
        ),
    )(*args)
    anywhere = pl.BlockSpec(memory_space=pl.ANY)
    outs = pl.pallas_call(
        hand_over,
        out_shape=tuple(jax.ShapeDtypeStruct(x.shape, f32) for x in outs),
        in_specs=[anywhere] * 3,
        out_specs=(anywhere,) * 3,
        scratch_shapes=[V(x.shape, f32) for x in outs] + [dma((10,)), dma((10,))],
        name="hand_over",
    )(*outs)
    return (
        outs[0].reshape(alpha.shape),
        outs[1].reshape(static_control.shape),
        outs[2].reshape(static_control.shape),
    )


def solution(mesh):
    placed = (
        P("mem", None, None, "gy", "gx"),
        P(None, None, "gy", "gx"),
        P("mem", None, None, "gy", "gx"),
        P(None, None, "gy", "gx"),
        P(None, None, ("gx", "gy")),
        P(None, ("gx", "gy")),
        P(("gx", "gy")),
        P(("gx", "gy")),
        P(("gx", "gy"), None),
        P(("gx", "gy")),
    )
    return jax.shard_map(
        per_device,
        mesh=mesh,
        in_specs=placed,
        out_specs=(
            P("mem", None, None, "gy", "gx"),
            P(None, None, "gy", "gx"),
            P(None, None, "gy", "gx"),
        ),
        check_vma=False,
    )
```

```python
import math

import jax
import jax.numpy as jnp
from jax import lax
from jax.experimental import pallas as pl
from jax.experimental.pallas import tpu as pltpu
from jax.sharding import PartitionSpec as P

f32, bf16, i32 = jnp.float32, jnp.bfloat16, jnp.int32
MESH = pl.DeviceIdType.MESH

MEMBERS = 128
ITERS = 2
ENS = 0.8660254037844386 / math.sqrt(MEMBERS - 1)
STATIC = 0.5
DESCENT = 0.2
GAIN = 4.0


def four_passes():
    taps = [1.0]
    for _ in range(4):
        wide = [0.0] * (len(taps) + 2)
        for i, t in enumerate(taps):
            wide[i] += 0.45 * t
            wide[i + 1] += 0.1 * t
            wide[i + 2] += 0.45 * t
        taps = wide
    return taps[4:]


TAP = four_passes()

CHUNK = 256
CHUNKS = 16
AHEAD = 3
BELOW, ABOVE, OWN = 0, 1, 2


def split2(x):
    hi = x.astype(bf16)
    return hi, (x - hi.astype(f32)).astype(bf16)


def split3(x):
    hi = x.astype(bf16)
    rest = x - hi.astype(f32)
    mid = rest.astype(bf16)
    return hi, mid, (rest - mid.astype(f32)).astype(bf16)


def dot(a, b):
    return jnp.dot(a, b, preferred_element_type=f32)


def dot_nt(a, b):
    return lax.dot_general(a, b, (((1,), (1,)), ((), ())), preferred_element_type=f32)


def iota(shape, dim):
    return lax.broadcasted_iota(i32, shape, dim)


def tap_of(distance):
    out = jnp.zeros(distance.shape, f32)
    for d in range(5):
        out = jnp.where(distance == d, TAP[d], out)
    return out


def body(
    alpha, pert, stat, sig, coef, interp, oval, owgt, tile, cell,
    alpha_out, stat_out, inc_out,
    own, work, buf, xb, pack, side, wf, wa, y_all, y_a, y_b, y_c, yh_s, vh_s, eb, eh_s, msend, mrecv,
    f_dn, f_up, f_up2, f_mem, nrecv, gb, g_dn, g_up, g_dn2, gx_s, gh_s,
    feat, ft, key_s, sb, tb, rb, qt, cm, ov, lh, gacc,
    ps, pr, fs, fr, as_, ar, o1s, o1r, o2s, o2r, ms, mr, bs, br, ns, nr, ds_, dr, al, ao,
):
    mem, gx, gy = lax.axis_index("mem"), lax.axis_index("gx"), lax.axis_index("gy")
    ngx, ngy = lax.axis_size("gx"), lax.axis_size("gy")
    par = lax.rem(gy, 2)
    partner = gy + 1 - 2 * par
    gy_f = gy + 2 - 4 * par
    has_f = (gy_f >= 0) & (gy_f < ngy)
    gy_b = gy - 2 + 4 * par
    has_b = (gy_b >= 0) & (gy_b < ngy)
    top = jnp.where(gy == 0, 1.0, 0.0)
    bottom = jnp.where(gy == ngy - 1, 1.0, 0.0)
    west = jnp.where(gx == 0, 1.0, 0.0)
    east = jnp.where(gx == ngx - 1, 1.0, 0.0)
    has_l, has_r = gx > 0, gx < ngx - 1
    lane8 = iota((8, 128), 1)

    barrier = pltpu.get_barrier_semaphore()

    def greet(m, x, y):
        pl.semaphore_signal(barrier, inc=1, device_id=(m, lax.rem(x + ngx, ngx), lax.rem(y + ngy, ngy)), device_id_type=MESH)

    greet(mem, gx, partner)
    for j in range(2, ngy, 2):
        greet(mem, gx, gy + j)
    for j in range(1, ngx):
        greet(mem, gx + j, gy)
    greet(1 - mem, gx, gy)
    for j in range(1, ngy, 2):
        greet(1 - mem, gx, gy + j)
    for dx in (-1, 1):
        greet(1 - mem, gx + dx, gy)
        for dy in (-1, 1):
            greet(1 - mem, gx + dx, gy + dy)
        for dy in (-2, 2):
            greet(mem, gx + dx, gy + dy)
    pl.semaphore_wait(barrier, ngx + ngy + 10)

    def remote(src, dst, s, r, device):
        return pltpu.make_async_remote_copy(
            src_ref=src, dst_ref=dst, send_sem=s, recv_sem=r, device_id=device, device_id_type=MESH
        )

    def rows_of(i):
        return pl.ds(pl.multiple_of(i * CHUNK, CHUNK), CHUNK)

    def half(h):
        return pl.ds(pl.multiple_of(h * (CHUNK // 2), CHUNK // 2), CHUNK // 2)

    def third(n):
        return pl.ds(n * 128, 128 if n < 2 else 72)

    after = (mem, gx, lax.rem(gy_f + ngy, ngy))

    def direct(h):
        return remote(own.at[half(h)], buf.at[par, half(h)], ps.at[h], pr.at[h], (mem, gx, partner))

    def arrival(h):
        return remote(own.at[half(h)], buf.at[1 - par, half(h)], ps.at[h], pr.at[h], (mem, gx, partner))

    def forward(h):
        return remote(buf.at[1 - par, half(h)], buf.at[par, half(h)], fs.at[h], fr.at[h], after)

    def direct_x(n):
        h = 2 * CHUNKS + n
        return remote(xb.at[OWN, third(n)], xb.at[par, third(n)], ps.at[h], pr.at[h], (mem, gx, partner))

    def arrival_x(n):
        h = 2 * CHUNKS + n
        return remote(xb.at[OWN, third(n)], xb.at[1 - par, third(n)], ps.at[h], pr.at[h], (mem, gx, partner))

    def forward_x(n):
        h = 2 * CHUNKS + n
        return remote(xb.at[1 - par, third(n)], xb.at[par, third(n)], fs.at[h], fr.at[h], after)

    def issue(i):
        own[rows_of(i), :] = pert[rows_of(i), :].astype(f32)
        direct(2 * i).start()
        direct(2 * i + 1).start()

    def pump(i):
        for h in (2 * i, 2 * i + 1):
            arrival(h).wait_recv()
            pl.when(has_f)(lambda h=h: forward(h).start())
        if i + AHEAD < CHUNKS:
            issue(i + AHEAD)

    def landed(i):
        @pl.when(has_b)
        def _():
            forward(2 * i).wait_recv()
            forward(2 * i + 1).wait_recv()

    for i in range(AHEAD):
        issue(i)
    fetch = pltpu.make_async_copy(alpha, work, al.at[0])
    fetch.start()

    px, pa = iota((128, 128), 0), iota((128, 128), 1)
    own_group = (iota((16, 128), 1) >> 3) == iota((16, 128), 0)

    def around(x):
        for s in (8, 16, 32, 64):
            x = x + pltpu.roll(x, s, 1)
        return x

    tri = jnp.where(px < pa, 1.0, 0.0).astype(bf16)
    totals = jnp.zeros((64, 1), f32)
    for b in range(8):
        t = tile[:, b * 128 : (b + 1) * 128]
        one = jnp.where(iota((64, 128), 0) == t, 1.0, 0.0)
        before = dot(one.astype(bf16), tri) + totals
        rank = jnp.sum(before * one, axis=0, keepdims=True).astype(i32)
        totals = totals + jnp.sum(one, axis=1, keepdims=True)
        key_s[0:1, b * 128 : (b + 1) * 128] = (rank >> 3) * 512 + t * 8 + (rank & 7)
    feat[...] = jnp.zeros(feat.shape, f32)
    feat[0:16] = coef[...]
    feat[16:20] = interp[...]
    feat[20:21] = (cell[...] >> 9).astype(f32)
    feat[21:22] = ((cell[...] & 255) >> 1).astype(f32)
    feat[22:23] = oval[...]
    feat[23:24] = owgt[...]
    for n, part in enumerate(split3(feat[...])):
        ft[n * 32 : (n + 1) * 32] = part
    ft[96:128] = jnp.zeros((32, 1024), bf16)
    pump(0)

    def sort_records(q):
        total = jnp.zeros((128, 128), f32)
        key = key_s[0:1, :]
        lane = iota((128, 128), 1)
        for g in range(4):
            pick = jnp.where(iota((128, 1024), 0) + (g * 512 + q * 128) == key, 1.0, 0.0).astype(bf16)
            x = dot_nt(pick, ft[...])
            x = x + pltpu.roll(x, 96, 1) + pltpu.roll(x, 64, 1)
            x = pltpu.roll(x, 32 * g, 1) if g else x
            total = total + jnp.where((lane >= 32 * g) & (lane < 32 * g + 32), x, 0.0)
        sb[q * 128 : (q + 1) * 128] = total

    sort_records(0)
    sort_records(1)
    pump(1)
    sort_records(2)
    sort_records(3)
    pump(2)

    def o1(j):
        to = lax.rem(gx + j, ngx)
        return remote(
            sb.at[pl.ds(pl.multiple_of(to * 64, 64), 64)], tb.at[gx], o1s.at[j], o1r.at[gx], (mem, to, gy)
        )

    def o1_in(j):
        of = lax.rem(gx - j + ngx, ngx)
        return remote(sb.at[pl.ds(0, 64)], tb.at[of], o1s.at[j], o1r.at[of], (mem, of, gy))

    for j in range(1, ngx):
        o1(j).start()
    tb[gx] = sb[pl.ds(pl.multiple_of(gx * 64, 64), 64), :]
    pump(3)

    pack[...] = jnp.zeros(pack.shape, f32)

    def selection(i):
        j = pa - 8 * i
        last = jnp.where((j >= 0) & (j < 4) & (px == 124 + j), 1.0, 0.0)
        first = jnp.where((j >= 4) & (j < 8) & (px == j - 4), 1.0, 0.0)
        return jnp.concatenate([last, first], axis=1).astype(bf16)

    @pl.loop(0, CHUNKS)
    def _(i):
        picked = dot(pert[rows_of(i), :], selection(i))
        pack[0, :CHUNK] += picked[:, :128]
        pack[1, :CHUNK] += picked[:, 128:]

    scaled = sig[...] * (STATIC / ENS)
    xb[OWN, 256:320] = scaled
    hi, mid, lo = split3(scaled)
    sel = selection(0)
    picked = dot(hi, sel) + dot(mid, sel) + dot(lo, sel)
    for n in range(2):
        y_c[...] = picked[:, n * 128 : (n + 1) * 128]
        for r in range(4):
            x = jnp.concatenate([y_c[pl.ds(r, 8, stride=4), :], y_c[pl.ds(32 + r, 8, stride=4), :]], axis=0)
            x = jnp.where(own_group, around(x), 0.0)
            pack[n, CHUNK + r : CHUNK + r + 1] = jnp.sum(x, axis=0, keepdims=True)

    right, left = lax.rem(gx + 1, ngx), lax.rem(gx + ngx - 1, ngx)

    def to_right(src, dst, sems, recvs):
        return remote(src, dst, sems.at[0], recvs.at[0], (mem, right, gy))

    def to_left(src, dst, sems, recvs):
        return remote(src, dst, sems.at[1], recvs.at[1], (mem, left, gy))

    def exchange_lon(a_src, b_src, dst, sems, recvs, wait=True):
        a, b = to_right(a_src, dst.at[0], sems, recvs), to_left(b_src, dst.at[1], sems, recvs)

        @pl.when(has_r)
        def _():
            a.start()

        @pl.when(has_l)
        def _():
            b.start()

        if wait:
            finish_lon(a, b)

    def finish_lon(a, b):
        @pl.when(has_l)
        def _():
            a.wait_recv()

        @pl.when(has_r)
        def _():
            b.wait_recv()

        @pl.when(has_r)
        def _():
            a.wait_send()

        @pl.when(has_l)
        def _():
            b.wait_send()

    exchange_lon(pack.at[0], pack.at[1], side, as_, ar, False)
    pump(4)

    main = tap_of(jnp.abs(px - pa)) - west * tap_of(px + pa + 2) - east * tap_of(256 - px - pa)
    main_hi, main_lo = split2(main)

    def matrices(first, last):
        @pl.loop(first, last)
        def _(i):
            j = pa - 8 * i
            d = jnp.where(j < 4, px + 4 - j, 124 + j - px)
            h_hi, h_lo = split2(jnp.where((j >= 0) & (j < 8), tap_of(d), 0.0))
            wf[i, 0:128] = jnp.concatenate([main_hi, h_hi], axis=1)
            wf[i, 128:256] = jnp.concatenate([main_hi, h_hi], axis=1)
            wf[i, 256:384] = jnp.concatenate([main_lo, h_lo], axis=1)
            j = px - 8 * i
            d = jnp.where(j < 4, pa + 4 - j, 124 + j - pa)
            h_hi, h_lo = split2(jnp.where((j >= 0) & (j < 8), tap_of(d), 0.0))
            wa[i, :, :128] = jnp.concatenate([main_hi, h_hi], axis=0)
            wa[i, :, 128:] = jnp.concatenate([main_lo, h_lo], axis=0)

    matrices(0, 8)
    pump(5)
    matrices(8, CHUNKS)
    pump(6)

    @pl.when(jnp.logical_not(has_b))
    def _():
        @pl.loop(0, CHUNKS)
        def _(i):
            buf[par, rows_of(i), :] = jnp.zeros((CHUNK, 128), f32)

        xb[par] = jnp.zeros(xb.shape[1:], f32)

    @pl.when(gx == 0)
    def _():
        side[0] = jnp.zeros(side.shape[1:], f32)
        for it in range(ITERS):
            mrecv[it, 0] = jnp.zeros(mrecv.shape[2:], f32)
            for n in range(4):
                nrecv[it, n, 0] = jnp.zeros((16, 128), f32)

    @pl.when(gx == ngx - 1)
    def _():
        side[1] = jnp.zeros(side.shape[1:], f32)
        for it in range(ITERS):
            mrecv[it, 1] = jnp.zeros(mrecv.shape[2:], f32)
            for n in range(4):
                nrecv[it, n, 1] = jnp.zeros((16, 128), f32)

    @pl.when(gy == 0)
    def _():
        f_dn[...] = jnp.zeros(f_dn.shape, f32)
        g_dn[...] = jnp.zeros(g_dn.shape, f32)
        for it in range(ITERS):
            nrecv[it, 1] = jnp.zeros((2, 16, 128), f32)

    @pl.when(gy < 2)
    def _():
        g_dn2[...] = jnp.zeros(g_dn2.shape, f32)
        for it in range(ITERS):
            nrecv[it, 3] = jnp.zeros((2, 16, 128), f32)

    @pl.when(gy == ngy - 1)
    def _():
        f_up[...] = jnp.zeros(f_up.shape, f32)
        g_up[...] = jnp.zeros(g_up.shape, f32)
        for it in range(ITERS):
            nrecv[it, 2] = jnp.zeros((2, 16, 128), f32)

    @pl.when(gy >= ngy - 2)
    def _():
        f_up2[...] = jnp.zeros(f_up2.shape, f32)

    fetch.wait()
    eb[...] = jnp.zeros(eb.shape, f32)
    yh_s[...] = jnp.zeros(yh_s.shape, f32)

    def lon(x, i):
        hi, lo = split2(x)
        return dot(jnp.concatenate([hi, lo], axis=1), wf[i, 0:256]) + dot(hi, wf[i, 256:384])

    def lon_chunks(first, last):
        @pl.loop(first, last)
        def _(i):
            wide = lon(work[rows_of(i), :], i)
            y_all[rows_of(i), :] = wide[:, :128]
            yh_s[:CHUNK] += wide[:, 128:]

    lon_chunks(0, 8)
    pump(7)
    lon_chunks(8, CHUNKS)
    for j in range(1, ngx):
        o1_in(j).wait_recv()

    def near(j):
        return mem if j % 2 == 0 else 1 - mem

    def o2(j):
        to = lax.rem(gy + j, ngy)
        return remote(
            tb.at[:, pl.ds(pl.multiple_of(to * 8, 8), 8)], rb.at[gy], o2s.at[j], o2r.at[gy], (near(j), gx, to)
        )

    def o2_in(j):
        of = lax.rem(gy - j + ngy, ngy)
        return remote(tb.at[:, pl.ds(0, 8)], rb.at[of], o2s.at[j], o2r.at[of], (near(j), gx, of))

    for j in range(1, ngy):
        o2(j).start()
    rb[gy] = tb[:, pl.ds(pl.multiple_of(gy * 8, 8), 8), :]
    def operator(q):
        turned = rb[q * 2 : q * 2 + 2].reshape(128, 128).T
        for g in range(4):
            at = pl.ds((g * 4 + q) * 128, 128)
            f = turned[g * 32 : (g + 1) * 32]
            rr, xx = f[20:21], f[21:22]
            for dc in range(2):
                upper, lower = f[16 + dc : 17 + dc], f[18 + dc : 19 + dc]
                for row in range(5):
                    w = jnp.where(rr == float(row), upper, 0.0) + jnp.where(rr == float(row - 1), lower, 0.0)
                    qt[dc * 80 + row * 16 : dc * 80 + row * 16 + 16, at] = f[0:16] * w
            cm[:, at] = jnp.where(px.astype(f32) == xx, 1.0, 0.0).astype(bf16)
            ov[0:1, at] = f[22:23]
            ov[1:2, at] = f[23:24]

    def lat(row, i):
        d = abs(row - i)
        if d > 4:
            return None
        c = GAIN * TAP[d]
        if 0 <= row < 4:
            if row + i + 2 <= 4:
                c = c - top * (GAIN * TAP[row + i + 2])
            if 8 - row - i <= 4:
                c = c - bottom * (GAIN * TAP[8 - row - i])
        return c

    COEF = [[lat(row - 4, i) for i in range(4)] for row in range(12)]

    def lat_out(y):
        z = []
        for row in range(12):
            acc = None
            for i in range(4):
                if COEF[row][i] is not None:
                    term = COEF[row][i] * y[i]
                    acc = term if acc is None else acc + term
            z.append(acc)
        return z

    def lat_in(q):
        v = []
        for i in range(4):
            acc = None
            for row in range(12):
                if COEF[row][i] is not None:
                    term = COEF[row][i] * q[row]
                    acc = term if acc is None else acc + term
            v.append(acc)
        return v

    def every4(start):
        return pl.ds(start, 8, stride=4)

    def pert_rows(start):
        at = [every4(start + r) for r in range(4)]
        return (
            [buf[BELOW, a, :] for a in at] + [own[a, :] for a in at] + [buf[ABOVE, a, :] for a in at]
        )

    def xb_rows(start):
        return [xb[b, every4(start + r), :] for b in (BELOW, OWN, ABOVE) for r in range(4)]

    def eb_at(row, c8):
        return pl.ds((row + 1) * 16 + c8 * 8, 8)

    def accumulate(parts, count):
        for c8 in range(2):
            acc = [eb[eb_at(row, c8), :] for row in range(12)]
            for y, first, rows in parts:
                for k in range(count):
                    start = k * 64 + c8 * 32
                    z = lat_out([y[every4(first + start + r), :] for r in range(4)])
                    p = rows(start)
                    acc = [acc[row] + z[row] * p[row] for row in range(12)]
            for row in range(12):
                eb[eb_at(row, c8), :] = acc[row]

    def clear():
        eb[...] = jnp.zeros(eb.shape, f32)
        yh_s[...] = jnp.zeros(yh_s.shape, f32)

    def rows_from(i):
        return lambda start: pert_rows(pl.multiple_of(i * CHUNK, CHUNK) + start)

    def member_pair(i, xs):
        for y, x, n in zip((y_a, y_b), xs, (i, i + 1)):
            wide = lon(x, n)
            y[...] = wide[:, :128]
            yh_s[:CHUNK] += wide[:, 128:]
        accumulate([(y_a, 0, rows_from(i)), (y_b, 0, rows_from(i + 1))], 4)

    def arrived_pair(i):
        landed(i)
        landed(i + 1)
        accumulate([(y_all, n * CHUNK, rows_from(n)) for n in (i, i + 1)], 4)

    def static_chunk(src):
        wide = lon(src[...] * jnp.where(mem == 0, 1.0, 0.0), 0)
        y_c[...] = wide[:, :128]
        yh_s[CHUNK:] = wide[:, 128:]
        accumulate([(y_c, 0, lambda start: xb_rows(256 + start))], 1)

    lane16 = iota((16, 128), 1)
    group16, place16 = lane16 >> 3, lane16 & 7

    def turn(x, s):
        s = s % 128
        return pltpu.roll(x, s, 1) if s else x

    def halo_columns():
        for c8 in range(2):
            acc = [jnp.zeros((8, 128), f32) for _ in range(12)]
            for k in range(5):
                start = k * 64 + c8 * 32
                z = lat_out([yh_s[every4(start + r), :] for r in range(4)])
                p = xb_rows(start if k < 4 else 328 + c8 * 32)
                acc = [acc[row] + z[row] * p[row] for row in range(12)]
            for row in range(12):
                eh_s[row * 16 + c8 * 8 : row * 16 + c8 * 8 + 8] = acc[row]
        eh = around(eh_s[...])
        halo = jnp.zeros((16, 128), f32)
        for row in range(12):
            halo = jnp.where(group16 == row, eh[row * 16 : row * 16 + 16], halo)
        msend[0:16] = halo

    def reduce_and_observe(it):
        whole = remote(eb.at[pl.ds(16, 192)], f_mem.at[it], bs.at[it, 0], br.at[it, 0], (1 - mem, gx, gy))
        whole.start()
        if it > 0:
            halo_columns()
        edge = jnp.zeros((16, 128), f32)
        for row in range(12):
            at = row * 16
            edge = jnp.where(lane16 == 8 * row + 4, turn(eb[16 + at : 32 + at], 8 * row + 4), edge)
        halo = msend[0:16]
        msend[16:32] = edge

        def columns():
            out = []
            for flip in range(2):
                m = mem if flip == 0 else 1 - mem
                out.append((has_r, has_l, remote(msend, mrecv.at[it, 0, mem], ms.at[it, flip], mr.at[it, flip], (m, right, gy))))
                out.append((has_l, has_r, remote(msend, mrecv.at[it, 1, mem], ms.at[it, 2 + flip], mr.at[it, 2 + flip], (m, left, gy))))
            out.append((None, None, remote(msend, mrecv.at[it, 2, 0], ms.at[it, 4], mr.at[it, 4], (1 - mem, gx, gy))))
            return out

        run([(c, x) for c, _, x in columns()], "start")
        run([(c, x) for _, c, x in columns()] + [(None, whole)], "wait_recv")
        run([(c, x) for c, _, x in columns()] + [(None, whole)], "wait_send")
        m_l = mrecv[it, 0, 0] + mrecv[it, 0, 1]
        m_r = mrecv[it, 1, 0] + mrecv[it, 1, 1]
        m_o = halo + mrecv[it, 2, 0, 0:16]
        for row in range(12):
            at = row * 16
            e = eb[16 + at : 32 + at] + f_mem[it, at : at + 16]
            e = e + jnp.where(lane16 < 4, turn(m_l[0:16], -8 * row - 4), 0.0)
            e = e + jnp.where(lane16 >= 124, turn(m_r[0:16], 124 - 8 * row), 0.0)
            eb[16 + at : 32 + at] = e
        xv = jnp.where((place16 == 4) & (lane16 < 96), m_r[16:32] + m_o, 0.0)
        eb[0:16] = xv
        eb[208:224] = xv

        def rows_out():
            return [
                (gy < ngy - 1, gy > 0, remote(eb.at[pl.ds(144, 80)], f_dn.at[it], bs.at[it, 1], br.at[it, 1], (1 - mem, gx, lax.rem(gy + 1, ngy)))),
                (gy > 0, gy < ngy - 1, remote(eb.at[pl.ds(0, 96)], f_up.at[it], bs.at[it, 2], br.at[it, 2], (1 - mem, gx, lax.rem(gy + ngy - 1, ngy)))),
                (gy > 1, gy < ngy - 2, remote(eb.at[pl.ds(0, 32)], f_up2.at[it], bs.at[it, 3], br.at[it, 3], (mem, gx, lax.rem(gy + ngy - 2, ngy)))),
            ]

        run([(c, x) for c, _, x in rows_out()], "start")
        run([(c, x) for _, c, x in rows_out()], "wait_recv")
        run([(c, x) for c, _, x in rows_out()], "wait_send")
        x = xv + turn(f_dn[it, 64:80], -32) + turn(f_up[it, 0:16], 32)
        x = (x + turn(jnp.where(lane16 == 4, f_up2[it, 0:16], 0.0), 64)) * ENS
        for r in range(5):
            dx = eb[80 + r * 16 : 96 + r * 16] + f_up[it, (r + 1) * 16 : (r + 2) * 16]
            dx = (dx + (f_dn[it, r * 16 : r * 16 + 16] if r < 4 else f_up2[it, 16:32])) * ENS
            moved = jnp.where(lane16 == 127, turn(x, 127 - 8 * (r + 4) - 4), turn(dx, 127))
            if it == ITERS - 1 and r < 4:
                inc_out[every4(r), :] = dx[:8]
                inc_out[every4(32 + r), :] = dx[8:]
            for n, v in ((0, dx), (1, moved)):
                hi, lo = split2(v)
                lh[n * 80 + r * 16 : n * 80 + r * 16 + 16, :128] = hi
                lh[n * 80 + r * 16 : n * 80 + r * 16 + 16, 128:] = lo

        gacc[...] = jnp.zeros(gacc.shape, f32)

        @pl.loop(0, 8)
        def _(n):
            at = pl.ds(pl.multiple_of(n * 256, 256), 256)
            c = cm[:, at]
            u = dot(lh[...], jnp.concatenate([c, c], axis=0))
            q = qt[:, at]
            hx = jnp.sum(q * u, axis=0, keepdims=True)
            misfit = ov[1:2, at] * (hx - ov[0:1, at])
            hi, lo = split2(q * misfit)
            both = dot_nt(jnp.concatenate([hi, lo], axis=0), c)
            gacc[...] += both[:160] + both[160:]

        lane80 = iota((80, 128), 1)
        g0, g1 = gacc[0:80], gacc[80:160]
        gb[16:96] = g0 + jnp.where(lane80 == 0, 0.0, turn(g1, 1))
        sides = jnp.zeros((16, 128), f32)
        for r in range(5):
            at = r * 16
            g5 = gb[16 + at : 32 + at]
            sides = jnp.where(group16 == r, turn(g5, 8 * r + 4), sides)
            sides = jnp.where(lane16 == 64 + 8 * r, turn(g1[at : at + 16], 64 + 8 * r - 127), sides)
        gb[0:16] = sides
        gb[96:112] = sides

        def terms():
            out = [
                (gy < ngy - 1, gy > 0, remote(gb.at[pl.ds(16, 96)], g_dn.at[it], ds_.at[it, 0], dr.at[it, 0], (1 - mem, gx, lax.rem(gy + 1, ngy)))),
                (gy > 0, gy < ngy - 1, remote(gb.at[pl.ds(0, 80)], g_up.at[it], ds_.at[it, 1], dr.at[it, 1], (1 - mem, gx, lax.rem(gy + ngy - 1, ngy)))),
                (gy < ngy - 2, gy > 1, remote(gb.at[pl.ds(80, 32)], g_dn2.at[it], ds_.at[it, 2], dr.at[it, 2], (mem, gx, lax.rem(gy + 2, ngy)))),
            ]
            for n, (m, step) in enumerate(((mem, 0), (1 - mem, 1), (1 - mem, -1), (mem, 2))):
                to, of = gy + step, gy - step
                there, here = (to >= 0) & (to < ngy), (of >= 0) & (of < ngy)
                row = lax.rem(to + ngy, ngy)
                for k, (x, c, d) in enumerate(((right, has_r, has_l), (left, has_l, has_r))):
                    copy = remote(gb.at[pl.ds(0, 16)], nrecv.at[it, n, k], ns.at[it, 2 * n + k], nr.at[it, 2 * n + k], (m, x, row))
                    out.append((c & there, d & here, copy))
            return out

        run([(c, x) for c, _, x in terms()], "start")
        run([(c, x) for _, c, x in terms()], "wait_recv")
        run([(c, x) for c, _, x in terms()], "wait_send")
        beside = [nrecv[it, n] for n in range(4)]
        centre = [sides, g_dn[it, 80:96], g_up[it, 0:16], g_dn2[it, 16:32]]

        def halos(n):
            own = jnp.where((place16 == 4) & (lane16 < 40), turn(centre[n], -60), 0.0)
            return jnp.where(place16 < 4, beside[n][0], beside[n][1] + own)

        def row_of(n, v, r):
            return v + jnp.where(lane16 == 0, turn(beside[n][0], -64 - 8 * r), 0.0)

        halo_own, halo_dn, halo_up, halo_dn2 = [halos(n) for n in range(4)]

        def ext(v, r):
            return jnp.where(lane16 < 8, turn(v, -8 * r), 0.0)

        for r in range(4):
            at = r * 16
            below, own, above = row_of(1, g_dn[it, at : at + 16], r), row_of(0, gb[16 + at : 32 + at], r), row_of(2, g_up[it, 16 + at : 32 + at], r)
            hb, ho, ha = ext(halo_dn, r), ext(halo_own, r), ext(halo_up, r)
            if r == 0:
                below, hb = below + row_of(3, g_dn2[it, 0:16], 4), hb + ext(halo_dn2, 4)
                own, ho = own + row_of(1, g_dn[it, 64:80], 4), ho + ext(halo_dn, 4)
                above, ha = above + row_of(0, gb[80:96], 4), ha + ext(halo_own, 4)
            for n, (v, h) in enumerate(((below, hb), (own, ho), (above, ha))):
                at = n * 64 + r * 16
                gx_s[at : at + 16] = v
                gh_s[at : at + 16] = h
        gh_s[...] = around(gh_s[...])

        for c8 in range(2):
            g = [gh_s[row * 16 + c8 * 8 : row * 16 + c8 * 8 + 8] for row in range(12)]
            for k in range(5):
                start = k * 64 + c8 * 32
                p = xb_rows(start if k < 4 else 328 + c8 * 32)
                v = lat_in([p[row] * g[row] for row in range(12)])
                for r in range(4):
                    yh_s[every4(start + r), :] = v[r]
        hi, lo = split2(yh_s[...])
        vh_s[0] = hi
        vh_s[1] = lo

    def run(copies, what):
        for condition, copy in copies:
            if condition is None:
                getattr(copy, what)()
            else:
                pl.when(condition)(lambda copy=copy: getattr(copy, what)())

    def gradient_rows(parts, count):
        for c8 in range(2):
            g = [gx_s[row * 16 + c8 * 8 : row * 16 + c8 * 8 + 8] for row in range(12)]
            for y, rows in parts:
                for k in range(count):
                    start = k * 64 + c8 * 32
                    p = rows(start)
                    v = lat_in([p[row] * g[row] for row in range(12)])
                    for r in range(4):
                        y[every4(start + r), :] = v[r]

    def gradient(y, halo, i):
        n = y.shape[0]
        hi, lo = split2(y[...])
        hi = jnp.concatenate([hi, vh_s[0, halo : halo + n]], axis=1)
        lo = jnp.concatenate([lo, vh_s[1, halo : halo + n]], axis=1)
        both = dot(hi, wa[i])
        return both[:, :128] + both[:, 128:] + dot(lo, wa[i, :, :128])

    def member_steps(i):
        gradient_rows([(y_a, rows_from(i)), (y_b, rows_from(i + 1))], 4)
        out = []
        for y, n in ((y_a, i), (y_b, i + 1)):
            x = (1.0 - DESCENT) * work[rows_of(n), :] - (DESCENT * ENS) * gradient(y, 0, n)
            work[rows_of(n), :] = x
            out.append(x)
        return out

    def done(i):
        return pltpu.make_async_copy(work.at[rows_of(i)], alpha_out.at[rows_of(i)], ao.at[i])

    def static_step(src):
        gradient_rows([(y_c, lambda start: xb_rows(256 + start))], 1)
        stat_out[...] = (1.0 - DESCENT) * src[...] - (DESCENT * ENS) * gradient(y_c, CHUNK, 0)

    for i in range(8, CHUNKS):
        pump(i)
        if i == 8:
            finish_lon(to_right(pack.at[0], side.at[0], as_, ar), to_left(pack.at[1], side.at[1], as_, ar))
            xb[OWN, :256] = side[0, :256] + side[1, :256]
            xb[OWN, 320:328] = side[0, 256:264] + side[1, 256:264]
        if 8 <= i < 11:
            direct_x(i - 8).start()
        if 12 <= i < 15:
            arrival_x(i - 12).wait_recv()
            pl.when(has_f)(lambda i=i: forward_x(i - 12).start())
        if i < 14:
            arrived_pair(2 * (i - 8))

    for j in range(1, ngy):
        o2_in(j).wait_recv()
    for q in range(4):
        operator(q)
    arrived_pair(CHUNKS - 4)

    @pl.when(has_b)
    def _():
        for n in range(3):
            forward_x(n).wait_recv()

    for b in (BELOW, OWN, ABOVE):
        for r in range(4):
            x = around(jnp.where(own_group, xb[b, 320 + r : 321 + r], 0.0))
            xb[b, every4(328 + r), :] = x[:8]
            xb[b, every4(360 + r), :] = x[8:]
    static_chunk(stat)
    halo_columns()
    arrived_pair(CHUNKS - 2)
    reduce_and_observe(0)
    clear()

    @pl.loop(0, CHUNKS // 2)
    def _(i):
        member_pair(2 * i, member_steps(2 * i))

    static_step(stat)
    static_chunk(stat_out)
    reduce_and_observe(1)

    @pl.loop(0, CHUNKS // 2)
    def _(i):
        member_steps(2 * i)
        done(2 * i).start()
        done(2 * i + 1).start()

    static_step(stat_out)
    for i in range(CHUNKS):
        done(i).wait()

    for h in range(2 * CHUNKS):
        direct(h).wait_send()
    for n in range(3):
        direct_x(n).wait_send()

    @pl.when(has_f)
    def _():
        for h in range(2 * CHUNKS):
            forward(h).wait_send()
        for n in range(3):
            forward_x(n).wait_send()

    for j in range(1, ngx):
        o1(j).wait_send()
    for j in range(1, ngy):
        o2(j).wait_send()


def hand_over(a, b, c, a_out, b_out, c_out, a_s, b_s, c_s, ins, outs):
    parts = [pl.ds(n * (a.shape[0] // 8), a.shape[0] // 8) for n in range(8)]
    moves = [(a.at[p], a_s.at[p], a_out.at[p]) for p in parts] + [(b, b_s, b_out), (c, c_s, c_out)]
    fetches = [pltpu.make_async_copy(x, y, ins.at[n]) for n, (x, y, _) in enumerate(moves)]
    stores = [pltpu.make_async_copy(y, z, outs.at[n]) for n, (_, y, z) in enumerate(moves)]
    for copy in fetches:
        copy.start()
    for fetch, store in zip(fetches, stores):
        fetch.wait()
        store.start()
    for copy in stores:
        copy.wait()


def per_device(
    alpha, static_control, perturbations, sigma, obs_coef, interp_weights, obs_values, obs_weights, obs_tile, obs_cell
):
    rows = alpha.size // 128
    vmem = pl.BlockSpec(memory_space=pltpu.VMEM)
    args = (
        alpha.reshape(rows, 128),
        perturbations.reshape(rows, 128),
        static_control.reshape(64, 128),
        sigma.reshape(64, 128),
        obs_coef.reshape(16, 1024),
        interp_weights,
        obs_values.reshape(1, 1024),
        obs_weights.reshape(1, 1024),
        obs_tile.reshape(1, 1024),
        obs_cell.reshape(1, 1024),
    )
    dma = pltpu.SemaphoreType.DMA
    V = pltpu.VMEM
    scratch = [
        V((rows, 128), f32),
        V((rows, 128), f32),
        V((2, rows, 128), f32),
        V((3, 392, 128), f32),
        V((2, 264, 128), f32),
        V((2, 264, 128), f32),
        V((CHUNKS, 384, 256), bf16),
        V((CHUNKS, 256, 256), bf16),
        V((rows, 128), f32),
        V((CHUNK, 128), f32),
        V((CHUNK, 128), f32),
        V((64, 128), f32),
        V((320, 128), f32),
        V((2, 320, 128), bf16),
        V((224, 128), f32),
        V((192, 128), f32),
        V((32, 128), f32),
        V((ITERS, 3, 2, 32, 128), f32),
        V((ITERS, 80, 128), f32),
        V((ITERS, 96, 128), f32),
        V((ITERS, 32, 128), f32),
        V((ITERS, 192, 128), f32),
        V((ITERS, 4, 2, 16, 128), f32),
        V((112, 128), f32),
        V((ITERS, 96, 128), f32),
        V((ITERS, 80, 128), f32),
        V((ITERS, 32, 128), f32),
        V((192, 128), f32),
        V((192, 128), f32),
        V((32, 1024), f32),
        V((128, 1024), bf16),
        V((8, 1024), i32),
        V((512, 128), f32),
        V((8, 64, 128), f32),
        V((8, 8, 8, 128), f32),
        V((160, 2048), f32),
        V((128, 2048), bf16),
        V((8, 2048), f32),
        V((160, 256), bf16),
        V((160, 128), f32),
        dma((2 * CHUNKS + 3,)), dma((2 * CHUNKS + 3,)), dma((2 * CHUNKS + 3,)), dma((2 * CHUNKS + 3,)),
        dma((2,)), dma((2,)),
        dma((8,)), dma((8,)), dma((8,)), dma((8,)),
        dma((ITERS, 5)), dma((ITERS, 5)),
        dma((ITERS, 4)), dma((ITERS, 4)),
        dma((ITERS, 8)), dma((ITERS, 8)),
        dma((ITERS, 3)), dma((ITERS, 3)),
        dma((1,)), dma((CHUNKS,)),
    ]
    outs = pl.pallas_call(
        body,
        out_shape=(
            jax.ShapeDtypeStruct((rows, 128), f32),
            jax.ShapeDtypeStruct((64, 128), f32),
            jax.ShapeDtypeStruct((64, 128), f32),
        ),
        in_specs=[pl.BlockSpec(memory_space=pl.ANY)] + [vmem] * (len(args) - 1),
        out_specs=(pl.BlockSpec(memory_space=pl.ANY), vmem, vmem),
        scratch_shapes=scratch,
        name="assimilate",
        compiler_params=pltpu.CompilerParams(
            collective_id=0, has_side_effects=True, vmem_limit_bytes=56 << 20
        ),
    )(*args)
    anywhere = pl.BlockSpec(memory_space=pl.ANY)
    outs = pl.pallas_call(
        hand_over,
        out_shape=tuple(jax.ShapeDtypeStruct(x.shape, f32) for x in outs),
        in_specs=[anywhere] * 3,
        out_specs=(anywhere,) * 3,
        scratch_shapes=[V(x.shape, f32) for x in outs] + [dma((10,)), dma((10,))],
        name="hand_over",
    )(*outs)
    return (
        outs[0].reshape(alpha.shape),
        outs[1].reshape(static_control.shape),
        outs[2].reshape(static_control.shape),
    )


def solution(mesh):
    placed = (
        P("mem", None, None, "gy", "gx"),
        P(None, None, "gy", "gx"),
        P("mem", None, None, "gy", "gx"),
        P(None, None, "gy", "gx"),
        P(None, None, ("gx", "gy")),
        P(None, ("gx", "gy")),
        P(("gx", "gy")),
        P(("gx", "gy")),
        P(("gx", "gy"), None),
        P(("gx", "gy")),
    )
    return jax.shard_map(
        per_device,
        mesh=mesh,
        in_specs=placed,
        out_specs=(
            P("mem", None, None, "gy", "gx"),
            P(None, None, "gy", "gx"),
            P(None, None, "gy", "gx"),
        ),
        check_vma=False,
    )
```
